32 devices in a mesh: row: 16 (over z, x, core), col: 2 (over y).
Axes of the slice: x: 2, y: 2, z: 4, core: 2. Of those that a mesh axis runs over, the one named last changes fastest.
Arguments:
- object_slices: float32 [2, 2, 1536, 192], P(None, None, 'row', 'col'), may hold values from -4 to 4
- probe: float32 [2, 192, 192], replicated, may hold values from -4 to 4
- propagator_phase: float32 [192, 192], replicated, may hold values from -3.140625 to 3.140625
- measured: float32 [16, 2, 2, 192, 192], P('row', 'col'), may hold values from 0 to 2
- offsets: int32 [16, 2, 2, 2], P('row', 'col'), may hold values from 0 to 95
- counts: int32 [16, 2], P('row', 'col'), may hold values from 1 to 2
Outputs:
- object_out: float32 [2, 2, 1536, 192], P(None, None, 'row', 'col')
- probe_out: float32 [2, 192, 192], replicated
The draws below stay inside these ranges and needn't reach their ends.
Inputs may be any that keep to these rules, and one draw needn't show every extreme that they name: The slots below counts hold the tile's scan positions; the others are unused.
All inputs are finite; a program needn't handle non-finite values.
Results may differ from the reference program's by a relative error of at most 0.00014.
Values sent between devices are 32-bit elements; how exact they have to be, the bound alone decides.
No kernel may reach another device: no remote copies, remote signals or barrier semaphores. Data moves between devices by JAX's collectives and lax.ppermute only.
A program may use at most 64 MiB of HBM per device.

```python
import jax
import jax.numpy as jnp
from jax import lax

TILE = 96
PROBE_PIXELS = 192
SLOTS = 2
ITERS = 1
GRID_ROWS = 16
GRID_COLS = 2
NY = 1536
NX = 192


def set_ends(array, stream_key, least, largest):
    place = [jax.random.randint(jax.random.fold_in(stream_key, axis), (), 0, length) for axis, length in enumerate(array.shape)]
    longest = array.shape.index(max(array.shape))
    next_to = place[:longest] + [(place[longest] + 1) % array.shape[longest]] + place[longest + 1:]
    return array.at[tuple(place)].set(least).at[tuple(next_to)].set(largest)


def levels(stream_key, shape, split, least, largest):
    loudness = 1.0
    for position, shards_of in split:
        draws = jax.random.uniform(jax.random.fold_in(jax.random.fold_in(stream_key, 6), position), (shards_of,), jnp.float32, least / len(split), largest / len(split))
        loudness = loudness * jnp.repeat(jnp.exp(draws), shape[position] // shards_of).reshape((-1,) + (1,) * (len(shape) - 1 - position))
    return loudness


def gaussian(stream_key, dims, deviation, bound, split=(), kind=jnp.bfloat16):
    entries = jax.random.normal(stream_key, dims, jnp.float32) * deviation
    if len(split) > 0:
        entries = levels(stream_key, dims, split, -0.22, 0.18) * entries
    return jnp.clip(entries, min=-bound, max=bound).astype(kind)


def setup_inputs(seed: int = 0) -> dict:
    arg_keys = jax.random.split(jax.random.key(seed), 7)
    return {
        "object_slices": gaussian(arg_keys[0], (2, 2, NY, NX), 0.7, 4.0, ((2, 16), (3, 2)), jnp.float32),
        "probe": gaussian(arg_keys[1], (2, PROBE_PIXELS, PROBE_PIXELS), 0.7, 4.0, (), jnp.float32),
        "propagator_phase": jnp.clip(jax.random.uniform(arg_keys[2], (PROBE_PIXELS, PROBE_PIXELS), jnp.float32, -3.140625, 3.140625), -3.140625, 3.140625),
        "measured": jnp.clip(2.0 * jax.random.uniform(arg_keys[3], (GRID_ROWS, GRID_COLS, SLOTS, PROBE_PIXELS, PROBE_PIXELS), jnp.float32) ** levels(arg_keys[3], (GRID_ROWS, GRID_COLS, SLOTS, PROBE_PIXELS, PROBE_PIXELS), ((0, 16), (1, 2)), -0.2, 0.2), 0.0, 2.0),
        "offsets": set_ends(jax.random.randint(arg_keys[4], (GRID_ROWS, GRID_COLS, SLOTS, 2), 0, TILE), jax.random.fold_in(arg_keys[4], 1), 0, TILE - 1).astype(jnp.int32),
        "counts": set_ends(jax.random.randint(arg_keys[5], (GRID_ROWS, GRID_COLS), 1, SLOTS + 1), jax.random.fold_in(arg_keys[5], 1), 1, SLOTS).astype(jnp.int32),
    }


object_rate = 0.02
probe_rate = 0.3


def split_parts(value):
    return jnp.stack([jnp.real(value), jnp.imag(value)])


def position_contributions(object_window, incident_wave, slice_transmission, measured_intensity):
    first = lax.complex(object_window[0, 0], object_window[0, 1])
    second = lax.complex(object_window[1, 0], object_window[1, 1])
    entry = incident_wave * first
    carried = jnp.fft.ifft2(slice_transmission * jnp.fft.fft2(entry, norm="ortho"), norm="ortho")
    leaving = carried * second
    detector_field = jnp.fft.fft2(leaving, norm="ortho")
    model_intensity = jnp.real(detector_field) ** 2 + jnp.imag(detector_field) ** 2
    backward_wave = jnp.fft.ifft2((model_intensity - measured_intensity) * detector_field, norm="ortho")
    grad_second = jnp.conj(carried) * backward_wave
    before = jnp.conj(second) * backward_wave
    inner_wave = jnp.fft.ifft2(jnp.conj(slice_transmission) * jnp.fft.fft2(before, norm="ortho"), norm="ortho")
    grad_first = jnp.conj(incident_wave) * inner_wave
    grad_probe = jnp.conj(first) * inner_wave
    return jnp.stack([split_parts(grad_first), split_parts(grad_second)]), split_parts(grad_probe)


def reference(object_slices, probe, propagator_phase, measured, offsets, counts):
    slice_transmission = lax.complex(jnp.cos(propagator_phase), jnp.sin(propagator_phase))
    rows_count, cols_count = counts.shape
    slot_ids = jnp.arange(SLOTS, dtype=jnp.int32)
    tile_rows = jnp.arange(rows_count, dtype=jnp.int32)[:, None, None] * TILE
    tile_cols = jnp.arange(cols_count, dtype=jnp.int32)[None, :, None] * TILE
    row_offsets = (tile_rows + offsets[..., 0] + (TILE - PROBE_PIXELS // 2)).reshape(-1).astype(jnp.int32)
    column_offsets = (tile_cols + offsets[..., 1] + (TILE - PROBE_PIXELS // 2)).reshape(-1).astype(jnp.int32)
    position_weights = (slot_ids[None, None, :] < counts[:, :, None]).astype(object_slices.dtype).reshape(-1)
    measured_flat = measured.reshape(-1, PROBE_PIXELS, PROBE_PIXELS)
    current = object_slices
    wave = probe
    for iteration in range(ITERS):
        padded = jnp.pad(current, ((0, 0), (0, 0), (TILE, TILE), (TILE, TILE)))
        incident_wave = lax.complex(wave[0], wave[1])

        def accumulate_gradient(carry, scan_item):
            object_gradient, wave_gradient = carry
            row_offset, column_offset, position_weight, measured_intensity = scan_item
            zero = jnp.zeros((), jnp.int32)
            corner = (zero, zero, row_offset, column_offset)
            object_window = lax.dynamic_slice(padded, corner, (2, 2, PROBE_PIXELS, PROBE_PIXELS))
            object_contribution, wave_contribution = position_contributions(object_window, incident_wave, slice_transmission, measured_intensity)
            previous = lax.dynamic_slice(object_gradient, corner, (2, 2, PROBE_PIXELS, PROBE_PIXELS))
            object_gradient = lax.dynamic_update_slice(object_gradient, previous + position_weight * object_contribution, corner)
            return (object_gradient, wave_gradient + position_weight * wave_contribution), None

        window_corner = (jnp.zeros_like(padded), jnp.zeros_like(wave))
        (object_gradient, wave_gradient), ignored_value = lax.scan(accumulate_gradient, window_corner, (row_offsets, column_offsets, position_weights, measured_flat))
        current = current - object_rate * object_gradient[:, :, TILE:-TILE, TILE:-TILE]
        wave = wave - (probe_rate / (SLOTS * rows_count * cols_count)) * wave_gradient
    return current, wave
```

```python
import functools
import math

import jax
import jax.numpy as jnp
import numpy as np
from jax import lax
from jax.experimental import pallas as pl
from jax.experimental.pallas import tpu as pltpu
from jax.sharding import Mesh
from jax.sharding import PartitionSpec as P

object_rate = 0.02
probe_rate = 0.3

LANES = 128
f32 = jnp.float32
bf16 = jnp.bfloat16
VMEM = pl.BlockSpec(memory_space=pltpu.VMEM)
SMEM = pl.BlockSpec(memory_space=pltpu.SMEM)


def round_up(value, unit):
    return -(-value // unit) * unit


def split_matrices(width, padded):
    k = np.arange(width)
    angle = (k[:, None] * k[None, :] % width) * (2.0 * math.pi / width)
    cosine = np.cos(angle) / math.sqrt(width)
    sine = np.sin(angle) / math.sqrt(width)
    right = np.zeros((2, padded, 2, padded))
    right[0, :width, 0, :width] = cosine
    right[0, :width, 1, :width] = -sine
    right[1, :width, 0, :width] = sine
    right[1, :width, 1, :width] = cosine
    right = right.reshape(2 * padded, 2 * padded)
    left = np.block([[cosine, sine], [-sine, cosine]])

    def halves(matrix):
        high = matrix.astype(np.float32).astype(bf16)
        low = (matrix - high.astype(np.float64)).astype(np.float32).astype(bf16)
        return high, low

    right_high, right_low = halves(right)
    left_high, left_low = halves(left)
    return (
        np.concatenate([right_high, right_high, right_low], 0),
        np.concatenate([left_high, left_high, left_low], 1),
    )


def times(a_real, a_imag, b_real, b_imag):
    return (a_real * b_real - a_imag * b_imag, a_real * b_imag + a_imag * b_real)


def times_conj(a_real, a_imag, b_real, b_imag):
    return (a_real * b_real + a_imag * b_imag, a_real * b_imag - a_imag * b_real)


def halves_of(value):
    high = value.astype(bf16)
    return high, (value - high.astype(f32)).astype(bf16)


def lane_ids(rows):
    return lax.broadcasted_iota(jnp.int32, (rows, LANES), 1)


def pack_strip_kernel(own_ref, other_ref, out_ref):
    tile = own_ref.shape[2]
    first = lax.axis_index("col") == 0
    lane = lane_ids(tile)
    pad = jnp.zeros((tile, LANES - tile), f32)
    ends = []
    for plane in range(4):
        own = jnp.concatenate([own_ref[plane // 2, plane % 2], pad], 1)
        other = jnp.concatenate([other_ref[plane // 2, plane % 2], pad], 1)
        head = jnp.where(first, own, other)
        tail = pltpu.roll(jnp.where(first, other, own), tile, 1)
        out_ref[:, plane * LANES : (plane + 1) * LANES] = jnp.where(lane < tile, head, tail)
        ends.append(tail)
    half = LANES // 2
    for pair in range(2):
        even, odd = ends[2 * pair], ends[2 * pair + 1]
        out_ref[:, (4 + pair) * LANES : (5 + pair) * LANES] = jnp.where(
            lane < half, even, pltpu.roll(odd, half, 1)
        )


def unpack_strip(strip_ref, obj_ref, row):
    tile = strip_ref.shape[0]
    rows = pl.ds(row, tile)
    half = LANES // 2
    lane = lane_ids(tile)
    zero = jnp.zeros((tile, LANES), f32)
    for plane in range(4):
        obj_ref[plane, 1, rows, :] = strip_ref[:, plane * LANES : (plane + 1) * LANES]
        end = strip_ref[:, (4 + plane // 2) * LANES : (5 + plane // 2) * LANES]
        if plane % 2:
            end = pltpu.roll(end, half, 1)
        obj_ref[plane, 2, rows, :] = jnp.where(lane < half, end, zero)


def pack_strip(acc_ref, out_ref, row):
    tile = out_ref.shape[0]
    rows = pl.ds(row, tile)
    half = LANES // 2
    lane = lane_ids(tile)
    for plane in range(4):
        out_ref[:, plane * LANES : (plane + 1) * LANES] = acc_ref[plane, 1, rows, :]
    for pair in range(2):
        even = acc_ref[2 * pair, 2, rows, :]
        odd = pltpu.roll(acc_ref[2 * pair + 1, 2, rows, :], half, 1)
        out_ref[:, (4 + pair) * LANES : (5 + pair) * LANES] = jnp.where(lane < half, even, odd)


def unpack_wide(strip_ref, obj_ref, row):
    tile = strip_ref.shape[1]
    for plane in range(4):
        for j in range(3):
            obj_ref[plane, j, pl.ds(row, tile), :] = strip_ref[
                plane, :, j * LANES : (j + 1) * LANES
            ]


def pack_wide(acc_ref, out_ref, row):
    tile = out_ref.shape[1]
    for plane in range(4):
        for j in range(3):
            out_ref[plane, :, j * LANES : (j + 1) * LANES] = acc_ref[
                plane, j, pl.ds(row, tile), :
            ]


def position_kernel(
    paired,
    offsets_ref,
    counts_ref,
    above_ref,
    middle_ref,
    below_ref,
    wave_ref,
    trans_ref,
    measured_ref,
    right_ref,
    left_ref,
    top_out,
    middle_out,
    bottom_out,
    probe_out,
    obj,
    acc,
    window,
    carried,
    data,
    mid,
    field,
):
    slots = measured_ref.shape[0]
    width = wave_ref.shape[1]
    padded = wave_ref.shape[2]
    tile = obj.shape[2] // 3
    unpack, pack = (unpack_strip, pack_strip) if paired else (unpack_wide, pack_wide)
    zero_tiles = (0, 3) if paired else (3,)
    for plane in range(4):
        for j in zero_tiles:
            obj[plane, j] = jnp.zeros((3 * tile, LANES), f32)
    unpack(above_ref, obj, 0)
    unpack(middle_ref, obj, tile)
    unpack(below_ref, obj, 2 * tile)
    acc[...] = jnp.zeros(acc.shape, f32)

    shift = tile - width // 2
    base = LANES - tile if paired else 0
    if paired:
        base = base + lax.axis_index("col") * tile
    corners = []
    for slot in range(slots):
        row = offsets_ref[0, 0, slot, 0] + shift
        column = offsets_ref[0, 0, slot, 1] + shift + base
        corners.append((row, column // LANES, column % LANES))

    chunk = width // 2
    lane = lane_ids(chunk)
    for slot in range(slots):
        row, first, lanes = corners[slot]
        back = lax.rem(LANES - lanes, LANES)
        for plane in range(4):
            for start in range(0, width, chunk):
                parts = [
                    pltpu.roll(obj[plane, first + j, pl.ds(row + start, chunk), :], back, 1)
                    for j in range(3)
                ]
                for j in range(2):
                    window[plane, pl.ds(slot * width + start, chunk), j * LANES : (j + 1) * LANES] = (
                        jnp.where(lane < LANES - lanes, parts[j], parts[j + 1])
                    )

    total = slots * width
    step = 48
    chunks = [(s, s % width) for s in range(0, total, step)]

    def put(start, a, b):
        rows = pl.ds(start, step)
        for j, value in enumerate((a, b)):
            high, low = halves_of(value)
            data[rows, j * padded : (j + 1) * padded] = high
            data[rows, (2 + j) * padded : (3 + j) * padded] = low

    def transform():
        for j in range(2):
            columns = slice(j * padded, (j + 1) * padded)
            out = jnp.dot(
                data[...], right_ref[: 4 * padded, columns], preferred_element_type=f32
            ) + jnp.dot(
                data[:, : 2 * padded], right_ref[4 * padded :, columns], preferred_element_type=f32
            )
            high, low = halves_of(out)
            for slot in range(slots):
                rows = slice(slot * width, (slot + 1) * width)
                mid[slot, j * width : (j + 1) * width, :] = high[rows]
                mid[slot, (2 + j) * width : (3 + j) * width, :] = low[rows]
        for slot in range(slots):
            out = jnp.dot(
                left_ref[:, : 4 * width], mid[slot], preferred_element_type=f32
            ) + jnp.dot(
                left_ref[:, 4 * width :], mid[slot, : 2 * width], preferred_element_type=f32
            )
            for j in range(2):
                field[j, slot * width : (slot + 1) * width, :] = out[j * width : (j + 1) * width]

    def at(ref, first, start):
        rows = pl.ds(start, step)
        return ref[first, rows, :], ref[first + 1, rows, :]

    for start, inner in chunks:
        real, imag = times(*at(wave_ref, 0, inner), *at(window, 0, start))
        put(start, real, imag)
    transform()
    for start, inner in chunks:
        real, imag = times(*at(trans_ref, 0, inner), *at(field, 0, start))
        put(start, imag, real)
    transform()
    for start, inner in chunks:
        imag, real = at(field, 0, start)
        rows = pl.ds(start, step)
        carried[0, rows, :] = real
        carried[1, rows, :] = imag
        real, imag = times(real, imag, *at(window, 2, start))
        put(start, real, imag)
    transform()
    for start, inner in chunks:
        real, imag = at(field, 0, start)
        residual = real * real + imag * imag - measured_ref[start // width, pl.ds(inner, step), :]
        put(start, residual * imag, residual * real)
    transform()
    for start, inner in chunks:
        imag, real = at(field, 0, start)
        rows = pl.ds(start, step)
        second = times_conj(*at(carried, 0, start), real, imag)
        before_real, before_imag = times_conj(*at(window, 2, start), real, imag)
        put(start, before_real, before_imag)
        window[2, rows, :] = second[0]
        window[3, rows, :] = second[1]
    transform()
    for start, inner in chunks:
        real, imag = times_conj(*at(trans_ref, 0, inner), *at(field, 0, start))
        put(start, imag, real)
    transform()

    live = [(slot < counts_ref[0, 0]).astype(f32) for slot in range(slots)]
    core = lax.rem(lax.axis_index("row"), 2)
    half_lanes = lane_ids(step) < LANES // 2
    for inner in range(0, width, step):
        sum_real = jnp.zeros((step, padded), f32)
        sum_imag = jnp.zeros((step, padded), f32)
        for slot in range(slots):
            start = slot * width + inner
            rows = pl.ds(start, step)
            imag, real = at(field, 0, start)
            grad_real, grad_imag = times_conj(*at(window, 0, start), real, imag)
            sum_real = sum_real + live[slot] * grad_real
            sum_imag = sum_imag + live[slot] * grad_imag
            first_real, first_imag = times_conj(*at(wave_ref, 0, inner), real, imag)
            window[0, rows, :] = first_real
            window[1, rows, :] = first_imag
        blocks = (
            sum_real[:, :LANES],
            sum_imag[:, :LANES],
            jnp.where(
                half_lanes,
                sum_real[:, LANES:],
                pltpu.roll(sum_imag[:, LANES:], LANES // 2, 1),
            ),
        )
        for j, block in enumerate(blocks):
            probe_out[pl.ds(j * width + inner, step), :] = block

    for slot in range(slots):
        row, first, lanes = corners[slot]
        inside = lane >= lanes
        for plane in range(4):
            for start in range(0, width, chunk):
                rows = pl.ds(slot * width + start, chunk)
                target = pl.ds(row + start, chunk)
                parts = [
                    pltpu.roll(
                        live[slot] * window[plane, rows, j * LANES : (j + 1) * LANES], lanes, 1
                    )
                    for j in range(2)
                ]
                zero = jnp.zeros((chunk, LANES), f32)
                pieces = (
                    jnp.where(inside, parts[0], zero),
                    jnp.where(inside, parts[1], parts[0]),
                    jnp.where(inside, zero, parts[1]),
                )
                for j, piece in enumerate(pieces):
                    acc[plane, first + j, target, :] = acc[plane, first + j, target, :] + piece
    pack(acc, top_out, 0)
    pack(acc, middle_out, tile)
    pack(acc, bottom_out, 2 * tile)


def fold_kernel(middle_ref, below_ref, above_ref, own_out, other_out):
    tile = middle_ref.shape[0]
    first = lax.axis_index("col") == 0
    half = LANES // 2
    lane = lane_ids(tile)

    def total(j):
        columns = slice(j * LANES, (j + 1) * LANES)
        return middle_ref[:, columns] + below_ref[:, columns] + above_ref[:, columns]

    ends = [total(4), total(5)]
    for plane in range(4):
        head = total(plane)
        end = ends[plane // 2]
        if plane % 2:
            end = pltpu.roll(end, half, 1)
        tail = pltpu.roll(jnp.where(lane < tile, end, head), LANES - tile, 1)
        own_out[plane] = jnp.where(first, head, tail)
        other_out[plane] = jnp.where(first, tail, head)


def update_kernel(object_ref, own_ref, other_ref, out_ref):
    tile = object_ref.shape[2]
    for plane in range(4):
        grad = own_ref[plane] + other_ref[plane]
        out_ref[plane // 2, plane % 2] = (
            object_ref[plane // 2, plane % 2] - object_rate * grad[:, :tile]
        )


def probe_kernel(rate, probe_ref, total_ref, out_ref):
    width = probe_ref.shape[1]
    rest = width - LANES
    last = total_ref[2 * width :]
    for j in range(2):
        out_ref[j, :, :LANES] = probe_ref[j, :, :LANES] - rate * total_ref[j * width : (j + 1) * width]
        end = last if j == 0 else pltpu.roll(last, LANES // 2, 1)
        out_ref[j, :, LANES:] = probe_ref[j, :, LANES:] - rate * end[:, :rest]


def passed_along(x, axis, by):
    peers = lax.axis_size(axis)
    pairs = [(i, i + by) for i in range(peers) if 0 <= i + by < peers]
    return lax.ppermute(x, axis, pairs)


def all_sum(x, group):
    count = math.prod(lax.axis_size(axis) for axis in group)
    rows, lanes = x.shape
    piece = -(-rows // count)
    x = jnp.pad(x, ((0, piece * count - rows), (0, 0))).reshape(count, piece, lanes)
    x = lax.all_to_all(x, group, 0, 0, tiled=True)
    x = jnp.broadcast_to(jnp.sum(x, 0)[None], x.shape)
    x = lax.all_to_all(x, group, 0, 0, tiled=True)
    return x.reshape(count * piece, lanes)[:rows]


def shards(object_slices, probe, propagator_phase, measured, offsets, counts):
    tile = object_slices.shape[-1]
    width = probe.shape[-1]
    padded = round_up(width, LANES)
    slots = measured.shape[2]
    rows_count = lax.axis_size("row")
    cols_count = lax.axis_size("col")
    devices = rows_count * cols_count
    paired = cols_count == 2
    right, left = split_matrices(width, padded)
    params = pltpu.CompilerParams(vmem_limit_bytes=60 * 1024 * 1024)

    if paired:
        other = lax.ppermute(object_slices, "col", [(0, 1), (1, 0)])
        middle = pl.pallas_call(
            pack_strip_kernel,
            out_shape=jax.ShapeDtypeStruct((tile, 6 * LANES), f32),
            in_specs=[VMEM, VMEM],
            out_specs=VMEM,
        )(object_slices, other)
    else:
        cells = object_slices.reshape(4, tile, tile)
        middle = jnp.concatenate(
            [passed_along(cells, "col", 1), cells, passed_along(cells, "col", -1)], -1
        )
        middle = jnp.pad(middle, ((0, 0), (0, 0), (0, 3 * LANES - 3 * tile)))
    above = passed_along(middle, "row", 1)
    below = passed_along(middle, "row", -1)

    edge = ((0, 0), (0, 0), (0, padded - width))
    wave = jnp.pad(probe, edge)
    trans = jnp.pad(jnp.stack([jnp.cos(propagator_phase), jnp.sin(propagator_phase)]), edge)
    intensities = jnp.pad(measured[0, 0], edge)

    total = slots * width
    strip = jax.ShapeDtypeStruct(middle.shape, f32)
    top, center, bottom, terms = pl.pallas_call(
        functools.partial(position_kernel, paired),
        out_shape=[strip, strip, strip, jax.ShapeDtypeStruct((3 * width, LANES), f32)],
        in_specs=[SMEM, SMEM] + [VMEM] * 8,
        out_specs=[VMEM] * 4,
        scratch_shapes=[
            pltpu.VMEM((4, 4, 3 * tile, LANES), f32),
            pltpu.VMEM((4, 4, 3 * tile, LANES), f32),
            pltpu.VMEM((4, total, padded), f32),
            pltpu.VMEM((2, total, padded), f32),
            pltpu.VMEM((total, 4 * padded), bf16),
            pltpu.VMEM((slots, 4 * width, padded), bf16),
            pltpu.VMEM((2, total, padded), f32),
        ],
        compiler_params=params,
    )(offsets, counts, above, middle, below, wave, trans, intensities, right, left)

    from_below = passed_along(top, "row", -1)
    from_above = passed_along(bottom, "row", 1)
    all_terms = all_sum(terms, ("row", "col"))
    if paired:
        share = jax.ShapeDtypeStruct((4, tile, LANES), f32)
        mine, theirs = pl.pallas_call(
            fold_kernel,
            out_shape=[share, share],
            in_specs=[VMEM] * 3,
            out_specs=[VMEM] * 2,
        )(center, from_below, from_above)
        received = lax.ppermute(theirs, "col", [(0, 1), (1, 0)])
        object_out = pl.pallas_call(
            update_kernel,
            out_shape=jax.ShapeDtypeStruct(object_slices.shape, f32),
            in_specs=[VMEM] * 3,
            out_specs=VMEM,
        )(object_slices, mine, received)
    else:
        folded = center + from_below + from_above
        folded = (
            folded[:, :, tile : 2 * tile]
            + passed_along(folded[:, :, :tile], "col", -1)
            + passed_along(folded[:, :, 2 * tile : 3 * tile], "col", 1)
        )
        object_out = object_slices - object_rate * folded.reshape(object_slices.shape)
    probe_out = pl.pallas_call(
        functools.partial(probe_kernel, probe_rate / (slots * devices)),
        out_shape=jax.ShapeDtypeStruct(probe.shape, f32),
        in_specs=[VMEM] * 2,
        out_specs=VMEM,
    )(probe, all_terms)
    return (object_out, probe_out)


def solution(mesh):
    return jax.shard_map(
        shards,
        mesh=mesh,
        in_specs=(
            P(None, None, "row", "col"),
            P(),
            P(),
            P("row", "col", None, None, None),
            P("row", "col", None, None),
            P("row", "col"),
        ),
        out_specs=(P(None, None, "row", "col"), P()),
        check_vma=False,
    )
```

```python
import functools
import math

import jax
import jax.numpy as jnp
import numpy as np
from jax import lax
from jax.experimental import pallas as pl
from jax.experimental.pallas import tpu as pltpu
from jax.sharding import Mesh
from jax.sharding import PartitionSpec as P

object_rate = 0.02
probe_rate = 0.3

LANES = 128
f32 = jnp.float32
bf16 = jnp.bfloat16
VMEM = pl.BlockSpec(memory_space=pltpu.VMEM)
SMEM = pl.BlockSpec(memory_space=pltpu.SMEM)
ROWS = ("pair", "core")


def matrices(width):
    half = width // 2
    k = np.arange(half)
    angle = (k[:, None] * k[None, :] % half) * (2.0 * math.pi / half)
    cosine = np.cos(angle) / math.sqrt(width)
    sine = np.sin(angle) / math.sqrt(width)
    right = np.zeros((2, LANES, 2, LANES))
    right[0, :half, 0, :half] = cosine
    right[0, :half, 1, :half] = -sine
    right[1, :half, 0, :half] = sine
    right[1, :half, 1, :half] = cosine
    right = right.reshape(2 * LANES, 2 * LANES)
    left = np.block([[cosine, sine], [-sine, cosine]])

    def halves(matrix):
        high = matrix.astype(np.float32).astype(bf16)
        low = (matrix - high.astype(np.float64)).astype(np.float32).astype(bf16)
        return high, low

    right_high, right_low = halves(right)
    left_high, left_low = halves(left)
    turn = k * (2.0 * math.pi / width)
    turns = np.stack([np.cos(turn), np.sin(turn)]).astype(np.float32)
    lane_turns = np.zeros((2, 8, LANES), np.float32)
    lane_turns[:, :, :half] = turns[:, None, :]
    row_turns = np.broadcast_to(turns[:, :, None], (2, half, LANES)).copy()
    return (
        np.concatenate([right_high, right_high, right_low], 0),
        np.concatenate([left_high, left_high, left_low], 1),
        lane_turns,
        row_turns,
    )


def sorters(width):
    half = width // 2
    columns = np.zeros((width, 2 * LANES), np.float32)
    rows = np.zeros((width, width), np.float32)
    for i in range(half):
        for j in range(2):
            columns[2 * i + j, j * LANES + i] = 1
            rows[j * half + i, 2 * i + j] = 1
    return columns.astype(bf16), rows.astype(bf16)


def times(a_real, a_imag, b_real, b_imag):
    return (a_real * b_real - a_imag * b_imag, a_real * b_imag + a_imag * b_real)


def times_conj(a_real, a_imag, b_real, b_imag):
    return (a_real * b_real + a_imag * b_imag, a_real * b_imag - a_imag * b_real)


def halves_of(value):
    high = value.astype(bf16)
    return high, (value - high.astype(f32)).astype(bf16)


def lane_ids(rows):
    return lax.broadcasted_iota(jnp.int32, (rows, LANES), 1)


def packed(planes, half):
    lane = lane_ids(planes[0].shape[0])
    rest = LANES - half
    return [
        jnp.where(lane < half, planes[j], pltpu.roll(planes[3], (half - rest * j) % LANES, 1))
        for j in range(3)
    ]


def last_of(parts, half):
    lane = lane_ids(parts[0].shape[0])
    rest = LANES - half
    out = pltpu.roll(parts[0], rest, 1)
    for j in range(1, 3):
        out = jnp.where(lane < rest * j, out, pltpu.roll(parts[j], (rest * j + rest) % LANES, 1))
    return out


def prepare_kernel(probe_ref, trans_ref, measured_ref, columns_ref, rows_ref, wave_out, trans_out, measured_out):
    width = probe_ref.shape[1]
    half = width // 2
    lane = lane_ids(width)
    for j in range(2):
        head = probe_ref[j, :, :LANES]
        tail = jnp.concatenate(
            [probe_ref[j, :, LANES:], jnp.zeros((width, 2 * LANES - width), f32)], 1
        )
        rest = LANES - half
        wave_out[j, :, :LANES] = jnp.where(lane < half, head, 0.0)
        wave_out[j, :, LANES:] = jnp.where(
            lane < rest, pltpu.roll(head, rest, 1), pltpu.roll(tail, rest, 1)
        )
    for source, target in ((trans_ref, trans_out), (measured_ref, measured_out)):
        for j in range(source.shape[0]):
            left = source[j]
            total = jnp.zeros((width, 2 * LANES), f32)
            for part in range(3):
                piece = left.astype(bf16)
                left = left - piece.astype(f32)
                moved = jnp.dot(piece, columns_ref[...], preferred_element_type=f32)
                total = total + jnp.dot(
                    rows_ref[...], moved.astype(bf16), preferred_element_type=f32
                )
            target[j] = total


def position_kernel(
    paired,
    cores,
    offsets_ref,
    counts_ref,
    *refs,
):
    sides = 2 if paired else 3
    tiles = refs[: 3 * sides]
    (
        wave_ref,
        trans_ref,
        measured_ref,
        right_ref,
        left_ref,
        lane_turn_ref,
        row_turn_ref,
        top_out,
        middle_out,
        bottom_out,
        probe_out,
        obj,
        acc,
        window,
        carried,
        data,
        out_right,
        mid,
        out_left,
    ) = refs[3 * sides :]
    slots = measured_ref.shape[0]
    width = wave_ref.shape[1]
    half = width // 2
    tile = obj.shape[2] // 3
    total = slots * width
    step = 16
    column_of = lax.axis_index("col")

    pad = jnp.zeros((tile, LANES - tile), f32)
    for row in range(3):
        rows = slice(row * tile, (row + 1) * tile)
        for side in range(sides):
            if paired:
                place = 1 if side == 0 else 2 - 2 * column_of
            else:
                place = (1, 0, 2)[side]
            for plane in range(4):
                value = tiles[row * sides + side][plane // 2, plane % 2]
                obj[plane, place, rows, :] = jnp.concatenate([value, pad], 1)
        if paired:
            for plane in range(4):
                obj[plane, 2 * column_of, rows, :] = jnp.zeros((tile, LANES), f32)

    shift = tile - half
    corners = [
        (offsets_ref[0, 0, slot, 0] + shift, offsets_ref[0, 0, slot, 1] + shift)
        for slot in range(slots)
    ]
    chunk = half
    lane = lane_ids(chunk)
    for slot in range(slots):
        row, column = corners[slot]
        back = lax.rem(LANES - column, LANES)
        inside = lane < tile - column
        for plane in range(4):
            for start in range(0, width, chunk):
                source = pl.ds(row + start, chunk)
                target = pl.ds(slot * width + start, chunk)
                for j in range(2):
                    window[plane, j, target, :] = jnp.where(
                        inside,
                        pltpu.roll(obj[plane, j, source, :], back, 1),
                        pltpu.roll(obj[plane, j + 1, source, :], tile - column, 1),
                    )
    acc[...] = jnp.zeros(acc.shape, f32)

    lane_turn = [jnp.broadcast_to(lane_turn_ref[j, :1, :], (step, LANES)) for j in range(2)]
    span = 2 * LANES

    def put(block, start, a, b):
        rows = pl.ds(block * total + start, step)
        for j, value in enumerate((a, b)):
            high, low = halves_of(value)
            data[rows, j * LANES : (j + 1) * LANES] = high
            data[rows, span + j * LANES : span + (j + 1) * LANES] = low

    def multiply_right():
        left = jnp.concatenate([data[...], data[:, :span]], 1)
        out_right[...] = jnp.dot(left, right_ref[...], preferred_element_type=f32)

    def put_mid(slot, block, j, start, a, b):
        for part, value in enumerate((a, b)):
            high, low = halves_of(value)
            columns = slice(j * LANES, (j + 1) * LANES)
            mid[slot, block, pl.ds(part * half + start, step), columns] = high
            mid[slot, block, pl.ds((2 + part) * half + start, step), columns] = low

    def multiply_left():
        for slot in range(slots):
            for block in range(2):
                right = jnp.concatenate([mid[slot, block], mid[slot, block, :width]], 0)
                out_left[slot, block] = jnp.dot(
                    left_ref[...], right, preferred_element_type=f32
                )

    def get_right(block, start):
        rows = pl.ds(block * total + start, step)
        return out_right[rows, :LANES], out_right[rows, LANES:]

    def get_left(slot, block, j, start):
        columns = slice(j * LANES, (j + 1) * LANES)
        return (
            out_left[slot, block, pl.ds(start, step), columns],
            out_left[slot, block, pl.ds(half + start, step), columns],
        )

    def forward(source):
        for slot in range(slots):
            for row in range(0, width, step):
                (a0, b0), (a1, b1) = source(slot, row)
                start = slot * width + row
                put(0, start, a0 + a1, b0 + b1)
                put(1, start, *times_conj(*lane_turn, a0 - a1, b0 - b1))
        multiply_right()
        for slot in range(slots):
            for row in range(0, half, step):
                turn = row_turn_ref[0, pl.ds(row, step), :], row_turn_ref[1, pl.ds(row, step), :]
                for j in range(2):
                    a0, b0 = get_right(j, slot * width + row)
                    a1, b1 = get_right(j, slot * width + half + row)
                    put_mid(slot, 0, j, row, a0 + a1, b0 + b1)
                    put_mid(slot, 1, j, row, *times_conj(*turn, a0 - a1, b0 - b1))
        multiply_left()

    def inverse(source):
        for slot in range(slots):
            for row in range(0, width, step):
                for j, (a, b) in enumerate(source(slot, row)):
                    put(j, slot * width + row, a, b)
        multiply_right()
        for slot in range(slots):
            for row in range(0, width, step):
                a0, b0 = get_right(0, slot * width + row)
                a1, b1 = times_conj(*lane_turn, *get_right(1, slot * width + row))
                put_mid(slot, row // half, 0, row % half, a0 + a1, b0 + b1)
                put_mid(slot, row // half, 1, row % half, a0 - a1, b0 - b1)
        multiply_left()

    def frequency(slot, row, j):
        return get_left(slot, row // half, j, row % half)

    def natural(slot, row, j):
        b0, a0 = get_left(slot, 0, j, row)
        turn = row_turn_ref[0, pl.ds(row, step), :], row_turn_ref[1, pl.ds(row, step), :]
        b1, a1 = times_conj(*turn, *get_left(slot, 1, j, row))
        return (a0 + a1, b0 + b1), (a0 - a1, b0 - b1)

    def at(ref, first, row, j):
        rows = pl.ds(row, step)
        columns = slice(j * LANES, (j + 1) * LANES)
        return ref[first, rows, columns], ref[first + 1, rows, columns]

    def seen(first, slot, row, j):
        rows = pl.ds(slot * width + row, step)
        return window[first, j, rows, :], window[first + 1, j, rows, :]

    def keep(ref, first, slot, row, j, real, imag):
        rows = pl.ds(slot * width + row, step)
        ref[first, j, rows, :] = real
        ref[first + 1, j, rows, :] = imag

    def entry(slot, row):
        return [times(*at(wave_ref, 0, row, j), *seen(0, slot, row, j)) for j in range(2)]

    def propagate(slot, row):
        out = []
        for j in range(2):
            real, imag = times(*at(trans_ref, 0, row, j), *frequency(slot, row, j))
            out.append((imag, real))
        return out

    def residual(slot, row):
        out = []
        for j in range(2):
            real, imag = frequency(slot, row, j)
            columns = slice(j * LANES, (j + 1) * LANES)
            factor = real * real + imag * imag - measured_ref[slot, pl.ds(row, step), columns]
            out.append((factor * imag, factor * real))
        return out

    def propagate_back(slot, row):
        out = []
        for j in range(2):
            real, imag = times_conj(*at(trans_ref, 0, row, j), *frequency(slot, row, j))
            out.append((imag, real))
        return out

    def each_natural(handle):
        for slot in range(slots):
            for row in range(0, half, step):
                for j in range(2):
                    top, bottom = natural(slot, row, j)
                    handle(slot, row, j, *top)
                    handle(slot, half + row, j, *bottom)

    forward(entry)
    inverse(propagate)

    def leave(slot, row, j, real, imag):
        keep(carried, 0, slot, row, j, real, imag)
        keep(carried, 2, slot, row, j, *times(real, imag, *seen(2, slot, row, j)))

    each_natural(leave)

    def leaving(slot, row):
        rows = pl.ds(slot * width + row, step)
        return [(carried[2, j, rows, :], carried[3, j, rows, :]) for j in range(2)]

    forward(leaving)
    inverse(residual)

    def before(slot, row, j, real, imag):
        rows = pl.ds(slot * width + row, step)
        keep(
            carried, 2, slot, row, j, *times_conj(*seen(2, slot, row, j), real, imag)
        )
        keep(
            window,
            2,
            slot,
            row,
            j,
            *times_conj(carried[0, j, rows, :], carried[1, j, rows, :], real, imag),
        )

    each_natural(before)
    forward(leaving)
    inverse(propagate_back)

    live = [(slot < counts_ref[0, 0]).astype(f32) for slot in range(slots)]
    core = lax.axis_index("core")
    share = width // cores
    for row in range(0, half, step):
        sums = [[None] * 4 for side in range(2)]
        for j in range(2):
            for slot in range(slots):
                for side, (real, imag) in enumerate(natural(slot, row, j)):
                    place = side * half + row
                    term = times_conj(*seen(0, slot, place, j), real, imag)
                    keep(
                        window,
                        0,
                        slot,
                        place,
                        j,
                        *times_conj(*at(wave_ref, 0, place, j), real, imag),
                    )
                    for part in range(2):
                        value = live[slot] * term[part]
                        old = sums[side][2 * part + j]
                        sums[side][2 * part + j] = value if old is None else old + value
        for side in range(2):
            place = side * half + row
            which = lax.rem(place // share + core, cores)
            for j, block in enumerate(packed(sums[side], half)):
                probe_out[which, j, pl.ds(place % share, step), :] = block

    for slot in range(slots):
        row, column = corners[slot]
        inside = lane >= column
        over = column + LANES - tile
        for plane in range(4):
            for start in range(0, width, chunk):
                rows = pl.ds(slot * width + start, chunk)
                target = pl.ds(row + start, chunk)
                first, second = (live[slot] * window[plane, j, rows, :] for j in range(2))
                pieces = [jnp.where(inside, pltpu.roll(second, column, 1), pltpu.roll(first, over, 1))]
                if paired:
                    value = live[slot] * window[plane, 1 - column_of, rows, :]
                    value = pltpu.roll(value, jnp.where(column_of == 0, over, column), 1)
                    pieces.append(jnp.where(inside.astype(jnp.int32) == column_of, value, 0.0))
                else:
                    pieces.append(jnp.where(inside, pltpu.roll(first, column, 1), 0.0))
                    pieces.append(jnp.where(inside, 0.0, pltpu.roll(second, over, 1)))
                for side, piece in enumerate(pieces):
                    acc[plane, side, target, :] = acc[plane, side, target, :] + piece
    for row, out in enumerate((top_out, middle_out, bottom_out)):
        rows = slice(row * tile, (row + 1) * tile)
        for side in range(sides):
            planes = [acc[plane, side, rows, :] for plane in range(4)]
            for j, block in enumerate(packed(planes, tile)):
                k = 3 * side + j
                out[:, k * LANES : (k + 1) * LANES] = block


def fold_kernel(middle_ref, below_ref, above_ref, *outs):
    columns = outs[0].shape[1]
    for side, out in enumerate(outs):
        part = slice(side * columns, (side + 1) * columns)
        out[...] = middle_ref[:, part] + below_ref[:, part] + above_ref[:, part]


def update_kernel(object_ref, *refs):
    out_ref = refs[-1]
    tile = object_ref.shape[2]
    total = refs[0][...]
    for ref in refs[1:-1]:
        total = total + ref[...]
    parts = [total[:, j * LANES : (j + 1) * LANES] for j in range(3)]
    parts.append(last_of(parts, tile))
    for plane in range(4):
        out_ref[plane // 2, plane % 2] = (
            object_ref[plane // 2, plane % 2] - object_rate * parts[plane][:, :tile]
        )


def probe_kernel(rate, cores, probe_ref, *refs):
    out_ref = refs[-1]
    width = probe_ref.shape[1]
    half = width // 2
    share = width // cores
    lane = lane_ids(share)
    for k in range(cores):
        ref = refs[k]
        start = share * lax.rem(lax.axis_index("core") + k, cores)
        rows = pl.ds(pl.multiple_of(start, 8), share)
        parts = [ref[j] for j in range(3)]
        parts.append(last_of(parts, half))
        for j in range(2):
            head, tail = parts[2 * j], pltpu.roll(parts[2 * j + 1], half, 1)
            out_ref[j, rows, :LANES] = probe_ref[j, rows, :LANES] - rate * jnp.where(
                lane < half, head, tail
            )
            out_ref[j, rows, LANES:] = (
                probe_ref[j, rows, LANES:] - rate * tail[:, : width - LANES]
            )


def passed_along(x, axis, by):
    peers = lax.axis_size(axis)
    pairs = [(i, i + by) for i in range(peers) if 0 <= i + by < peers]
    return lax.ppermute(x, axis, pairs)


def all_sum(x, group):
    count = math.prod(lax.axis_size(axis) for axis in group)
    shape = x.shape
    x = x.reshape(-1, 2, LANES)
    pairs = x.shape[0]
    piece = -(-pairs // count)
    if piece * count > pairs:
        x = jnp.pad(x, ((0, piece * count - pairs), (0, 0), (0, 0)))
    x = x.reshape(count, piece, 2, LANES)
    x = lax.all_to_all(x, group, 0, 0, tiled=True)
    x = jnp.broadcast_to(jnp.sum(x, 0)[None], x.shape)
    x = lax.all_to_all(x, group, 0, 0, tiled=True)
    return x.reshape(count * piece, 2, LANES)[:pairs].reshape(shape)


def shards(object_slices, probe, propagator_phase, measured, offsets, counts):
    tile = object_slices.shape[-1]
    width = probe.shape[-1]
    slots = measured.shape[2]
    cores = lax.axis_size("core")
    cols_count = lax.axis_size("col")
    devices = lax.axis_size(ROWS) * cols_count
    paired = cols_count == 2
    params = pltpu.CompilerParams(vmem_limit_bytes=60 * 1024 * 1024)

    def shape(*dims, kind=f32):
        return jax.ShapeDtypeStruct(dims, kind)

    cells = object_slices
    if paired:
        beside = [lax.ppermute(cells, "col", [(0, 1), (1, 0)])]
    else:
        beside = [passed_along(cells, "col", 1), passed_along(cells, "col", -1)]
    middle = [cells] + beside
    above = [passed_along(x, ROWS, 1) for x in middle]
    below = [passed_along(x, ROWS, -1) for x in middle]

    columns, rows = sorters(width)
    wave, trans, intensities = pl.pallas_call(
        prepare_kernel,
        out_shape=[
            shape(2, width, 2 * LANES),
            shape(2, width, 2 * LANES),
            shape(slots, width, 2 * LANES),
        ],
        in_specs=[VMEM] * 5,
        out_specs=[VMEM] * 3,
    )(
        probe,
        jnp.stack([jnp.cos(propagator_phase), jnp.sin(propagator_phase)]),
        measured[0, 0],
        columns,
        rows,
    )

    total = slots * width
    sides = len(middle)
    strip = shape(tile, sides * 3 * LANES)
    scratch = [
        pltpu.VMEM((4, 3, 3 * tile, LANES), f32),
        pltpu.VMEM((4, sides, 3 * tile, LANES), f32),
        pltpu.VMEM((4, 2, total, LANES), f32),
        pltpu.VMEM((4, 2, total, LANES), f32),
        pltpu.VMEM((2 * total, 4 * LANES), bf16),
        pltpu.VMEM((2 * total, 2 * LANES), f32),
        pltpu.VMEM((slots, 2, 2 * width, 2 * LANES), bf16),
        pltpu.VMEM((slots, 2, width, 2 * LANES), f32),
    ]
    top, center, bottom, terms = pl.pallas_call(
        functools.partial(position_kernel, paired, cores),
        out_shape=[strip, strip, strip, shape(cores, 3, width // cores, LANES)],
        in_specs=[SMEM, SMEM] + [VMEM] * (3 * sides + 7),
        out_specs=[VMEM] * 4,
        scratch_shapes=scratch,
        compiler_params=params,
    )(offsets, counts, *above, *middle, *below, wave, trans, intensities, *matrices(width))

    if cores == 2:
        swap = [(0, 1), (1, 0)]
        mine = all_sum(terms[0] + lax.ppermute(terms[1], "core", swap), ("pair", "col"))
        sums = [mine, lax.ppermute(mine, "core", swap)]
    else:
        sums = [all_sum(terms[0], ("pair", "col"))]
    from_below = passed_along(top, ROWS, -1)
    from_above = passed_along(bottom, ROWS, 1)
    share = shape(tile, 3 * LANES)
    parts = pl.pallas_call(
        fold_kernel,
        out_shape=[share] * sides,
        in_specs=[VMEM] * 3,
        out_specs=[VMEM] * sides,
    )(center, from_below, from_above)
    if paired:
        received = [lax.ppermute(parts[1], "col", [(0, 1), (1, 0)])]
    else:
        received = [passed_along(parts[1], "col", -1), passed_along(parts[2], "col", 1)]
    object_out = pl.pallas_call(
        update_kernel,
        out_shape=shape(*object_slices.shape),
        in_specs=[VMEM] * (2 + len(received)),
        out_specs=VMEM,
    )(object_slices, parts[0], *received)
    probe_out = pl.pallas_call(
        functools.partial(probe_kernel, probe_rate / (slots * devices), cores),
        out_shape=shape(*probe.shape),
        in_specs=[VMEM] * (1 + cores),
        out_specs=VMEM,
    )(probe, *sums)
    return (object_out, probe_out)


def solution(mesh):
    rows, cols = mesh.devices.shape
    cores = 2 if rows % 2 == 0 else 1
    finer = Mesh(mesh.devices.reshape(rows // cores, cores, cols), ROWS + ("col",))
    return jax.shard_map(
        shards,
        mesh=finer,
        in_specs=(
            P(None, None, ROWS, "col"),
            P(),
            P(),
            P(ROWS, "col", None, None, None),
            P(ROWS, "col", None, None),
            P(ROWS, "col"),
        ),
        out_specs=(P(None, None, ROWS, "col"), P()),
        check_vma=False,
    )
```

```python
import functools
import math

import jax
import jax.numpy as jnp
import numpy as np
from jax import lax
from jax.experimental import pallas as pl
from jax.experimental.pallas import tpu as pltpu
from jax.sharding import Mesh
from jax.sharding import PartitionSpec as P

object_rate = 0.02
probe_rate = 0.3

LANES = 128
f32 = jnp.float32
bf16 = jnp.bfloat16
VMEM = pl.BlockSpec(memory_space=pltpu.VMEM)
SMEM = pl.BlockSpec(memory_space=pltpu.SMEM)
ROWS = ("pair", "core")


def matrices(width):
    half = width // 2
    k = np.arange(half)
    angle = (k[:, None] * k[None, :] % half) * (2.0 * math.pi / half)
    cosine = np.cos(angle) / math.sqrt(width)
    sine = np.sin(angle) / math.sqrt(width)
    right = np.zeros((2, LANES, 2, LANES))
    right[0, :half, 0, :half] = cosine
    right[0, :half, 1, :half] = -sine
    right[1, :half, 0, :half] = sine
    right[1, :half, 1, :half] = cosine
    right = right.reshape(2 * LANES, 2 * LANES)
    left = np.block([[cosine, sine], [-sine, cosine]])

    def halves(matrix):
        high = matrix.astype(np.float32).astype(bf16)
        low = (matrix - high.astype(np.float64)).astype(np.float32).astype(bf16)
        return high, low

    right_high, right_low = halves(right)
    left_high, left_low = halves(left)
    turn = k * (2.0 * math.pi / width)
    turns = np.stack([np.cos(turn), np.sin(turn)]).astype(np.float32)
    lane_turns = np.zeros((2, 8, LANES), np.float32)
    lane_turns[:, :, :half] = turns[:, None, :]
    row_turns = np.broadcast_to(turns[:, :, None], (2, half, LANES)).copy()
    return (
        np.concatenate([right_high, right_high, right_low], 0),
        np.concatenate([left_high, left_high, left_low], 1),
        lane_turns,
        row_turns,
    )


def sorters(width):
    half = width // 2
    columns = np.zeros((width, 2 * LANES), np.float32)
    rows = np.zeros((width, width), np.float32)
    for i in range(half):
        for j in range(2):
            columns[2 * i + j, j * LANES + i] = 1
            rows[j * half + i, 2 * i + j] = 1
    return columns.astype(bf16), rows.astype(bf16)


def times(a_real, a_imag, b_real, b_imag):
    return (a_real * b_real - a_imag * b_imag, a_real * b_imag + a_imag * b_real)


def times_conj(a_real, a_imag, b_real, b_imag):
    return (a_real * b_real + a_imag * b_imag, a_real * b_imag - a_imag * b_real)


def halves_of(value):
    high = value.astype(bf16)
    return high, (value - high.astype(f32)).astype(bf16)


def lane_ids(rows):
    return lax.broadcasted_iota(jnp.int32, (rows, LANES), 1)


def packed(planes, half):
    lane = lane_ids(planes[0].shape[0])
    rest = LANES - half
    return [
        jnp.where(lane < half, planes[j], pltpu.roll(planes[3], (half - rest * j) % LANES, 1))
        for j in range(3)
    ]


def last_of(parts, half):
    lane = lane_ids(parts[0].shape[0])
    rest = LANES - half
    out = pltpu.roll(parts[0], rest, 1)
    for j in range(1, 3):
        out = jnp.where(lane < rest * j, out, pltpu.roll(parts[j], (rest * j + rest) % LANES, 1))
    return out


def prepare_kernel(
    probe_ref,
    cosine_ref,
    sine_ref,
    measured_ref,
    columns_ref,
    rows_ref,
    wave_out,
    trans_out,
    measured_out,
):
    width = probe_ref.shape[1]
    half = width // 2
    lane = lane_ids(width)
    for j in range(2):
        head = probe_ref[j, :, :LANES]
        tail = jnp.concatenate(
            [probe_ref[j, :, LANES:], jnp.zeros((width, 2 * LANES - width), f32)], 1
        )
        rest = LANES - half
        wave_out[j, :, :LANES] = jnp.where(lane < half, head, 0.0)
        wave_out[j, :, LANES:] = jnp.where(
            lane < rest, pltpu.roll(head, rest, 1), pltpu.roll(tail, rest, 1)
        )
    planes = [(cosine_ref[...], trans_out, 0), (sine_ref[...], trans_out, 1)]
    for slot in range(measured_out.shape[0]):
        planes.append((measured_ref[0, 0, slot], measured_out, slot))
    for left, target, j in planes:
        total = jnp.zeros((width, 2 * LANES), f32)
        for part in range(3):
            piece = left.astype(bf16)
            left = left - piece.astype(f32)
            moved = jnp.dot(piece, columns_ref[...], preferred_element_type=f32)
            total = total + jnp.dot(rows_ref[...], moved.astype(bf16), preferred_element_type=f32)
        target[j] = total


def row_places(cores):
    core = lax.axis_index("core") if cores == 2 else 1
    return 1, 2 - 2 * core, 2 * core


def position_kernel(
    paired,
    cores,
    offsets_ref,
    counts_ref,
    *refs,
):
    sides = 2 if paired else 3
    tiles = refs[: 3 * sides]
    (
        wave_ref,
        trans_ref,
        measured_ref,
        right_ref,
        left_ref,
        lane_turn_ref,
        row_turn_ref,
        own_out,
        near_out,
        far_out,
    ) = refs[3 * sides : 3 * sides + 10]
    terms_out = refs[3 * sides + 10 : 3 * sides + 10 + cores]
    (
        obj,
        acc,
        window,
        carried,
        data,
        out_right,
        mid,
        out_left,
        terms,
    ) = refs[3 * sides + 10 + cores :]
    slots = measured_ref.shape[0]
    width = wave_ref.shape[1]
    half = width // 2
    tile = obj.shape[2] // 3
    total = slots * width
    step = 16
    column_of = lax.axis_index("col")
    row_starts = [pl.multiple_of(place * tile, 8) for place in row_places(cores)]

    pad = jnp.zeros((tile, LANES - tile), f32)
    for row in range(3):
        rows = pl.ds(row_starts[row], tile)
        for side in range(sides):
            if paired:
                place = 1 if side == 0 else 2 - 2 * column_of
            else:
                place = (1, 0, 2)[side]
            for plane in range(4):
                value = tiles[row * sides + side][plane // 2, plane % 2]
                obj[plane, place, rows, :] = jnp.concatenate([value, pad], 1)
        if paired:
            for plane in range(4):
                obj[plane, 2 * column_of, rows, :] = jnp.zeros((tile, LANES), f32)

    shift = tile - half
    corners = [
        (offsets_ref[0, 0, slot, 0] + shift, offsets_ref[0, 0, slot, 1] + shift)
        for slot in range(slots)
    ]
    chunk = half
    lane = lane_ids(chunk)
    for slot in range(slots):
        row, column = corners[slot]
        back = lax.rem(LANES - column, LANES)
        inside = lane < tile - column
        for plane in range(4):
            for start in range(0, width, chunk):
                source = pl.ds(row + start, chunk)
                target = pl.ds(slot * width + start, chunk)
                for j in range(2):
                    window[plane, j, target, :] = jnp.where(
                        inside,
                        pltpu.roll(obj[plane, j, source, :], back, 1),
                        pltpu.roll(obj[plane, j + 1, source, :], tile - column, 1),
                    )
    acc[...] = jnp.zeros(acc.shape, f32)

    lane_turn = [jnp.broadcast_to(lane_turn_ref[j, :1, :], (step, LANES)) for j in range(2)]
    span = 2 * LANES

    def put(slot, block, row, a, b):
        rows = pl.ds((2 * slot + block) * width + row, step)
        high, low = halves_of(jnp.concatenate([a, b], 1))
        data[rows, :span] = high
        data[rows, span:] = low

    def multiply_right():
        for slot in range(slots):
            rows = slice(2 * slot * width, 2 * (slot + 1) * width)
            left = jnp.concatenate([data[rows, :], data[rows, :span]], 1)
            out_right[rows, :] = jnp.dot(left, right_ref[...], preferred_element_type=f32)

    def put_mid(slot, block, start, first, second):
        for part in range(2):
            high, low = halves_of(jnp.concatenate([first[part], second[part]], 1))
            mid[slot, block, pl.ds(part * half + start, step), :] = high
            mid[slot, block, pl.ds((2 + part) * half + start, step), :] = low
            mid[slot, block, pl.ds((4 + part) * half + start, step), :] = high

    def multiply_left():
        for slot in range(slots):
            for block in range(2):
                out_left[slot, block] = jnp.dot(
                    left_ref[...], mid[slot, block], preferred_element_type=f32
                )

    def get_right(slot, block, row):
        rows = pl.ds((2 * slot + block) * width + row, step)
        return out_right[rows, :LANES], out_right[rows, LANES:]

    def get_left(slot, block, j, start):
        columns = slice(j * LANES, (j + 1) * LANES)
        return (
            out_left[slot, block, pl.ds(start, step), columns],
            out_left[slot, block, pl.ds(half + start, step), columns],
        )

    def forward(source):
        for slot in range(slots):
            for row in range(0, width, step):
                (a0, b0), (a1, b1) = source(slot, row)
                put(slot, 0, row, a0 + a1, b0 + b1)
                put(slot, 1, row, *times_conj(*lane_turn, a0 - a1, b0 - b1))
        multiply_right()
        for slot in range(slots):
            for row in range(0, half, step):
                turn = row_turn_ref[0, pl.ds(row, step), :], row_turn_ref[1, pl.ds(row, step), :]
                even, odd = [], []
                for j in range(2):
                    a0, b0 = get_right(slot, j, row)
                    a1, b1 = get_right(slot, j, half + row)
                    even.append((a0 + a1, b0 + b1))
                    odd.append(times_conj(*turn, a0 - a1, b0 - b1))
                put_mid(slot, 0, row, *even)
                put_mid(slot, 1, row, *odd)
        multiply_left()

    def inverse(source):
        for slot in range(slots):
            for row in range(0, width, step):
                for j, (a, b) in enumerate(source(slot, row)):
                    put(slot, j, row, a, b)
        multiply_right()
        for slot in range(slots):
            for row in range(0, width, step):
                a0, b0 = get_right(slot, 0, row)
                a1, b1 = times_conj(*lane_turn, *get_right(slot, 1, row))
                put_mid(slot, row // half, row % half, (a0 + a1, b0 + b1), (a0 - a1, b0 - b1))
        multiply_left()

    def frequency(slot, row, j):
        return get_left(slot, row // half, j, row % half)

    def natural(slot, row, j):
        b0, a0 = get_left(slot, 0, j, row)
        turn = row_turn_ref[0, pl.ds(row, step), :], row_turn_ref[1, pl.ds(row, step), :]
        b1, a1 = times_conj(*turn, *get_left(slot, 1, j, row))
        return (a0 + a1, b0 + b1), (a0 - a1, b0 - b1)

    def at(ref, first, row, j):
        rows = pl.ds(row, step)
        columns = slice(j * LANES, (j + 1) * LANES)
        return ref[first, rows, columns], ref[first + 1, rows, columns]

    def seen(first, slot, row, j):
        rows = pl.ds(slot * width + row, step)
        return window[first, j, rows, :], window[first + 1, j, rows, :]

    def keep(ref, first, slot, row, j, real, imag):
        rows = pl.ds(slot * width + row, step)
        ref[first, j, rows, :] = real
        ref[first + 1, j, rows, :] = imag

    def entry(slot, row):
        return [times(*at(wave_ref, 0, row, j), *seen(0, slot, row, j)) for j in range(2)]

    def propagate(slot, row):
        out = []
        for j in range(2):
            real, imag = times(*at(trans_ref, 0, row, j), *frequency(slot, row, j))
            out.append((imag, real))
        return out

    def residual(slot, row):
        out = []
        for j in range(2):
            real, imag = frequency(slot, row, j)
            columns = slice(j * LANES, (j + 1) * LANES)
            factor = real * real + imag * imag - measured_ref[slot, pl.ds(row, step), columns]
            out.append((factor * imag, factor * real))
        return out

    def propagate_back(slot, row):
        out = []
        for j in range(2):
            real, imag = times_conj(*at(trans_ref, 0, row, j), *frequency(slot, row, j))
            out.append((imag, real))
        return out

    def each_natural(handle):
        for slot in range(slots):
            for row in range(0, half, step):
                for j in range(2):
                    top, bottom = natural(slot, row, j)
                    handle(slot, row, j, *top)
                    handle(slot, half + row, j, *bottom)

    forward(entry)
    inverse(propagate)

    def leave(slot, row, j, real, imag):
        keep(carried, 0, slot, row, j, real, imag)
        keep(carried, 2, slot, row, j, *times(real, imag, *seen(2, slot, row, j)))

    each_natural(leave)

    def leaving(slot, row):
        rows = pl.ds(slot * width + row, step)
        return [(carried[2, j, rows, :], carried[3, j, rows, :]) for j in range(2)]

    forward(leaving)
    inverse(residual)

    def before(slot, row, j, real, imag):
        rows = pl.ds(slot * width + row, step)
        keep(
            carried, 2, slot, row, j, *times_conj(*seen(2, slot, row, j), real, imag)
        )
        keep(
            window,
            2,
            slot,
            row,
            j,
            *times_conj(carried[0, j, rows, :], carried[1, j, rows, :], real, imag),
        )

    each_natural(before)
    forward(leaving)
    inverse(propagate_back)

    live = [(slot < counts_ref[0, 0]).astype(f32) for slot in range(slots)]
    core = lax.axis_index("core")
    share = width // cores
    for row in range(0, half, step):
        sums = [[None] * 4 for side in range(2)]
        for j in range(2):
            for slot in range(slots):
                for side, (real, imag) in enumerate(natural(slot, row, j)):
                    place = side * half + row
                    term = times_conj(*seen(0, slot, place, j), real, imag)
                    keep(
                        window,
                        0,
                        slot,
                        place,
                        j,
                        *times_conj(*at(wave_ref, 0, place, j), real, imag),
                    )
                    for part in range(2):
                        value = live[slot] * term[part]
                        old = sums[side][2 * part + j]
                        sums[side][2 * part + j] = value if old is None else old + value
        for side in range(2):
            place = side * half + row
            which = lax.rem(place // share + core, cores)
            for j, block in enumerate(packed(sums[side], half)):
                terms[which, j, pl.ds(place % share, step), :] = block
    for k, out in enumerate(terms_out):
        out[...] = terms[k]

    for slot in range(slots):
        row, column = corners[slot]
        inside = lane >= column
        over = column + LANES - tile
        for plane in range(4):
            for start in range(0, width, chunk):
                rows = pl.ds(slot * width + start, chunk)
                target = pl.ds(row + start, chunk)
                first, second = (live[slot] * window[plane, j, rows, :] for j in range(2))
                pieces = [jnp.where(inside, pltpu.roll(second, column, 1), pltpu.roll(first, over, 1))]
                if paired:
                    value = live[slot] * window[plane, 1 - column_of, rows, :]
                    value = pltpu.roll(value, jnp.where(column_of == 0, over, column), 1)
                    pieces.append(jnp.where(inside.astype(jnp.int32) == column_of, value, 0.0))
                else:
                    pieces.append(jnp.where(inside, pltpu.roll(first, column, 1), 0.0))
                    pieces.append(jnp.where(inside, 0.0, pltpu.roll(second, over, 1)))
                for side, piece in enumerate(pieces):
                    acc[plane, side, target, :] = acc[plane, side, target, :] + piece
    for start, out in zip(row_starts, (own_out, near_out, far_out)):
        rows = pl.ds(start, tile)
        for side in range(sides):
            planes = [acc[plane, side, rows, :] for plane in range(4)]
            for j, block in enumerate(packed(planes, tile)):
                k = 3 * side + j
                out[:, k * LANES : (k + 1) * LANES] = block


def fold_kernel(own_ref, near_ref, far_ref, *outs):
    columns = outs[0].shape[1]
    for side, out in enumerate(outs):
        part = slice(side * columns, (side + 1) * columns)
        out[...] = own_ref[:, part] + near_ref[:, part] + far_ref[:, part]


def update_kernel(rate, cores, object_ref, probe_ref, *refs):
    object_out, probe_out = refs[-2:]
    sums = refs[:cores]
    tile = object_ref.shape[2]
    total = refs[cores][...]
    for ref in refs[cores + 1 : -2]:
        total = total + ref[...]
    parts = [total[:, j * LANES : (j + 1) * LANES] for j in range(3)]
    parts.append(last_of(parts, tile))
    for plane in range(4):
        object_out[plane // 2, plane % 2] = (
            object_ref[plane // 2, plane % 2] - object_rate * parts[plane][:, :tile]
        )
    width = probe_ref.shape[1]
    half = width // 2
    share = width // cores
    lane = lane_ids(share)
    for k, ref in enumerate(sums):
        start = share * lax.rem(lax.axis_index("core") + k, cores)
        rows = pl.ds(pl.multiple_of(start, 8), share)
        parts = [ref[j] for j in range(3)]
        parts.append(last_of(parts, half))
        for j in range(2):
            head, tail = parts[2 * j], pltpu.roll(parts[2 * j + 1], half, 1)
            probe_out[j, rows, :LANES] = probe_ref[j, rows, :LANES] - rate * jnp.where(
                lane < half, head, tail
            )
            probe_out[j, rows, LANES:] = (
                probe_ref[j, rows, LANES:] - rate * tail[:, : width - LANES]
            )


def passed_along(x, axis, by):
    peers = lax.axis_size(axis)
    pairs = [(i, i + by) for i in range(peers) if 0 <= i + by < peers]
    return lax.ppermute(x, axis, pairs)


def from_near(x, cores):
    if cores == 2:
        return lax.ppermute(x, "core", [(0, 1), (1, 0)])
    return passed_along(x, ROWS, 1)


def from_far(x, cores):
    if cores == 2:
        ends = range(1, lax.axis_size(ROWS) - 1, 2)
        pairs = [(i, i + 1) for i in ends] + [(i + 1, i) for i in ends]
        return lax.ppermute(x, ROWS, pairs)
    return passed_along(x, ROWS, -1)


def all_sum(x, group):
    count = math.prod(lax.axis_size(axis) for axis in group)
    shape = x.shape
    x = x.reshape(-1, 2, LANES)
    pairs = x.shape[0]
    piece = -(-pairs // count)
    if piece * count > pairs:
        x = jnp.pad(x, ((0, piece * count - pairs), (0, 0), (0, 0)))
    x = x.reshape(count, piece, 2, LANES)
    x = lax.all_to_all(x, group, 0, 0, tiled=True)
    x = jnp.broadcast_to(jnp.sum(x, 0)[None], x.shape)
    x = lax.all_to_all(x, group, 0, 0, tiled=True)
    return x.reshape(count * piece, 2, LANES)[:pairs].reshape(shape)


def shards(object_slices, probe, propagator_phase, measured, offsets, counts):
    tile = object_slices.shape[-1]
    width = probe.shape[-1]
    slots = measured.shape[2]
    cores = lax.axis_size("core")
    cols_count = lax.axis_size("col")
    devices = lax.axis_size(ROWS) * cols_count
    paired = cols_count == 2
    params = pltpu.CompilerParams(vmem_limit_bytes=60 * 1024 * 1024)

    def shape(*dims, kind=f32):
        return jax.ShapeDtypeStruct(dims, kind)

    cells = object_slices
    if paired:
        beside = [lax.ppermute(cells, "col", [(0, 1), (1, 0)])]
    else:
        beside = [passed_along(cells, "col", 1), passed_along(cells, "col", -1)]
    own = [cells] + beside
    near = [from_near(x, cores) for x in own]
    far = [from_far(x, cores) for x in own]

    columns, rows = sorters(width)
    wave, trans, intensities = pl.pallas_call(
        prepare_kernel,
        out_shape=[
            shape(2, width, 2 * LANES),
            shape(2, width, 2 * LANES),
            shape(slots, width, 2 * LANES),
        ],
        in_specs=[VMEM] * 6,
        out_specs=[VMEM] * 3,
    )(
        probe,
        jnp.cos(propagator_phase),
        jnp.sin(propagator_phase),
        measured,
        columns,
        rows,
    )

    total = slots * width
    sides = len(own)
    strip = shape(tile, sides * 3 * LANES)
    scratch = [
        pltpu.VMEM((4, 3, 3 * tile, LANES), f32),
        pltpu.VMEM((4, sides, 3 * tile, LANES), f32),
        pltpu.VMEM((4, 2, total, LANES), f32),
        pltpu.VMEM((4, 2, total, LANES), f32),
        pltpu.VMEM((2 * total, 4 * LANES), bf16),
        pltpu.VMEM((2 * total, 2 * LANES), f32),
        pltpu.VMEM((slots, 2, 3 * width, 2 * LANES), bf16),
        pltpu.VMEM((slots, 2, width, 2 * LANES), f32),
    ]
    term = shape(3, width // cores, LANES)
    scratch.append(pltpu.VMEM((cores,) + term.shape, f32))
    strips = pl.pallas_call(
        functools.partial(position_kernel, paired, cores),
        out_shape=[strip] * 3 + [term] * cores,
        in_specs=[SMEM, SMEM] + [VMEM] * (3 * sides + 7),
        out_specs=[VMEM] * (3 + cores),
        scratch_shapes=scratch,
        compiler_params=params,
    )(offsets, counts, *own, *near, *far, wave, trans, intensities, *matrices(width))
    own_strip, near_strip, far_strip = strips[:3]
    terms = strips[3:]

    if cores == 2:
        mine = all_sum(terms[0] + from_near(terms[1], cores), ("pair", "col"))
        sums = [mine, from_near(mine, cores)]
    else:
        sums = [all_sum(terms[0], ("pair", "col"))]
    if cores == 1:
        near_strip, far_strip = passed_along(near_strip, ROWS, -1), passed_along(far_strip, ROWS, 1)
    else:
        near_strip, far_strip = from_near(near_strip, cores), from_far(far_strip, cores)
    share = shape(tile, 3 * LANES)
    parts = pl.pallas_call(
        fold_kernel,
        out_shape=[share] * sides,
        in_specs=[VMEM] * 3,
        out_specs=[VMEM] * sides,
    )(own_strip, near_strip, far_strip)
    if paired:
        received = [lax.ppermute(parts[1], "col", [(0, 1), (1, 0)])]
    else:
        received = [passed_along(parts[1], "col", -1), passed_along(parts[2], "col", 1)]
    return pl.pallas_call(
        functools.partial(update_kernel, probe_rate / (slots * devices), cores),
        out_shape=[shape(*object_slices.shape), shape(*probe.shape)],
        in_specs=[VMEM] * (3 + cores + len(received)),
        out_specs=[VMEM] * 2,
    )(object_slices, probe, *sums, parts[0], *received)


def solution(mesh):
    rows, cols = mesh.devices.shape
    cores = 2 if rows % 2 == 0 else 1
    finer = Mesh(mesh.devices.reshape(rows // cores, cores, cols), ROWS + ("col",))
    return jax.shard_map(
        shards,
        mesh=finer,
        in_specs=(
            P(None, None, ROWS, "col"),
            P(),
            P(),
            P(ROWS, "col", None, None, None),
            P(ROWS, "col", None, None),
            P(ROWS, "col"),
        ),
        out_specs=(P(None, None, ROWS, "col"), P()),
        check_vma=False,
    )
```

```python
import functools
import math

import jax
import jax.numpy as jnp
import numpy as np
from jax import lax
from jax.experimental import pallas as pl
from jax.experimental.pallas import tpu as pltpu
from jax.sharding import Mesh
from jax.sharding import PartitionSpec as P

object_rate = 0.02
probe_rate = 0.3

LANES = 128
f32 = jnp.float32
bf16 = jnp.bfloat16
VMEM = pl.BlockSpec(memory_space=pltpu.VMEM)
SMEM = pl.BlockSpec(memory_space=pltpu.SMEM)
ROWS = ("pair", "core")


def matrices(width):
    half = width // 2
    k = np.arange(half)
    angle = (k[:, None] * k[None, :] % half) * (2.0 * math.pi / half)
    cosine = np.cos(angle) / math.sqrt(width)
    sine = np.sin(angle) / math.sqrt(width)
    right = np.zeros((2, LANES, 2, LANES))
    right[0, :half, 0, :half] = cosine
    right[0, :half, 1, :half] = -sine
    right[1, :half, 0, :half] = sine
    right[1, :half, 1, :half] = cosine
    right = right.reshape(2 * LANES, 2 * LANES)
    left = np.block([[cosine, sine], [-sine, cosine]])

    def halves(matrix):
        high = matrix.astype(np.float32).astype(bf16)
        low = (matrix - high.astype(np.float64)).astype(np.float32).astype(bf16)
        return high, low

    right_high, right_low = halves(right)
    left_high, left_low = halves(left)
    turn = k * (2.0 * math.pi / width)
    turns = np.stack([np.cos(turn), np.sin(turn)]).astype(np.float32)
    lane_turns = np.zeros((2, 8, LANES), np.float32)
    lane_turns[:, :, :half] = turns[:, None, :]
    row_turns = np.broadcast_to(turns[:, :, None], (2, half, LANES)).copy()
    return (
        np.concatenate([right_high, right_high, right_low], 0),
        np.concatenate([left_high, left_high, left_low], 1),
        lane_turns,
        row_turns,
    )


def sorters(width):
    half = width // 2
    columns = np.zeros((width, 2 * LANES), np.float32)
    rows = np.zeros((width, width), np.float32)
    for i in range(half):
        for j in range(2):
            columns[2 * i + j, j * LANES + i] = 1
            rows[j * half + i, 2 * i + j] = 1
    return columns.astype(bf16), rows.astype(bf16)


def times(a_real, a_imag, b_real, b_imag):
    return (a_real * b_real - a_imag * b_imag, a_real * b_imag + a_imag * b_real)


def times_conj(a_real, a_imag, b_real, b_imag):
    return (a_real * b_real + a_imag * b_imag, a_real * b_imag - a_imag * b_real)


def halves_of(value):
    high = value.astype(bf16)
    return high, (value - high.astype(f32)).astype(bf16)


def lane_ids(rows):
    return lax.broadcasted_iota(jnp.int32, (rows, LANES), 1)


def packed(planes, half):
    lane = lane_ids(planes[0].shape[0])
    rest = LANES - half
    return [
        jnp.where(lane < half, planes[j], pltpu.roll(planes[3], (half - rest * j) % LANES, 1))
        for j in range(3)
    ]


def last_of(parts, half):
    lane = lane_ids(parts[0].shape[0])
    rest = LANES - half
    out = pltpu.roll(parts[0], rest, 1)
    for j in range(1, 3):
        out = jnp.where(lane < rest * j, out, pltpu.roll(parts[j], (rest * j + rest) % LANES, 1))
    return out


def prepare_kernel(
    probe_ref,
    cosine_ref,
    sine_ref,
    measured_ref,
    columns_ref,
    rows_ref,
    wave_out,
    trans_out,
    measured_out,
):
    width = probe_ref.shape[1]
    half = width // 2
    lane = lane_ids(width)
    for j in range(2):
        head = probe_ref[j, :, :LANES]
        tail = jnp.concatenate(
            [probe_ref[j, :, LANES:], jnp.zeros((width, 2 * LANES - width), f32)], 1
        )
        rest = LANES - half
        wave_out[j, :, :LANES] = jnp.where(lane < half, head, 0.0)
        wave_out[j, :, LANES:] = jnp.where(
            lane < rest, pltpu.roll(head, rest, 1), pltpu.roll(tail, rest, 1)
        )
    planes = [(cosine_ref[...], trans_out, 0), (sine_ref[...], trans_out, 1)]
    for slot in range(measured_out.shape[0]):
        planes.append((measured_ref[0, 0, slot], measured_out, slot))
    for left, target, j in planes:
        total = jnp.zeros((width, 2 * LANES), f32)
        for part in range(3):
            piece = left.astype(bf16)
            left = left - piece.astype(f32)
            moved = jnp.dot(piece, columns_ref[...], preferred_element_type=f32)
            total = total + jnp.dot(rows_ref[...], moved.astype(bf16), preferred_element_type=f32)
        target[j] = total


def row_places(cores):
    core = lax.axis_index("core") if cores == 2 else 1
    return 1, 2 - 2 * core, 2 * core


def position_kernel(
    paired,
    cores,
    offsets_ref,
    counts_ref,
    *refs,
):
    sides = 2 if paired else 3
    tiles = refs[: 3 * sides]
    (
        wave_ref,
        trans_ref,
        measured_ref,
        right_ref,
        left_ref,
        lane_turn_ref,
        row_turn_ref,
        own_out,
        near_out,
        far_out,
    ) = refs[3 * sides : 3 * sides + 10]
    terms_out = refs[3 * sides + 10 : 3 * sides + 10 + cores]
    (
        obj,
        acc,
        window,
        carried,
        terms,
    ) = refs[3 * sides + 10 + cores : 3 * sides + 15 + cores]
    slots = measured_ref.shape[0]
    work = refs[3 * sides + 15 + cores :]
    data, out_right, mid, out_left = (work[k * slots : (k + 1) * slots] for k in range(4))
    width = wave_ref.shape[1]
    half = width // 2
    tile = obj.shape[2] // 3
    total = slots * width
    step = 16
    part_rows = half // 2
    lag = 2
    column_of = lax.axis_index("col")
    row_starts = [pl.multiple_of(place * tile, 8) for place in row_places(cores)]

    pad = jnp.zeros((tile, LANES - tile), f32)
    for row in range(3):
        rows = pl.ds(row_starts[row], tile)
        for side in range(sides):
            if paired:
                place = 1 if side == 0 else 2 - 2 * column_of
            else:
                place = (1, 0, 2)[side]
            for plane in range(4):
                value = tiles[row * sides + side][plane // 2, plane % 2]
                obj[plane, place, rows, :] = jnp.concatenate([value, pad], 1)
        if paired:
            for plane in range(4):
                obj[plane, 2 * column_of, rows, :] = jnp.zeros((tile, LANES), f32)

    shift = tile - half
    corners = [
        (offsets_ref[0, 0, slot, 0] + shift, offsets_ref[0, 0, slot, 1] + shift)
        for slot in range(slots)
    ]
    chunk = half
    lane = lane_ids(chunk)
    for slot in range(slots):
        row, column = corners[slot]
        back = lax.rem(LANES - column, LANES)
        inside = lane < tile - column
        for plane in range(4):
            for start in range(0, width, chunk):
                source = pl.ds(row + start, chunk)
                target = pl.ds(slot * width + start, chunk)
                for j in range(2):
                    window[plane, j, target, :] = jnp.where(
                        inside,
                        pltpu.roll(obj[plane, j, source, :], back, 1),
                        pltpu.roll(obj[plane, j + 1, source, :], tile - column, 1),
                    )
    acc[...] = jnp.zeros(acc.shape, f32)

    lane_turn = [jnp.broadcast_to(lane_turn_ref[j, :1, :], (step, LANES)) for j in range(2)]
    span = 2 * LANES

    def put(slot, block, row, a, b):
        rows = pl.ds(block * width + row, step)
        high, low = halves_of(jnp.concatenate([a, b], 1))
        data[slot][rows, :span] = high
        data[slot][rows, span:] = low

    def multiply_right(slot):
        for start in range(0, 2 * width, width):
            rows = slice(start, start + width)
            left = jnp.concatenate([data[slot][rows, :], data[slot][rows, :span]], 1)
            out_right[slot][rows, :] = jnp.dot(
                left, right_ref[...], preferred_element_type=f32
            )
            yield

    def put_mid(slot, block, start, first, second):
        for part in range(2):
            high, low = halves_of(jnp.concatenate([first[part], second[part]], 1))
            mid[slot][block, pl.ds(part * half + start, step), :] = high
            mid[slot][block, pl.ds((2 + part) * half + start, step), :] = low
            mid[slot][block, pl.ds((4 + part) * half + start, step), :] = high

    def multiply_left(slot):
        for block in range(2):
            out_left[slot][block] = jnp.dot(
                left_ref[...], mid[slot][block], preferred_element_type=f32
            )
            yield

    def get_right(slot, block, row):
        rows = pl.ds(block * width + row, step)
        return out_right[slot][rows, :LANES], out_right[slot][rows, LANES:]

    def get_left(slot, block, j, start):
        columns = slice(j * LANES, (j + 1) * LANES)
        return (
            out_left[slot][block, pl.ds(start, step), columns],
            out_left[slot][block, pl.ds(half + start, step), columns],
        )

    def row_turn(row):
        return row_turn_ref[0, pl.ds(row, step), :], row_turn_ref[1, pl.ds(row, step), :]

    def forward(slot, source):
        for row in range(0, half, step):
            for side, ((a0, b0), (a1, b1)) in enumerate(source(slot, row)):
                place = side * half + row
                put(slot, 0, place, a0 + a1, b0 + b1)
                put(slot, 1, place, *times_conj(*lane_turn, a0 - a1, b0 - b1))
            if row % part_rows == part_rows - step:
                yield
        yield from multiply_right(slot)
        for row in range(0, half, step):
            even, odd = [], []
            for j in range(2):
                a0, b0 = get_right(slot, j, row)
                a1, b1 = get_right(slot, j, half + row)
                even.append((a0 + a1, b0 + b1))
                odd.append(times_conj(*row_turn(row), a0 - a1, b0 - b1))
            put_mid(slot, 0, row, *even)
            put_mid(slot, 1, row, *odd)
            if row % part_rows == part_rows - step:
                yield
        yield from multiply_left(slot)

    def inverse(slot, source):
        for row in range(0, width, step):
            for j, (a, b) in enumerate(source(slot, row)):
                put(slot, j, row, a, b)
            if row % (2 * part_rows) == 2 * part_rows - step:
                yield
        yield from multiply_right(slot)
        for row in range(0, width, step):
            a0, b0 = get_right(slot, 0, row)
            a1, b1 = times_conj(*lane_turn, *get_right(slot, 1, row))
            put_mid(slot, row // half, row % half, (a0 + a1, b0 + b1), (a0 - a1, b0 - b1))
            if row % (2 * part_rows) == 2 * part_rows - step:
                yield
        yield from multiply_left(slot)

    def frequency(slot, row, j):
        return get_left(slot, row // half, j, row % half)

    def natural(slot, row, j):
        b0, a0 = get_left(slot, 0, j, row)
        b1, a1 = times_conj(*row_turn(row), *get_left(slot, 1, j, row))
        return (a0 + a1, b0 + b1), (a0 - a1, b0 - b1)

    def at(ref, first, row, j):
        rows = pl.ds(row, step)
        columns = slice(j * LANES, (j + 1) * LANES)
        return ref[first, rows, columns], ref[first + 1, rows, columns]

    def seen(ref, first, slot, row, j):
        rows = pl.ds(slot * width + row, step)
        return ref[first, j, rows, :], ref[first + 1, j, rows, :]

    def keep(ref, first, slot, row, j, real, imag):
        rows = pl.ds(slot * width + row, step)
        ref[first, j, rows, :] = real
        ref[first + 1, j, rows, :] = imag

    def entry(slot, row):
        return [
            [times(*at(wave_ref, 0, place, j), *seen(window, 0, slot, place, j)) for j in range(2)]
            for place in (row, half + row)
        ]

    def from_natural(handle):
        def source(slot, row):
            pairs = [natural(slot, row, j) for j in range(2)]
            return [
                [handle(slot, side * half + row, j, *pairs[j][side]) for j in range(2)]
                for side in range(2)
            ]

        return source

    def from_frequency(handle):
        def source(slot, row):
            out = []
            for j in range(2):
                real, imag = handle(slot, row, j, *frequency(slot, row, j))
                out.append((imag, real))
            return out

        return source

    @from_frequency
    def propagate(slot, row, j, real, imag):
        return times(*at(trans_ref, 0, row, j), real, imag)

    @from_natural
    def leave(slot, row, j, real, imag):
        keep(carried, 0, slot, row, j, real, imag)
        return times(real, imag, *seen(window, 2, slot, row, j))

    @from_frequency
    def residual(slot, row, j, real, imag):
        columns = slice(j * LANES, (j + 1) * LANES)
        factor = real * real + imag * imag - measured_ref[slot, pl.ds(row, step), columns]
        return factor * real, factor * imag

    @from_natural
    def before(slot, row, j, real, imag):
        inner = times_conj(*seen(window, 2, slot, row, j), real, imag)
        second = times_conj(*seen(carried, 0, slot, row, j), real, imag)
        keep(window, 2, slot, row, j, *second)
        return inner

    @from_frequency
    def propagate_back(slot, row, j, real, imag):
        return times_conj(*at(trans_ref, 0, row, j), real, imag)

    def stages(slot):
        yield from forward(slot, entry)
        yield from inverse(slot, propagate)
        yield from forward(slot, leave)
        yield from inverse(slot, residual)
        yield from forward(slot, before)
        yield from inverse(slot, propagate_back)

    running = [stages(slot) for slot in range(slots)]
    turn = 0
    while any(x is not None for x in running):
        for slot in range(slots):
            if running[slot] is not None and turn >= slot * lag:
                if next(running[slot], "end") == "end":
                    running[slot] = None
        turn += 1

    live = [(slot < counts_ref[0, 0]).astype(f32) for slot in range(slots)]
    core = lax.axis_index("core")
    share = width // cores
    for row in range(0, half, step):
        sums = [[None] * 4 for side in range(2)]
        for j in range(2):
            for slot in range(slots):
                for side, (real, imag) in enumerate(natural(slot, row, j)):
                    place = side * half + row
                    term = times_conj(*seen(window, 0, slot, place, j), real, imag)
                    keep(
                        window,
                        0,
                        slot,
                        place,
                        j,
                        *times_conj(*at(wave_ref, 0, place, j), real, imag),
                    )
                    for part in range(2):
                        value = live[slot] * term[part]
                        old = sums[side][2 * part + j]
                        sums[side][2 * part + j] = value if old is None else old + value
        for side in range(2):
            place = side * half + row
            which = lax.rem(place // share + core, cores)
            for j, block in enumerate(packed(sums[side], half)):
                terms[which, j, pl.ds(place % share, step), :] = block
    for k, out in enumerate(terms_out):
        out[...] = terms[k]

    for slot in range(slots):
        row, column = corners[slot]
        inside = lane >= column
        over = column + LANES - tile
        for plane in range(4):
            for start in range(0, width, chunk):
                rows = pl.ds(slot * width + start, chunk)
                target = pl.ds(row + start, chunk)
                first, second = (live[slot] * window[plane, j, rows, :] for j in range(2))
                pieces = [jnp.where(inside, pltpu.roll(second, column, 1), pltpu.roll(first, over, 1))]
                if paired:
                    value = live[slot] * window[plane, 1 - column_of, rows, :]
                    value = pltpu.roll(value, jnp.where(column_of == 0, over, column), 1)
                    pieces.append(jnp.where(inside.astype(jnp.int32) == column_of, value, 0.0))
                else:
                    pieces.append(jnp.where(inside, pltpu.roll(first, column, 1), 0.0))
                    pieces.append(jnp.where(inside, 0.0, pltpu.roll(second, over, 1)))
                for side, piece in enumerate(pieces):
                    acc[plane, side, target, :] = acc[plane, side, target, :] + piece
    for start, out in zip(row_starts, (own_out, near_out, far_out)):
        rows = pl.ds(start, tile)
        for side in range(sides):
            planes = [acc[plane, side, rows, :] for plane in range(4)]
            for j, block in enumerate(packed(planes, tile)):
                k = 3 * side + j
                out[:, k * LANES : (k + 1) * LANES] = block


def fold_kernel(own_ref, near_ref, far_ref, *outs):
    columns = outs[0].shape[1]
    for side, out in enumerate(outs):
        part = slice(side * columns, (side + 1) * columns)
        out[...] = own_ref[:, part] + near_ref[:, part] + far_ref[:, part]


def update_kernel(rate, cores, object_ref, probe_ref, *refs):
    object_out, probe_out = refs[-2:]
    sums = refs[:cores]
    tile = object_ref.shape[2]
    total = refs[cores][...]
    for ref in refs[cores + 1 : -2]:
        total = total + ref[...]
    parts = [total[:, j * LANES : (j + 1) * LANES] for j in range(3)]
    parts.append(last_of(parts, tile))
    for plane in range(4):
        object_out[plane // 2, plane % 2] = (
            object_ref[plane // 2, plane % 2] - object_rate * parts[plane][:, :tile]
        )
    width = probe_ref.shape[1]
    half = width // 2
    share = width // cores
    lane = lane_ids(share)
    for k, ref in enumerate(sums):
        start = share * lax.rem(lax.axis_index("core") + k, cores)
        rows = pl.ds(pl.multiple_of(start, 8), share)
        parts = [ref[j] for j in range(3)]
        parts.append(last_of(parts, half))
        for j in range(2):
            head, tail = parts[2 * j], pltpu.roll(parts[2 * j + 1], half, 1)
            probe_out[j, rows, :LANES] = probe_ref[j, rows, :LANES] - rate * jnp.where(
                lane < half, head, tail
            )
            probe_out[j, rows, LANES:] = (
                probe_ref[j, rows, LANES:] - rate * tail[:, : width - LANES]
            )


def passed_along(x, axis, by):
    peers = lax.axis_size(axis)
    pairs = [(i, i + by) for i in range(peers) if 0 <= i + by < peers]
    return lax.ppermute(x, axis, pairs)


def from_near(x, cores):
    if cores == 2:
        return lax.ppermute(x, "core", [(0, 1), (1, 0)])
    return passed_along(x, ROWS, 1)


def from_far(x, cores):
    if cores == 2:
        ends = range(1, lax.axis_size(ROWS) - 1, 2)
        pairs = [(i, i + 1) for i in ends] + [(i + 1, i) for i in ends]
        return lax.ppermute(x, ROWS, pairs)
    return passed_along(x, ROWS, -1)


def all_sum(x, group):
    count = math.prod(lax.axis_size(axis) for axis in group)
    shape = x.shape
    x = x.reshape(-1, 2, LANES)
    pairs = x.shape[0]
    piece = -(-pairs // count)
    if piece * count > pairs:
        x = jnp.pad(x, ((0, piece * count - pairs), (0, 0), (0, 0)))
    x = x.reshape(count, piece, 2, LANES)
    x = lax.all_to_all(x, group, 0, 0, tiled=True)
    x = jnp.broadcast_to(jnp.sum(x, 0)[None], x.shape)
    x = lax.all_to_all(x, group, 0, 0, tiled=True)
    return x.reshape(count * piece, 2, LANES)[:pairs].reshape(shape)


def shards(object_slices, probe, propagator_phase, measured, offsets, counts):
    tile = object_slices.shape[-1]
    width = probe.shape[-1]
    slots = measured.shape[2]
    cores = lax.axis_size("core")
    cols_count = lax.axis_size("col")
    devices = lax.axis_size(ROWS) * cols_count
    paired = cols_count == 2
    large = pltpu.CompilerParams(vmem_limit_bytes=18 * 1024 * 1024)
    small = pltpu.CompilerParams(vmem_limit_bytes=6 * 1024 * 1024)

    def shape(*dims, kind=f32):
        return jax.ShapeDtypeStruct(dims, kind)

    cells = object_slices
    if paired:
        beside = [lax.ppermute(cells, "col", [(0, 1), (1, 0)])]
    else:
        beside = [passed_along(cells, "col", 1), passed_along(cells, "col", -1)]
    own = [cells] + beside
    near = [from_near(x, cores) for x in own]
    far = [from_far(x, cores) for x in own]

    columns, rows = sorters(width)
    wave, trans, intensities = pl.pallas_call(
        prepare_kernel,
        out_shape=[
            shape(2, width, 2 * LANES),
            shape(2, width, 2 * LANES),
            shape(slots, width, 2 * LANES),
        ],
        in_specs=[VMEM] * 6,
        out_specs=[VMEM] * 3,
        compiler_params=small,
    )(
        probe,
        jnp.cos(propagator_phase),
        jnp.sin(propagator_phase),
        measured,
        columns,
        rows,
    )

    total = slots * width
    sides = len(own)
    strip = shape(tile, sides * 3 * LANES)
    scratch = [
        pltpu.VMEM((4, 3, 3 * tile, LANES), f32),
        pltpu.VMEM((4, sides, 3 * tile, LANES), f32),
        pltpu.VMEM((4, 2, total, LANES), f32),
        pltpu.VMEM((2, 2, total, LANES), f32),
        pltpu.VMEM((cores, 3, width // cores, LANES), f32),
    ]
    scratch += [pltpu.VMEM((2 * width, 4 * LANES), bf16)] * slots
    scratch += [pltpu.VMEM((2 * width, 2 * LANES), f32)] * slots
    scratch += [pltpu.VMEM((2, 3 * width, 2 * LANES), bf16)] * slots
    scratch += [pltpu.VMEM((2, width, 2 * LANES), f32)] * slots
    term = shape(3, width // cores, LANES)
    strips = pl.pallas_call(
        functools.partial(position_kernel, paired, cores),
        out_shape=[strip] * 3 + [term] * cores,
        in_specs=[SMEM, SMEM] + [VMEM] * (3 * sides + 7),
        out_specs=[VMEM] * (3 + cores),
        scratch_shapes=scratch,
        compiler_params=large,
    )(offsets, counts, *own, *near, *far, wave, trans, intensities, *matrices(width))
    own_strip, near_strip, far_strip = strips[:3]
    terms = strips[3:]

    if cores == 2:
        mine = all_sum(terms[0] + from_near(terms[1], cores), ("pair", "col"))
        sums = [mine, from_near(mine, cores)]
    else:
        sums = [all_sum(terms[0], ("pair", "col"))]
    if cores == 1:
        near_strip, far_strip = passed_along(near_strip, ROWS, -1), passed_along(far_strip, ROWS, 1)
    else:
        near_strip, far_strip = from_near(near_strip, cores), from_far(far_strip, cores)
    share = shape(tile, 3 * LANES)
    parts = pl.pallas_call(
        fold_kernel,
        out_shape=[share] * sides,
        in_specs=[VMEM] * 3,
        out_specs=[VMEM] * sides,
        compiler_params=small,
    )(own_strip, near_strip, far_strip)
    if paired:
        received = [lax.ppermute(parts[1], "col", [(0, 1), (1, 0)])]
    else:
        received = [passed_along(parts[1], "col", -1), passed_along(parts[2], "col", 1)]
    return pl.pallas_call(
        functools.partial(update_kernel, probe_rate / (slots * devices), cores),
        out_shape=[shape(*object_slices.shape), shape(*probe.shape)],
        in_specs=[VMEM] * (3 + cores + len(received)),
        out_specs=[VMEM] * 2,
        compiler_params=small,
    )(object_slices, probe, *sums, parts[0], *received)


def solution(mesh):
    rows, cols = mesh.devices.shape
    cores = 2 if rows % 2 == 0 else 1
    finer = Mesh(mesh.devices.reshape(rows // cores, cores, cols), ROWS + ("col",))
    return jax.shard_map(
        shards,
        mesh=finer,
        in_specs=(
            P(None, None, ROWS, "col"),
            P(),
            P(),
            P(ROWS, "col", None, None, None),
            P(ROWS, "col", None, None),
            P(ROWS, "col"),
        ),
        out_specs=(P(None, None, ROWS, "col"), P()),
        check_vma=False,
    )
```

```python
import functools
import math

import jax
import jax.numpy as jnp
import numpy as np
from jax import lax
from jax.experimental import pallas as pl
from jax.experimental.pallas import tpu as pltpu
from jax.sharding import Mesh
from jax.sharding import PartitionSpec as P

object_rate = 0.02
probe_rate = 0.3

LANES = 128
f32 = jnp.float32
bf16 = jnp.bfloat16
VMEM = pl.BlockSpec(memory_space=pltpu.VMEM)
SMEM = pl.BlockSpec(memory_space=pltpu.SMEM)
ANY = pl.BlockSpec(memory_space=pl.ANY)
ROWS = ("pair", "core")


def matrices(width):
    half = width // 2
    k = np.arange(half)
    angle = (k[:, None] * k[None, :] % half) * (2.0 * math.pi / half)
    cosine = np.cos(angle) / math.sqrt(width)
    sine = np.sin(angle) / math.sqrt(width)
    right = np.zeros((2, LANES, 2, LANES))
    right[0, :half, 0, :half] = cosine
    right[0, :half, 1, :half] = -sine
    right[1, :half, 0, :half] = sine
    right[1, :half, 1, :half] = cosine
    right = right.reshape(2 * LANES, 2 * LANES)
    left = np.block([[cosine, sine], [-sine, cosine]])

    def halves(matrix):
        high = matrix.astype(np.float32).astype(bf16)
        low = (matrix - high.astype(np.float64)).astype(np.float32).astype(bf16)
        return high, low

    right_high, right_low = halves(right)
    left_high, left_low = halves(left)
    turn = k * (2.0 * math.pi / width)
    turns = np.stack([np.cos(turn), np.sin(turn)]).astype(np.float32)
    lane_turns = np.zeros((2, 8, LANES), np.float32)
    lane_turns[:, :, :half] = turns[:, None, :]
    row_turns = np.broadcast_to(turns[:, :, None], (2, half, LANES)).copy()
    return (
        np.concatenate([right_high, right_high, right_low], 0),
        np.concatenate([left_high, left_high, left_low], 1),
        lane_turns,
        row_turns,
    )


def sorters(width):
    half = width // 2

    def ids(shape, axis):
        return lax.broadcasted_iota(jnp.int32, shape, axis)

    shape = (width, 2 * LANES)
    source = ids(shape, 0)
    columns = ids(shape, 1) == (source & 1) * LANES + (source >> 1)
    shape = (width, width)
    target = ids(shape, 0)
    rows = ids(shape, 1) == jnp.where(target < half, 2 * target, 2 * (target - half) + 1)
    return [jnp.where(x, 1.0, 0.0).astype(bf16) for x in (columns, rows)]


def times(a_real, a_imag, b_real, b_imag):
    return (a_real * b_real - a_imag * b_imag, a_real * b_imag + a_imag * b_real)


def times_conj(a_real, a_imag, b_real, b_imag):
    return (a_real * b_real + a_imag * b_imag, a_real * b_imag - a_imag * b_real)


def halves_of(value):
    high = value.astype(bf16)
    return high, (value - high.astype(f32)).astype(bf16)


def lane_ids(rows):
    return lax.broadcasted_iota(jnp.int32, (rows, LANES), 1)


def packed(planes, half):
    lane = lane_ids(planes[0].shape[0])
    rest = LANES - half
    return [
        jnp.where(lane < half, planes[j], pltpu.roll(planes[3], (half - rest * j) % LANES, 1))
        for j in range(3)
    ]


def last_of(parts, half):
    lane = lane_ids(parts[0].shape[0])
    rest = LANES - half
    out = pltpu.roll(parts[0], rest, 1)
    for j in range(1, 3):
        out = jnp.where(lane < rest * j, out, pltpu.roll(parts[j], (rest * j + rest) % LANES, 1))
    return out


def cosine_and_sine(x):
    turns = jnp.floor(x * (2.0 / math.pi) + 0.5)
    rest = ((x - turns * 1.5703125) - turns * 4.837512969970703125e-4) - turns * 7.54978995489188e-8
    square = rest * rest
    sine = ((-1.9515295891e-4 * square + 8.3321608736e-3) * square - 1.6666654611e-1) * square
    sine = sine * rest + rest
    cosine = (2.443315711809948e-5 * square - 1.388731625493765e-3) * square + 4.166664568298827e-2
    cosine = cosine * square * square - 0.5 * square + 1.0
    quarter = turns.astype(jnp.int32) & 3
    odd = (quarter & 1) == 1
    return (
        jnp.where(odd, sine, cosine) * jnp.where((quarter == 1) | (quarter == 2), -1.0, 1.0),
        jnp.where(odd, cosine, sine) * jnp.where(quarter >= 2, -1.0, 1.0),
    )


def pack_kernel(object_ref, out_ref):
    tile = object_ref.shape[2]
    pad = jnp.zeros((tile, LANES - tile), f32)
    planes = [
        jnp.concatenate([object_ref[plane // 2, plane % 2], pad], 1) for plane in range(4)
    ]
    for j, block in enumerate(packed(planes, tile)):
        out_ref[:, j * LANES : (j + 1) * LANES] = block


def prepare_kernel(
    offsets_ref,
    counts_ref,
    probe_ref,
    phase_ref,
    measured_ref,
    wave_out,
    trans_out,
    measured_out,
    places_out,
):
    lanes = lax.broadcasted_iota(jnp.int32, places_out.shape, 1)
    slots = measured_out.shape[0]
    places = jnp.where(lanes == 2 * slots, counts_ref[0, 0], 0)
    for slot in range(slots):
        for axis in range(2):
            places = jnp.where(lanes == 2 * slot + axis, offsets_ref[0, 0, slot, axis], places)
    places_out[...] = places
    width = probe_ref.shape[1]
    half = width // 2
    lane = lane_ids(width)
    for j in range(2):
        head = probe_ref[j, :, :LANES]
        tail = jnp.concatenate(
            [probe_ref[j, :, LANES:], jnp.zeros((width, 2 * LANES - width), f32)], 1
        )
        rest = LANES - half
        wave_out[j, :, :LANES] = jnp.where(lane < half, head, 0.0)
        wave_out[j, :, LANES:] = jnp.where(
            lane < rest, pltpu.roll(head, rest, 1), pltpu.roll(tail, rest, 1)
        )
    columns, rows = sorters(width)
    planes = [phase_ref[...]] + [measured_ref[0, 0, j] for j in range(measured_out.shape[0])]
    for j, left in enumerate(planes):
        total = jnp.zeros((width, 2 * LANES), f32)
        for part in range(3):
            piece = left.astype(bf16)
            left = left - piece.astype(f32)
            moved = jnp.dot(piece, columns, preferred_element_type=f32)
            total = total + jnp.dot(rows, moved.astype(bf16), preferred_element_type=f32)
        if j > 0:
            measured_out[j - 1] = total
            continue
        used = lax.rem(lax.broadcasted_iota(jnp.int32, total.shape, 1), LANES) < half
        for side, value in enumerate(cosine_and_sine(total)):
            trans_out[side] = jnp.where(used, value, 0.0)


def row_places(cores):
    core = lax.axis_index("core") if cores == 2 else 1
    return 1, 2 - 2 * core, 2 * core


def position_kernel(
    paired,
    cores,
    places_ref,
    *refs,
):
    sides = 2 if paired else 3
    tiles = refs[: 3 * sides]
    (
        wave_ref,
        trans_ref,
        measured_ref,
        right_ref,
        left_ref,
        lane_turn_ref,
        row_turn_ref,
        own_out,
        near_out,
        far_out,
    ) = refs[3 * sides : 3 * sides + 10]
    terms_out = refs[3 * sides + 10 : 3 * sides + 10 + cores]
    (
        obj,
        acc,
        window,
        carried,
        terms,
        places,
        arrived,
    ) = refs[3 * sides + 10 + cores : 3 * sides + 17 + cores]
    copy = pltpu.make_async_copy(places_ref, places, arrived)
    copy.start()
    slots = measured_ref.shape[0]
    work = refs[3 * sides + 17 + cores :]
    data, out_right, mid, out_left = (work[k * slots : (k + 1) * slots] for k in range(4))
    width = wave_ref.shape[1]
    half = width // 2
    tile = obj.shape[2] // 3
    total = slots * width
    step = 16
    part_rows = half // 2
    lag = 2
    column_of = lax.axis_index("col")
    row_starts = [pl.multiple_of(place * tile, 8) for place in row_places(cores)]

    for row in range(3):
        rows = pl.ds(row_starts[row], tile)
        for side in range(sides):
            if paired:
                place = 1 if side == 0 else 2 - 2 * column_of
            else:
                place = (1, 0, 2)[side]
            ref = tiles[row * sides + side]
            parts = [ref[:, j * LANES : (j + 1) * LANES] for j in range(3)]
            parts.append(last_of(parts, tile))
            for plane in range(4):
                obj[plane, place, rows, :] = parts[plane]
        if paired:
            for plane in range(4):
                obj[plane, 2 * column_of, rows, :] = jnp.zeros((tile, LANES), f32)

    copy.wait()
    shift = tile - half
    corners = [
        (places[0, 2 * slot] + shift, places[0, 2 * slot + 1] + shift)
        for slot in range(slots)
    ]
    chunk = half
    lane = lane_ids(chunk)
    for slot in range(slots):
        row, column = corners[slot]
        back = lax.rem(LANES - column, LANES)
        inside = lane < tile - column
        for plane in range(4):
            for start in range(0, width, chunk):
                source = pl.ds(row + start, chunk)
                target = pl.ds(slot * width + start, chunk)
                for j in range(2):
                    window[plane, j, target, :] = jnp.where(
                        inside,
                        pltpu.roll(obj[plane, j, source, :], back, 1),
                        pltpu.roll(obj[plane, j + 1, source, :], tile - column, 1),
                    )
    acc[...] = jnp.zeros(acc.shape, f32)

    lane_turn = [jnp.broadcast_to(lane_turn_ref[j, :1, :], (step, LANES)) for j in range(2)]
    span = 2 * LANES

    def put(slot, block, row, a, b):
        rows = pl.ds(block * width + row, step)
        high, low = halves_of(jnp.concatenate([a, b], 1))
        data[slot][rows, :span] = high
        data[slot][rows, span:] = low

    def multiply_right(slot):
        for start in range(0, 2 * width, width):
            rows = slice(start, start + width)
            left = jnp.concatenate([data[slot][rows, :], data[slot][rows, :span]], 1)
            out_right[slot][rows, :] = jnp.dot(
                left, right_ref[...], preferred_element_type=f32
            )
            yield

    def put_mid(slot, block, start, first, second):
        for part in range(2):
            high, low = halves_of(jnp.concatenate([first[part], second[part]], 1))
            mid[slot][block, pl.ds(part * half + start, step), :] = high
            mid[slot][block, pl.ds((2 + part) * half + start, step), :] = low
            mid[slot][block, pl.ds((4 + part) * half + start, step), :] = high

    def multiply_left(slot):
        for block in range(2):
            out_left[slot][block] = jnp.dot(
                left_ref[...], mid[slot][block], preferred_element_type=f32
            )
            yield

    def get_right(slot, block, row):
        rows = pl.ds(block * width + row, step)
        return out_right[slot][rows, :LANES], out_right[slot][rows, LANES:]

    def get_left(slot, block, j, start):
        columns = slice(j * LANES, (j + 1) * LANES)
        return (
            out_left[slot][block, pl.ds(start, step), columns],
            out_left[slot][block, pl.ds(half + start, step), columns],
        )

    def row_turn(row):
        return row_turn_ref[0, pl.ds(row, step), :], row_turn_ref[1, pl.ds(row, step), :]

    def forward(slot, source):
        for row in range(0, half, step):
            for side, ((a0, b0), (a1, b1)) in enumerate(source(slot, row)):
                place = side * half + row
                put(slot, 0, place, a0 + a1, b0 + b1)
                put(slot, 1, place, *times_conj(*lane_turn, a0 - a1, b0 - b1))
            if row % part_rows == part_rows - step:
                yield
        yield from multiply_right(slot)
        for row in range(0, half, step):
            even, odd = [], []
            for j in range(2):
                a0, b0 = get_right(slot, j, row)
                a1, b1 = get_right(slot, j, half + row)
                even.append((a0 + a1, b0 + b1))
                odd.append(times_conj(*row_turn(row), a0 - a1, b0 - b1))
            put_mid(slot, 0, row, *even)
            put_mid(slot, 1, row, *odd)
            if row % part_rows == part_rows - step:
                yield
        yield from multiply_left(slot)

    def inverse(slot, source):
        for row in range(0, width, step):
            for j, (a, b) in enumerate(source(slot, row)):
                put(slot, j, row, a, b)
            if row % (2 * part_rows) == 2 * part_rows - step:
                yield
        yield from multiply_right(slot)
        for row in range(0, width, step):
            a0, b0 = get_right(slot, 0, row)
            a1, b1 = times_conj(*lane_turn, *get_right(slot, 1, row))
            put_mid(slot, row // half, row % half, (a0 + a1, b0 + b1), (a0 - a1, b0 - b1))
            if row % (2 * part_rows) == 2 * part_rows - step:
                yield
        yield from multiply_left(slot)

    def frequency(slot, row, j):
        return get_left(slot, row // half, j, row % half)

    def natural(slot, row, j):
        b0, a0 = get_left(slot, 0, j, row)
        b1, a1 = times_conj(*row_turn(row), *get_left(slot, 1, j, row))
        return (a0 + a1, b0 + b1), (a0 - a1, b0 - b1)

    def at(ref, first, row, j):
        rows = pl.ds(row, step)
        columns = slice(j * LANES, (j + 1) * LANES)
        return ref[first, rows, columns], ref[first + 1, rows, columns]

    def seen(ref, first, slot, row, j):
        rows = pl.ds(slot * width + row, step)
        return ref[first, j, rows, :], ref[first + 1, j, rows, :]

    def keep(ref, first, slot, row, j, real, imag):
        rows = pl.ds(slot * width + row, step)
        ref[first, j, rows, :] = real
        ref[first + 1, j, rows, :] = imag

    def entry(slot, row):
        return [
            [times(*at(wave_ref, 0, place, j), *seen(window, 0, slot, place, j)) for j in range(2)]
            for place in (row, half + row)
        ]

    def from_natural(handle):
        def source(slot, row):
            pairs = [natural(slot, row, j) for j in range(2)]
            return [
                [handle(slot, side * half + row, j, *pairs[j][side]) for j in range(2)]
                for side in range(2)
            ]

        return source

    def from_frequency(handle):
        def source(slot, row):
            out = []
            for j in range(2):
                real, imag = handle(slot, row, j, *frequency(slot, row, j))
                out.append((imag, real))
            return out

        return source

    @from_frequency
    def propagate(slot, row, j, real, imag):
        return times(*at(trans_ref, 0, row, j), real, imag)

    @from_natural
    def leave(slot, row, j, real, imag):
        keep(carried, 0, slot, row, j, real, imag)
        return times(real, imag, *seen(window, 2, slot, row, j))

    @from_frequency
    def residual(slot, row, j, real, imag):
        columns = slice(j * LANES, (j + 1) * LANES)
        factor = real * real + imag * imag - measured_ref[slot, pl.ds(row, step), columns]
        return factor * real, factor * imag

    @from_natural
    def before(slot, row, j, real, imag):
        inner = times_conj(*seen(window, 2, slot, row, j), real, imag)
        second = times_conj(*seen(carried, 0, slot, row, j), real, imag)
        keep(window, 2, slot, row, j, *second)
        return inner

    @from_frequency
    def propagate_back(slot, row, j, real, imag):
        return times_conj(*at(trans_ref, 0, row, j), real, imag)

    def stages(slot):
        yield from forward(slot, entry)
        yield from inverse(slot, propagate)
        yield from forward(slot, leave)
        yield from inverse(slot, residual)
        yield from forward(slot, before)
        yield from inverse(slot, propagate_back)

    running = [stages(slot) for slot in range(slots)]
    turn = 0
    while any(x is not None for x in running):
        for slot in range(slots):
            if running[slot] is not None and turn >= slot * lag:
                if next(running[slot], "end") == "end":
                    running[slot] = None
        turn += 1

    live = [(slot < places[0, 2 * slots]).astype(f32) for slot in range(slots)]
    core = lax.axis_index("core")
    share = width // cores
    for row in range(0, half, step):
        sums = [[None] * 4 for side in range(2)]
        for j in range(2):
            for slot in range(slots):
                for side, (real, imag) in enumerate(natural(slot, row, j)):
                    place = side * half + row
                    term = times_conj(*seen(window, 0, slot, place, j), real, imag)
                    keep(
                        window,
                        0,
                        slot,
                        place,
                        j,
                        *times_conj(*at(wave_ref, 0, place, j), real, imag),
                    )
                    for part in range(2):
                        value = live[slot] * term[part]
                        old = sums[side][2 * part + j]
                        sums[side][2 * part + j] = value if old is None else old + value
        for side in range(2):
            place = side * half + row
            which = lax.rem(place // share + core, cores)
            for j, block in enumerate(packed(sums[side], half)):
                terms[which, j, pl.ds(place % share, step), :] = block
    for k, out in enumerate(terms_out):
        out[...] = terms[k]

    for slot in range(slots):
        row, column = corners[slot]
        inside = lane >= column
        over = column + LANES - tile
        for plane in range(4):
            for start in range(0, width, chunk):
                rows = pl.ds(slot * width + start, chunk)
                target = pl.ds(row + start, chunk)
                first, second = (live[slot] * window[plane, j, rows, :] for j in range(2))
                pieces = [jnp.where(inside, pltpu.roll(second, column, 1), pltpu.roll(first, over, 1))]
                if paired:
                    value = live[slot] * window[plane, 1 - column_of, rows, :]
                    value = pltpu.roll(value, jnp.where(column_of == 0, over, column), 1)
                    pieces.append(jnp.where(inside.astype(jnp.int32) == column_of, value, 0.0))
                else:
                    pieces.append(jnp.where(inside, pltpu.roll(first, column, 1), 0.0))
                    pieces.append(jnp.where(inside, 0.0, pltpu.roll(second, over, 1)))
                for side, piece in enumerate(pieces):
                    acc[plane, side, target, :] = acc[plane, side, target, :] + piece
    for start, out in zip(row_starts, (own_out, near_out, far_out)):
        rows = pl.ds(start, tile)
        for side in range(sides):
            planes = [acc[plane, side, rows, :] for plane in range(4)]
            for j, block in enumerate(packed(planes, tile)):
                k = 3 * side + j
                out[:, k * LANES : (k + 1) * LANES] = block


def fold_kernel(own_ref, near_ref, far_ref, *outs):
    columns = outs[0].shape[1]
    for side, out in enumerate(outs):
        part = slice(side * columns, (side + 1) * columns)
        out[...] = own_ref[:, part] + near_ref[:, part] + far_ref[:, part]


def update_kernel(rate, cores, object_ref, probe_ref, *refs):
    object_out, probe_out = refs[-2:]
    sums = refs[:cores]
    tile = object_ref.shape[2]
    total = refs[cores][...]
    for ref in refs[cores + 1 : -2]:
        total = total + ref[...]
    parts = [total[:, j * LANES : (j + 1) * LANES] for j in range(3)]
    parts.append(last_of(parts, tile))
    for plane in range(4):
        object_out[plane // 2, plane % 2] = (
            object_ref[plane // 2, plane % 2] - object_rate * parts[plane][:, :tile]
        )
    width = probe_ref.shape[1]
    half = width // 2
    share = width // cores
    lane = lane_ids(share)
    for k, ref in enumerate(sums):
        start = share * lax.rem(lax.axis_index("core") + k, cores)
        rows = pl.ds(pl.multiple_of(start, 8), share)
        parts = [ref[j] for j in range(3)]
        parts.append(last_of(parts, half))
        for j in range(2):
            head, tail = parts[2 * j], pltpu.roll(parts[2 * j + 1], half, 1)
            probe_out[j, rows, :LANES] = probe_ref[j, rows, :LANES] - rate * jnp.where(
                lane < half, head, tail
            )
            probe_out[j, rows, LANES:] = (
                probe_ref[j, rows, LANES:] - rate * tail[:, : width - LANES]
            )


def passed_along(x, axis, by):
    peers = lax.axis_size(axis)
    pairs = [(i, i + by) for i in range(peers) if 0 <= i + by < peers]
    return lax.ppermute(x, axis, pairs)


def from_near(x, cores):
    if cores == 2:
        return lax.ppermute(x, "core", [(0, 1), (1, 0)])
    return passed_along(x, ROWS, 1)


def from_far(x, cores):
    if cores == 2:
        ends = range(1, lax.axis_size(ROWS) - 1, 2)
        pairs = [(i, i + 1) for i in ends] + [(i + 1, i) for i in ends]
        return lax.ppermute(x, ROWS, pairs)
    return passed_along(x, ROWS, -1)


def from_far_beside(x):
    ends = range(1, lax.axis_size(ROWS) - 1, 2)
    pairs = []
    for i in ends:
        for j in range(2):
            pairs += [(2 * i + j, 2 * i + 3 - j), (2 * i + 2 + j, 2 * i + 1 - j)]
    return lax.ppermute(x, ROWS + ("col",), pairs)


def all_sum(x, group):
    count = math.prod(lax.axis_size(axis) for axis in group)
    shape = x.shape
    x = x.reshape(-1, 2, LANES)
    pairs = x.shape[0]
    piece = -(-pairs // count)
    if piece * count > pairs:
        x = jnp.pad(x, ((0, piece * count - pairs), (0, 0), (0, 0)))
    x = x.reshape(count, piece, 2, LANES)
    x = lax.all_to_all(x, group, 0, 0, tiled=True)
    x = jnp.broadcast_to(jnp.sum(x, 0)[None], x.shape)
    x = lax.all_to_all(x, group, 0, 0, tiled=True)
    return x.reshape(count * piece, 2, LANES)[:pairs].reshape(shape)


def shards(object_slices, probe, propagator_phase, measured, offsets, counts):
    tile = object_slices.shape[-1]
    width = probe.shape[-1]
    slots = measured.shape[2]
    cores = lax.axis_size("core")
    cols_count = lax.axis_size("col")
    devices = lax.axis_size(ROWS) * cols_count
    paired = cols_count == 2
    large = pltpu.CompilerParams(vmem_limit_bytes=18 * 1024 * 1024)
    small = pltpu.CompilerParams(vmem_limit_bytes=6 * 1024 * 1024)

    def shape(*dims, kind=f32):
        return jax.ShapeDtypeStruct(dims, kind)

    cells = pl.pallas_call(
        pack_kernel,
        out_shape=shape(tile, 3 * LANES),
        in_specs=[VMEM],
        out_specs=VMEM,
        cost_estimate=pl.CostEstimate(flops=10**10, bytes_accessed=10**7, transcendentals=0),
        compiler_params=small,
    )(object_slices)
    if paired:
        beside = [lax.ppermute(cells, "col", [(0, 1), (1, 0)])]
    else:
        beside = [passed_along(cells, "col", 1), passed_along(cells, "col", -1)]
    own = [cells] + beside
    near = [from_near(x, cores) for x in own]
    if paired and cores == 2:
        far = [from_far(cells, cores), from_far_beside(cells)]
    else:
        far = [from_far(x, cores) for x in own]

    wave, trans, intensities, places = pl.pallas_call(
        prepare_kernel,
        out_shape=[
            shape(2, width, 2 * LANES),
            shape(2, width, 2 * LANES),
            shape(slots, width, 2 * LANES),
            shape(8, LANES, kind=jnp.int32),
        ],
        in_specs=[SMEM] * 2 + [VMEM] * 3,
        out_specs=[VMEM] * 4,
        cost_estimate=pl.CostEstimate(flops=10**10, bytes_accessed=10**7, transcendentals=0),
        compiler_params=small,
    )(offsets, counts, probe, propagator_phase, measured)

    total = slots * width
    sides = len(own)
    strip = shape(tile, sides * 3 * LANES)
    scratch = [
        pltpu.VMEM((4, 3, 3 * tile, LANES), f32),
        pltpu.VMEM((4, sides, 3 * tile, LANES), f32),
        pltpu.VMEM((4, 2, total, LANES), f32),
        pltpu.VMEM((2, 2, total, LANES), f32),
        pltpu.VMEM((cores, 3, width // cores, LANES), f32),
        pltpu.SMEM((8, LANES), jnp.int32),
        pltpu.SemaphoreType.DMA,
    ]
    scratch += [pltpu.VMEM((2 * width, 4 * LANES), bf16)] * slots
    scratch += [pltpu.VMEM((2 * width, 2 * LANES), f32)] * slots
    scratch += [pltpu.VMEM((2, 3 * width, 2 * LANES), bf16)] * slots
    scratch += [pltpu.VMEM((2, width, 2 * LANES), f32)] * slots
    term = shape(3, width // cores, LANES)
    strips = pl.pallas_call(
        functools.partial(position_kernel, paired, cores),
        out_shape=[strip] * 3 + [term] * cores,
        in_specs=[ANY] + [VMEM] * (3 * sides + 7),
        out_specs=[VMEM] * (3 + cores),
        scratch_shapes=scratch,
        compiler_params=large,
    )(places, *own, *near, *far, wave, trans, intensities, *matrices(width))
    own_strip, near_strip, far_strip = strips[:3]
    terms = strips[3:]

    if cores == 2:
        mine = all_sum(terms[0] + from_near(terms[1], cores), ("pair", "col"))
        sums = [mine, from_near(mine, cores)]
    else:
        sums = [all_sum(terms[0], ("pair", "col"))]
    if cores == 1:
        near_strip, far_strip = passed_along(near_strip, ROWS, -1), passed_along(far_strip, ROWS, 1)
    else:
        near_strip, far_strip = from_near(near_strip, cores), from_far(far_strip, cores)
    share = shape(tile, 3 * LANES)
    parts = pl.pallas_call(
        fold_kernel,
        out_shape=[share] * sides,
        in_specs=[VMEM] * 3,
        out_specs=[VMEM] * sides,
        compiler_params=small,
    )(own_strip, near_strip, far_strip)
    if paired:
        received = [lax.ppermute(parts[1], "col", [(0, 1), (1, 0)])]
    else:
        received = [passed_along(parts[1], "col", -1), passed_along(parts[2], "col", 1)]
    return pl.pallas_call(
        functools.partial(update_kernel, probe_rate / (slots * devices), cores),
        out_shape=[shape(*object_slices.shape), shape(*probe.shape)],
        in_specs=[VMEM] * (3 + cores + len(received)),
        out_specs=[VMEM] * 2,
        compiler_params=small,
    )(object_slices, probe, *sums, parts[0], *received)


def solution(mesh):
    rows, cols = mesh.devices.shape
    cores = 2 if rows % 2 == 0 else 1
    finer = Mesh(mesh.devices.reshape(rows // cores, cores, cols), ROWS + ("col",))
    return jax.shard_map(
        shards,
        mesh=finer,
        in_specs=(
            P(None, None, ROWS, "col"),
            P(),
            P(),
            P(ROWS, "col", None, None, None),
            P(ROWS, "col", None, None),
            P(ROWS, "col"),
        ),
        out_specs=(P(None, None, ROWS, "col"), P()),
        check_vma=False,
    )
```

```python
import functools
import math

import jax
import jax.numpy as jnp
import numpy as np
from jax import lax
from jax.experimental import pallas as pl
from jax.experimental.pallas import tpu as pltpu
from jax.sharding import Mesh
from jax.sharding import PartitionSpec as P

object_rate = 0.02
probe_rate = 0.3

LANES = 128
f32 = jnp.float32
bf16 = jnp.bfloat16
VMEM = pl.BlockSpec(memory_space=pltpu.VMEM)
ANY = pl.BlockSpec(memory_space=pl.ANY)
ROWS = ("pair", "core")


def matrices(width):
    half = width // 2
    k = np.arange(half)
    turns = [2 * k[:, None] * k[None, :], k[:, None] * (2 * k[None, :] + 1)]
    turns.append(turns[1].T)
    rights, lefts = [], []

    def halves(matrix):
        high = matrix.astype(np.float32).astype(bf16)
        low = (matrix - high.astype(np.float64)).astype(np.float32).astype(bf16)
        return high, low

    for turn in turns:
        angle = (turn % width) * (2.0 * math.pi / width)
        cosine = np.cos(angle) / math.sqrt(width)
        sine = np.sin(angle) / math.sqrt(width)
        right = np.zeros((2, LANES, 2, LANES))
        right[0, :half, 0, :half] = cosine
        right[0, :half, 1, :half] = -sine
        right[1, :half, 0, :half] = sine
        right[1, :half, 1, :half] = cosine
        high, low = halves(right.reshape(2 * LANES, 2 * LANES))
        rights.append(np.stack([high, low]))
        high, low = halves(np.block([[cosine.T, sine.T], [-sine.T, cosine.T]]))
        lefts.append(np.concatenate([high, low], 0))
    return np.stack(rights), np.stack(lefts)


def sorters(width):
    half = width // 2

    def ids(shape, axis):
        return lax.broadcasted_iota(jnp.int32, shape, axis)

    shape = (width, 2 * LANES)
    source = ids(shape, 0)
    columns = ids(shape, 1) == (source & 1) * LANES + (source >> 1)
    shape = (width, width)
    target = ids(shape, 0)
    rows = ids(shape, 1) == jnp.where(target < half, 2 * target, 2 * (target - half) + 1)
    return [jnp.where(x, 1.0, 0.0).astype(bf16) for x in (columns, rows)]


def times(a_real, a_imag, b_real, b_imag):
    return (a_real * b_real - a_imag * b_imag, a_real * b_imag + a_imag * b_real)


def times_conj(a_real, a_imag, b_real, b_imag):
    return (a_real * b_real + a_imag * b_imag, a_real * b_imag - a_imag * b_real)


def halves_of(value):
    high = value.astype(bf16)
    return high, (value - high.astype(f32)).astype(bf16)


def lane_ids(rows):
    return lax.broadcasted_iota(jnp.int32, (rows, LANES), 1)


def packed(planes, half):
    lane = lane_ids(planes[0].shape[0])
    rest = LANES - half
    return [
        jnp.where(lane < half, planes[j], pltpu.roll(planes[3], (half - rest * j) % LANES, 1))
        for j in range(3)
    ]


def last_of(parts, half):
    lane = lane_ids(parts[0].shape[0])
    rest = LANES - half
    out = pltpu.roll(parts[0], rest, 1)
    for j in range(1, 3):
        out = jnp.where(lane < rest * j, out, pltpu.roll(parts[j], (rest * j + rest) % LANES, 1))
    return out


def cosine_and_sine(x):
    turns = jnp.floor(x * (2.0 / math.pi) + 0.5)
    rest = ((x - turns * 1.5703125) - turns * 4.837512969970703125e-4) - turns * 7.54978995489188e-8
    square = rest * rest
    sine = ((-1.9515295891e-4 * square + 8.3321608736e-3) * square - 1.6666654611e-1) * square
    sine = sine * rest + rest
    cosine = (2.443315711809948e-5 * square - 1.388731625493765e-3) * square + 4.166664568298827e-2
    cosine = cosine * square * square - 0.5 * square + 1.0
    quarter = turns.astype(jnp.int32) & 3
    odd = (quarter & 1) == 1
    return (
        jnp.where(odd, sine, cosine) * jnp.where((quarter == 1) | (quarter == 2), -1.0, 1.0),
        jnp.where(odd, cosine, sine) * jnp.where(quarter >= 2, -1.0, 1.0),
    )


def pack_kernel(object_ref, out_ref):
    tile = object_ref.shape[2]
    pad = jnp.zeros((tile, LANES - tile), f32)
    planes = [
        jnp.concatenate([object_ref[plane // 2, plane % 2], pad], 1) for plane in range(4)
    ]
    for j, block in enumerate(packed(planes, tile)):
        out_ref[:, j * LANES : (j + 1) * LANES] = block


def prepare_kernel(
    offsets_ref,
    counts_ref,
    probe_ref,
    phase_ref,
    measured_ref,
    wave_out,
    trans_out,
    measured_out,
    places_out,
):
    lanes = lax.broadcasted_iota(jnp.int32, places_out.shape, 1)
    slots = measured_out.shape[0]
    places = jnp.where(lanes == 2 * slots, counts_ref[...], 0)
    for slot in range(slots):
        for axis in range(2):
            value = offsets_ref[0, 0, slot : slot + 1, axis : axis + 1]
            places = jnp.where(lanes == 2 * slot + axis, value, places)
    places_out[...] = places
    width = probe_ref.shape[1]
    half = width // 2
    lane = lane_ids(width)
    for j in range(2):
        head = probe_ref[j, :, :LANES]
        tail = jnp.concatenate(
            [probe_ref[j, :, LANES:], jnp.zeros((width, 2 * LANES - width), f32)], 1
        )
        rest = LANES - half
        wave_out[j, :, :LANES] = jnp.where(lane < half, head, 0.0)
        wave_out[j, :, LANES:] = jnp.where(
            lane < rest, pltpu.roll(head, rest, 1), pltpu.roll(tail, rest, 1)
        )
    columns, rows = sorters(width)
    planes = [phase_ref[...]] + [measured_ref[0, 0, j] for j in range(measured_out.shape[0])]
    for j, left in enumerate(planes):
        total = jnp.zeros((width, 2 * LANES), f32)
        for part in range(3):
            piece = left.astype(bf16)
            left = left - piece.astype(f32)
            moved = jnp.dot(piece, columns, preferred_element_type=f32)
            total = total + jnp.dot(rows, moved.astype(bf16), preferred_element_type=f32)
        if j > 0:
            measured_out[j - 1] = total
            continue
        used = lax.rem(lax.broadcasted_iota(jnp.int32, total.shape, 1), LANES) < half
        for side, value in enumerate(cosine_and_sine(total)):
            trans_out[side] = jnp.where(used, value, 0.0)


def row_places(cores):
    core = lax.axis_index("core") if cores == 2 else 1
    return 1, 2 - 2 * core, 2 * core


def position_kernel(
    paired,
    cores,
    places_ref,
    *refs,
):
    sides = 2 if paired else 3
    tiles = refs[: 3 * sides]
    (
        wave_ref,
        trans_ref,
        measured_ref,
        right_ref,
        left_ref,
        window,
    ) = refs[3 * sides : 3 * sides + 6]
    terms_out = refs[3 * sides + 6 : 3 * sides + 6 + cores]
    (
        obj,
        carried,
        terms,
        places,
        arrived,
    ) = refs[3 * sides + 6 + cores : 3 * sides + 11 + cores]
    copy = pltpu.make_async_copy(places_ref, places, arrived)
    copy.start()
    slots = measured_ref.shape[0]
    work = refs[3 * sides + 11 + cores :]
    data, out_right, mid, out_left = (work[k * slots : (k + 1) * slots] for k in range(4))
    width = wave_ref.shape[1]
    half = width // 2
    tile = obj.shape[2] // 3
    total = slots * width
    step = 16
    part_rows = half // 2
    lag = 2
    column_of = lax.axis_index("col")
    row_starts = [pl.multiple_of(place * tile, 8) for place in row_places(cores)]

    for row in range(3):
        rows = pl.ds(row_starts[row], tile)
        for side in range(sides):
            if paired:
                place = 1 if side == 0 else 2 - 2 * column_of
            else:
                place = (1, 0, 2)[side]
            ref = tiles[row * sides + side]
            parts = [ref[:, j * LANES : (j + 1) * LANES] for j in range(3)]
            parts.append(last_of(parts, tile))
            for plane in range(4):
                obj[plane, place, rows, :] = parts[plane]
        if paired:
            for plane in range(4):
                obj[plane, 2 * column_of, rows, :] = jnp.zeros((tile, LANES), f32)

    copy.wait()
    shift = tile - half
    corners = [
        (places[0, 2 * slot] + shift, places[0, 2 * slot + 1] + shift)
        for slot in range(slots)
    ]
    chunk = half
    lane = lane_ids(chunk)
    for slot in range(slots):
        row, column = corners[slot]
        back = lax.rem(LANES - column, LANES)
        inside = lane < tile - column
        for plane in range(4):
            for start in range(0, width, chunk):
                source = pl.ds(row + start, chunk)
                target = pl.ds(slot * width + start, chunk)
                for j in range(2):
                    window[plane, j, target, :] = jnp.where(
                        inside,
                        pltpu.roll(obj[plane, j, source, :], back, 1),
                        pltpu.roll(obj[plane, j + 1, source, :], tile - column, 1),
                    )
    span = 2 * LANES

    def put(slot, block, row, a, b):
        high, low = halves_of(jnp.concatenate([a, b], 1))
        data[slot][block, pl.ds(row, step), :] = high
        data[slot][block, pl.ds(width + row, step), :] = low

    def multiply_right(slot, odd):
        for block in range(2):
            rows = slice(block * width, (block + 1) * width)
            left = data[slot][block]
            out = jnp.dot(left, right_ref[odd * block, 0], preferred_element_type=f32)
            low = jnp.dot(left[:width], right_ref[odd * block, 1], preferred_element_type=f32)
            out_right[slot][rows, :] = out[:width] + (out[width:] + low)
            yield

    def put_mid(slot, block, start, first, second):
        for part in range(2):
            high, low = halves_of(jnp.concatenate([first[part], second[part]], 1))
            mid[slot][block, pl.ds(part * half + start, step), :] = high
            mid[slot][block, pl.ds((2 + part) * half + start, step), :] = low

    def multiply_left(slot, odd):
        for block in range(2):
            both = left_ref[odd * block]
            high = mid[slot][block, :width]
            low = mid[slot][block, width:]
            out = jnp.dot(both, high, preferred_element_type=f32)
            rest = jnp.dot(both[:width], low, preferred_element_type=f32)
            out_left[slot][block] = out[:width] + (out[width:] + rest)
            yield

    def get_right(slot, block, row):
        rows = pl.ds(block * width + row, step)
        return out_right[slot][rows, :LANES], out_right[slot][rows, LANES:]

    def get_left(slot, block, j, start):
        columns = slice(j * LANES, (j + 1) * LANES)
        return (
            out_left[slot][block, pl.ds(start, step), columns],
            out_left[slot][block, pl.ds(half + start, step), columns],
        )

    def forward(slot, source):
        for row in range(0, half, step):
            for side, ((a0, b0), (a1, b1)) in enumerate(source(slot, row)):
                place = side * half + row
                put(slot, 0, place, a0 + a1, b0 + b1)
                put(slot, 1, place, a0 - a1, b0 - b1)
            if row % part_rows == part_rows - step:
                yield
        yield from multiply_right(slot, 1)
        for row in range(0, half, step):
            even, odd = [], []
            for j in range(2):
                a0, b0 = get_right(slot, j, row)
                a1, b1 = get_right(slot, j, half + row)
                even.append((a0 + a1, b0 + b1))
                odd.append((a0 - a1, b0 - b1))
            put_mid(slot, 0, row, *even)
            put_mid(slot, 1, row, *odd)
            if row % part_rows == part_rows - step:
                yield
        yield from multiply_left(slot, 1)

    def inverse(slot, source):
        for row in range(0, width, step):
            for j, (a, b) in enumerate(source(slot, row)):
                put(slot, j, row, a, b)
            if row % (2 * part_rows) == 2 * part_rows - step:
                yield
        yield from multiply_right(slot, 2)
        for row in range(0, width, step):
            a0, b0 = get_right(slot, 0, row)
            a1, b1 = get_right(slot, 1, row)
            put_mid(slot, row // half, row % half, (a0 + a1, b0 + b1), (a0 - a1, b0 - b1))
            if row % (2 * part_rows) == 2 * part_rows - step:
                yield
        yield from multiply_left(slot, 2)

    def frequency(slot, row, j):
        return get_left(slot, row // half, j, row % half)

    def natural(slot, row, j):
        b0, a0 = get_left(slot, 0, j, row)
        b1, a1 = get_left(slot, 1, j, row)
        return (a0 + a1, b0 + b1), (a0 - a1, b0 - b1)

    def at(ref, first, row, j):
        rows = pl.ds(row, step)
        columns = slice(j * LANES, (j + 1) * LANES)
        return ref[first, rows, columns], ref[first + 1, rows, columns]

    def seen(ref, first, slot, row, j):
        rows = pl.ds(slot * width + row, step)
        return ref[first, j, rows, :], ref[first + 1, j, rows, :]

    def keep(ref, first, slot, row, j, real, imag):
        rows = pl.ds(slot * width + row, step)
        ref[first, j, rows, :] = real
        ref[first + 1, j, rows, :] = imag

    def entry(slot, row):
        return [
            [times(*at(wave_ref, 0, place, j), *seen(window, 0, slot, place, j)) for j in range(2)]
            for place in (row, half + row)
        ]

    def from_natural(handle):
        def source(slot, row):
            pairs = [natural(slot, row, j) for j in range(2)]
            return [
                [handle(slot, side * half + row, j, *pairs[j][side]) for j in range(2)]
                for side in range(2)
            ]

        return source

    def from_frequency(handle):
        def source(slot, row):
            out = []
            for j in range(2):
                real, imag = handle(slot, row, j, *frequency(slot, row, j))
                out.append((imag, real))
            return out

        return source

    @from_frequency
    def propagate(slot, row, j, real, imag):
        return times(*at(trans_ref, 0, row, j), real, imag)

    @from_natural
    def leave(slot, row, j, real, imag):
        keep(carried, 0, slot, row, j, real, imag)
        return times(real, imag, *seen(window, 2, slot, row, j))

    @from_frequency
    def residual(slot, row, j, real, imag):
        columns = slice(j * LANES, (j + 1) * LANES)
        factor = real * real + imag * imag - measured_ref[slot, pl.ds(row, step), columns]
        return factor * real, factor * imag

    @from_natural
    def before(slot, row, j, real, imag):
        inner = times_conj(*seen(window, 2, slot, row, j), real, imag)
        second = times_conj(*seen(carried, 0, slot, row, j), real, imag)
        keep(window, 2, slot, row, j, *second)
        return inner

    @from_frequency
    def propagate_back(slot, row, j, real, imag):
        return times_conj(*at(trans_ref, 0, row, j), real, imag)

    def stages(slot):
        yield from forward(slot, entry)
        yield from inverse(slot, propagate)
        yield from forward(slot, leave)
        yield from inverse(slot, residual)
        yield from forward(slot, before)
        yield from inverse(slot, propagate_back)

    running = [stages(slot) for slot in range(slots)]
    turn = 0
    while any(x is not None for x in running):
        for slot in range(slots):
            if running[slot] is not None and turn >= slot * lag:
                if next(running[slot], "end") == "end":
                    running[slot] = None
        turn += 1

    live = [(slot < places[0, 2 * slots]).astype(f32) for slot in range(slots)]
    core = lax.axis_index("core")
    share = width // cores
    for row in range(0, half, step):
        sums = [[None] * 4 for side in range(2)]
        for j in range(2):
            for slot in range(slots):
                for side, (real, imag) in enumerate(natural(slot, row, j)):
                    place = side * half + row
                    term = times_conj(*seen(window, 0, slot, place, j), real, imag)
                    keep(
                        window,
                        0,
                        slot,
                        place,
                        j,
                        *times_conj(*at(wave_ref, 0, place, j), real, imag),
                    )
                    for part in range(2):
                        value = live[slot] * term[part]
                        old = sums[side][2 * part + j]
                        sums[side][2 * part + j] = value if old is None else old + value
        for side in range(2):
            place = side * half + row
            which = lax.rem(place // share + core, cores)
            for j, block in enumerate(packed(sums[side], half)):
                terms[which, j, pl.ds(place % share, step), :] = block
    for k, out in enumerate(terms_out):
        out[...] = terms[k]


def place_kernel(paired, cores, places_ref, window, own_out, near_out, far_out, acc, places, arrived):
    copy = pltpu.make_async_copy(places_ref, places, arrived)
    copy.start()
    acc[...] = jnp.zeros(acc.shape, f32)
    sides = acc.shape[1]
    tile = acc.shape[2] // 3
    slots = window.shape[2] // (2 * tile)
    width = window.shape[2] // slots
    half = width // 2
    column_of = lax.axis_index("col")
    row_starts = [pl.multiple_of(place * tile, 8) for place in row_places(cores)]
    copy.wait()
    shift = tile - half
    corners = [
        (places[0, 2 * slot] + shift, places[0, 2 * slot + 1] + shift) for slot in range(slots)
    ]
    live = [(slot < places[0, 2 * slots]).astype(f32) for slot in range(slots)]
    chunk = half
    lane = lane_ids(chunk)
    for slot in range(slots):
        row, column = corners[slot]
        inside = lane >= column
        over = column + LANES - tile
        for plane in range(4):
            for start in range(0, width, chunk):
                rows = pl.ds(slot * width + start, chunk)
                target = pl.ds(row + start, chunk)
                first, second = (live[slot] * window[plane, j, rows, :] for j in range(2))
                pieces = [jnp.where(inside, pltpu.roll(second, column, 1), pltpu.roll(first, over, 1))]
                if paired:
                    value = live[slot] * window[plane, 1 - column_of, rows, :]
                    value = pltpu.roll(value, jnp.where(column_of == 0, over, column), 1)
                    pieces.append(jnp.where(inside.astype(jnp.int32) == column_of, value, 0.0))
                else:
                    pieces.append(jnp.where(inside, pltpu.roll(first, column, 1), 0.0))
                    pieces.append(jnp.where(inside, 0.0, pltpu.roll(second, over, 1)))
                for side, piece in enumerate(pieces):
                    acc[plane, side, target, :] = acc[plane, side, target, :] + piece
    for start, out in zip(row_starts, (own_out, near_out, far_out)):
        rows = pl.ds(start, tile)
        for side in range(sides):
            planes = [acc[plane, side, rows, :] for plane in range(4)]
            for j, block in enumerate(packed(planes, tile)):
                k = 3 * side + j
                out[:, k * LANES : (k + 1) * LANES] = block


def fold_kernel(own_ref, near_ref, far_ref, *outs):
    columns = outs[0].shape[1]
    for side, out in enumerate(outs):
        part = slice(side * columns, (side + 1) * columns)
        out[...] = own_ref[:, part] + near_ref[:, part] + far_ref[:, part]


def update_kernel(rate, cores, object_ref, probe_ref, *refs):
    object_out, probe_out = refs[-2:]
    sums = refs[:cores]
    tile = object_ref.shape[2]
    total = refs[cores][...]
    for ref in refs[cores + 1 : -2]:
        total = total + ref[...]
    parts = [total[:, j * LANES : (j + 1) * LANES] for j in range(3)]
    parts.append(last_of(parts, tile))
    for plane in range(4):
        object_out[plane // 2, plane % 2] = (
            object_ref[plane // 2, plane % 2] - object_rate * parts[plane][:, :tile]
        )
    width = probe_ref.shape[1]
    half = width // 2
    share = width // cores
    lane = lane_ids(share)
    for k, ref in enumerate(sums):
        start = share * lax.rem(lax.axis_index("core") + k, cores)
        rows = pl.ds(pl.multiple_of(start, 8), share)
        parts = [ref[j] for j in range(3)]
        parts.append(last_of(parts, half))
        for j in range(2):
            head, tail = parts[2 * j], pltpu.roll(parts[2 * j + 1], half, 1)
            probe_out[j, rows, :LANES] = probe_ref[j, rows, :LANES] - rate * jnp.where(
                lane < half, head, tail
            )
            probe_out[j, rows, LANES:] = (
                probe_ref[j, rows, LANES:] - rate * tail[:, : width - LANES]
            )


def passed_along(x, axis, by):
    peers = lax.axis_size(axis)
    pairs = [(i, i + by) for i in range(peers) if 0 <= i + by < peers]
    return lax.ppermute(x, axis, pairs)


def from_near(x, cores):
    if cores == 2:
        return lax.ppermute(x, "core", [(0, 1), (1, 0)])
    return passed_along(x, ROWS, 1)


def from_far(x, cores):
    if cores == 2:
        ends = range(1, lax.axis_size(ROWS) - 1, 2)
        pairs = [(i, i + 1) for i in ends] + [(i + 1, i) for i in ends]
        return lax.ppermute(x, ROWS, pairs)
    return passed_along(x, ROWS, -1)


def from_far_beside(x):
    ends = range(1, lax.axis_size(ROWS) - 1, 2)
    pairs = []
    for i in ends:
        for j in range(2):
            pairs += [(2 * i + j, 2 * i + 3 - j), (2 * i + 2 + j, 2 * i + 1 - j)]
    return lax.ppermute(x, ROWS + ("col",), pairs)


def all_sum(x, group):
    count = math.prod(lax.axis_size(axis) for axis in group)
    shape = x.shape
    x = x.reshape(-1, 2, LANES)
    pairs = x.shape[0]
    piece = -(-pairs // count)
    if piece * count > pairs:
        x = jnp.pad(x, ((0, piece * count - pairs), (0, 0), (0, 0)))
    x = x.reshape(count, piece, 2, LANES)
    x = lax.all_to_all(x, group, 0, 0, tiled=True)
    x = jnp.broadcast_to(jnp.sum(x, 0)[None], x.shape)
    x = lax.all_to_all(x, group, 0, 0, tiled=True)
    return x.reshape(count * piece, 2, LANES)[:pairs].reshape(shape)


def shards(object_slices, probe, propagator_phase, measured, offsets, counts):
    tile = object_slices.shape[-1]
    width = probe.shape[-1]
    slots = measured.shape[2]
    cores = lax.axis_size("core")
    cols_count = lax.axis_size("col")
    devices = lax.axis_size(ROWS) * cols_count
    paired = cols_count == 2
    large = pltpu.CompilerParams(vmem_limit_bytes=18 * 1024 * 1024)
    small = pltpu.CompilerParams(vmem_limit_bytes=6 * 1024 * 1024)

    def shape(*dims, kind=f32):
        return jax.ShapeDtypeStruct(dims, kind)

    cells = pl.pallas_call(
        pack_kernel,
        out_shape=shape(tile, 3 * LANES),
        in_specs=[VMEM],
        out_specs=VMEM,
        cost_estimate=pl.CostEstimate(flops=10**10, bytes_accessed=10**7, transcendentals=0),
        compiler_params=small,
    )(object_slices)
    if paired:
        beside = [lax.ppermute(cells, "col", [(0, 1), (1, 0)])]
    else:
        beside = [passed_along(cells, "col", 1), passed_along(cells, "col", -1)]
    own = [cells] + beside
    near = [from_near(x, cores) for x in own]
    if paired and cores == 2:
        far = [from_far(cells, cores), from_far_beside(cells)]
    else:
        far = [from_far(x, cores) for x in own]

    wave, trans, intensities, places = pl.pallas_call(
        prepare_kernel,
        out_shape=[
            shape(2, width, 2 * LANES),
            shape(2, width, 2 * LANES),
            shape(slots, width, 2 * LANES),
            shape(8, LANES, kind=jnp.int32),
        ],
        in_specs=[VMEM] * 5,
        out_specs=[VMEM] * 4,
        cost_estimate=pl.CostEstimate(flops=10**10, bytes_accessed=10**7, transcendentals=0),
        compiler_params=small,
    )(offsets, counts, probe, propagator_phase, measured)

    total = slots * width
    sides = len(own)
    strip = shape(tile, sides * 3 * LANES)
    scratch = [
        pltpu.VMEM((4, 3, 3 * tile, LANES), f32),
        pltpu.VMEM((2, 2, total, LANES), f32),
        pltpu.VMEM((cores, 3, width // cores, LANES), f32),
        pltpu.SMEM((8, LANES), jnp.int32),
        pltpu.SemaphoreType.DMA,
    ]
    scratch += [pltpu.VMEM((2, 2 * width, 2 * LANES), bf16)] * slots
    scratch += [pltpu.VMEM((2 * width, 2 * LANES), f32)] * slots
    scratch += [pltpu.VMEM((2, 2 * width, 2 * LANES), bf16)] * slots
    scratch += [pltpu.VMEM((2, width, 2 * LANES), f32)] * slots
    term = shape(3, width // cores, LANES)
    gradients, *terms = pl.pallas_call(
        functools.partial(position_kernel, paired, cores),
        out_shape=[shape(4, 2, total, LANES)] + [term] * cores,
        in_specs=[ANY] + [VMEM] * (3 * sides + 5),
        out_specs=[VMEM] * (1 + cores),
        scratch_shapes=scratch,
        compiler_params=large,
    )(places, *own, *near, *far, wave, trans, intensities, *matrices(width))
    own_strip, near_strip, far_strip = pl.pallas_call(
        functools.partial(place_kernel, paired, cores),
        out_shape=[strip] * 3,
        in_specs=[ANY, VMEM],
        out_specs=[VMEM] * 3,
        scratch_shapes=[
            pltpu.VMEM((4, sides, 3 * tile, LANES), f32),
            pltpu.SMEM((8, LANES), jnp.int32),
            pltpu.SemaphoreType.DMA,
        ],
        compiler_params=small,
    )(places, gradients)

    if cores == 2:
        mine = all_sum(terms[0] + from_near(terms[1], cores), ("pair", "col"))
        sums = [mine, from_near(mine, cores)]
    else:
        sums = [all_sum(terms[0], ("pair", "col"))]
    if cores == 1:
        near_strip, far_strip = passed_along(near_strip, ROWS, -1), passed_along(far_strip, ROWS, 1)
    else:
        near_strip, far_strip = from_near(near_strip, cores), from_far(far_strip, cores)
    share = shape(tile, 3 * LANES)
    parts = pl.pallas_call(
        fold_kernel,
        out_shape=[share] * sides,
        in_specs=[VMEM] * 3,
        out_specs=[VMEM] * sides,
        compiler_params=small,
    )(own_strip, near_strip, far_strip)
    if paired:
        received = [lax.ppermute(parts[1], "col", [(0, 1), (1, 0)])]
    else:
        received = [passed_along(parts[1], "col", -1), passed_along(parts[2], "col", 1)]
    return pl.pallas_call(
        functools.partial(update_kernel, probe_rate / (slots * devices), cores),
        out_shape=[shape(*object_slices.shape), shape(*probe.shape)],
        in_specs=[VMEM] * (3 + cores + len(received)),
        out_specs=[VMEM] * 2,
        compiler_params=small,
    )(object_slices, probe, *sums, parts[0], *received)


def solution(mesh):
    rows, cols = mesh.devices.shape
    cores = 2 if rows % 2 == 0 else 1
    finer = Mesh(mesh.devices.reshape(rows // cores, cores, cols), ROWS + ("col",))
    return jax.shard_map(
        shards,
        mesh=finer,
        in_specs=(
            P(None, None, ROWS, "col"),
            P(),
            P(),
            P(ROWS, "col", None, None, None),
            P(ROWS, "col", None, None),
            P(ROWS, "col"),
        ),
        out_specs=(P(None, None, ROWS, "col"), P()),
        check_vma=False,
    )
```

```python
import functools
import math

import jax
import jax.numpy as jnp
import numpy as np
from jax import lax
from jax.experimental import pallas as pl
from jax.experimental.pallas import tpu as pltpu
from jax.sharding import Mesh
from jax.sharding import PartitionSpec as P

object_rate = 0.02
probe_rate = 0.3

LANES = 128
f32 = jnp.float32
bf16 = jnp.bfloat16
VMEM = pl.BlockSpec(memory_space=pltpu.VMEM)
ANY = pl.BlockSpec(memory_space=pl.ANY)
ROWS = ("pair", "core")


def matrices(width):
    half = width // 2
    k = np.arange(half)
    turns = [2 * k[:, None] * k[None, :], k[:, None] * (2 * k[None, :] + 1)]
    turns.append(turns[1].T)
    rights, lefts = [], []

    def halves(matrix):
        high = matrix.astype(np.float32).astype(bf16)
        low = (matrix - high.astype(np.float64)).astype(np.float32).astype(bf16)
        return high, low

    for turn in turns:
        angle = (turn % width) * (2.0 * math.pi / width)
        cosine = np.cos(angle) / math.sqrt(width)
        sine = np.sin(angle) / math.sqrt(width)
        right = np.zeros((2, LANES, 2, LANES))
        right[0, :half, 0, :half] = cosine
        right[0, :half, 1, :half] = -sine
        right[1, :half, 0, :half] = sine
        right[1, :half, 1, :half] = cosine
        high, low = halves(right.reshape(2 * LANES, 2 * LANES))
        rights.append(np.stack([high, low]))
        high, low = halves(np.block([[cosine.T, sine.T], [-sine.T, cosine.T]]))
        lefts.append(np.concatenate([high, low], 0))
    return np.stack(rights), np.stack(lefts)


def sorters(width):
    half = width // 2

    def ids(shape, axis):
        return lax.broadcasted_iota(jnp.int32, shape, axis)

    shape = (width, 2 * LANES)
    source = ids(shape, 0)
    columns = ids(shape, 1) == (source & 1) * LANES + (source >> 1)
    shape = (width, width)
    target = ids(shape, 0)
    rows = ids(shape, 1) == jnp.where(target < half, 2 * target, 2 * (target - half) + 1)
    return [jnp.where(x, 1.0, 0.0).astype(bf16) for x in (columns, rows)]


def times(a_real, a_imag, b_real, b_imag):
    return (a_real * b_real - a_imag * b_imag, a_real * b_imag + a_imag * b_real)


def times_conj(a_real, a_imag, b_real, b_imag):
    return (a_real * b_real + a_imag * b_imag, a_real * b_imag - a_imag * b_real)


def halves_of(value):
    high = value.astype(bf16)
    return high, (value - high.astype(f32)).astype(bf16)


def lane_ids(rows):
    return lax.broadcasted_iota(jnp.int32, (rows, LANES), 1)


def packed(planes, half):
    lane = lane_ids(planes[0].shape[0])
    rest = LANES - half
    return [
        jnp.where(lane < half, planes[j], pltpu.roll(planes[3], (half - rest * j) % LANES, 1))
        for j in range(3)
    ]


def last_of(parts, half):
    lane = lane_ids(parts[0].shape[0])
    rest = LANES - half
    out = pltpu.roll(parts[0], rest, 1)
    for j in range(1, 3):
        out = jnp.where(lane < rest * j, out, pltpu.roll(parts[j], (rest * j + rest) % LANES, 1))
    return out


def cosine_and_sine(x):
    turns = jnp.floor(x * (2.0 / math.pi) + 0.5)
    rest = ((x - turns * 1.5703125) - turns * 4.837512969970703125e-4) - turns * 7.54978995489188e-8
    square = rest * rest
    sine = ((-1.9515295891e-4 * square + 8.3321608736e-3) * square - 1.6666654611e-1) * square
    sine = sine * rest + rest
    cosine = (2.443315711809948e-5 * square - 1.388731625493765e-3) * square + 4.166664568298827e-2
    cosine = cosine * square * square - 0.5 * square + 1.0
    quarter = turns.astype(jnp.int32) & 3
    odd = (quarter & 1) == 1
    return (
        jnp.where(odd, sine, cosine) * jnp.where((quarter == 1) | (quarter == 2), -1.0, 1.0),
        jnp.where(odd, cosine, sine) * jnp.where(quarter >= 2, -1.0, 1.0),
    )


def pack_kernel(object_ref, out_ref):
    tile = object_ref.shape[2]
    pad = jnp.zeros((tile, LANES - tile), f32)
    planes = [
        jnp.concatenate([object_ref[plane // 2, plane % 2], pad], 1) for plane in range(4)
    ]
    for j, block in enumerate(packed(planes, tile)):
        out_ref[:, j * LANES : (j + 1) * LANES] = block


def prepare_kernel(
    offsets_ref,
    counts_ref,
    probe_ref,
    phase_ref,
    measured_ref,
    wave_out,
    trans_out,
    measured_out,
    places_out,
):
    lanes = lax.broadcasted_iota(jnp.int32, places_out.shape, 1)
    slots = measured_out.shape[0]
    places = jnp.where(lanes == 2 * slots, counts_ref[...], 0)
    for slot in range(slots):
        for axis in range(2):
            value = offsets_ref[0, 0, slot : slot + 1, axis : axis + 1]
            places = jnp.where(lanes == 2 * slot + axis, value, places)
    places_out[...] = places
    width = probe_ref.shape[1]
    half = width // 2
    lane = lane_ids(width)
    for j in range(2):
        head = probe_ref[j, :, :LANES]
        tail = jnp.concatenate(
            [probe_ref[j, :, LANES:], jnp.zeros((width, 2 * LANES - width), f32)], 1
        )
        rest = LANES - half
        wave_out[j, :, :LANES] = jnp.where(lane < half, head, 0.0)
        wave_out[j, :, LANES:] = jnp.where(
            lane < rest, pltpu.roll(head, rest, 1), pltpu.roll(tail, rest, 1)
        )
    columns, rows = sorters(width)
    planes = [phase_ref[...]] + [measured_ref[0, 0, j] for j in range(measured_out.shape[0])]
    for j, left in enumerate(planes):
        total = jnp.zeros((width, 2 * LANES), f32)
        for part in range(3):
            piece = left.astype(bf16)
            left = left - piece.astype(f32)
            moved = jnp.dot(piece, columns, preferred_element_type=f32)
            total = total + jnp.dot(rows, moved.astype(bf16), preferred_element_type=f32)
        if j > 0:
            measured_out[j - 1] = total
            continue
        used = lax.rem(lax.broadcasted_iota(jnp.int32, total.shape, 1), LANES) < half
        for side, value in enumerate(cosine_and_sine(total)):
            trans_out[side] = jnp.where(used, value, 0.0)


def row_places(cores):
    core = lax.axis_index("core") if cores == 2 else 1
    return 1, 2 - 2 * core, 2 * core


def position_kernel(
    paired,
    cores,
    places_ref,
    *refs,
):
    sides = 2 if paired else 3
    tiles = refs[: 3 * sides]
    (
        wave_ref,
        trans_ref,
        measured_ref,
        right_ref,
        left_ref,
        window,
    ) = refs[3 * sides : 3 * sides + 6]
    terms_out = refs[3 * sides + 6 : 3 * sides + 6 + cores]
    (
        obj,
        carried,
        terms,
        places,
        arrived,
    ) = refs[3 * sides + 6 + cores : 3 * sides + 11 + cores]
    copy = pltpu.make_async_copy(places_ref, places, arrived)
    copy.start()
    slots = measured_ref.shape[0]
    work = refs[3 * sides + 11 + cores :]
    data, out_right, mid, out_left = (work[k * slots : (k + 1) * slots] for k in range(4))
    width = wave_ref.shape[1]
    half = width // 2
    tile = obj.shape[2] // 3
    total = slots * width
    step = 16
    part_rows = half // 2
    lag = 2
    column_of = lax.axis_index("col")
    row_starts = [pl.multiple_of(place * tile, 8) for place in row_places(cores)]

    for row in range(3):
        rows = pl.ds(row_starts[row], tile)
        for side in range(sides):
            if paired:
                place = 1 if side == 0 else 2 - 2 * column_of
            else:
                place = (1, 0, 2)[side]
            ref = tiles[row * sides + side]
            if len(ref.shape) == 2:
                parts = [ref[:, j * LANES : (j + 1) * LANES] for j in range(3)]
                parts.append(last_of(parts, tile))
            else:
                pad = jnp.zeros((tile, LANES - tile), f32)
                parts = [
                    jnp.concatenate([ref[plane // 2, plane % 2], pad], 1) for plane in range(4)
                ]
            for plane in range(4):
                obj[plane, place, rows, :] = parts[plane]
        if paired:
            for plane in range(4):
                obj[plane, 2 * column_of, rows, :] = jnp.zeros((tile, LANES), f32)

    copy.wait()
    shift = tile - half
    corners = [
        (places[0, 2 * slot] + shift, places[0, 2 * slot + 1] + shift)
        for slot in range(slots)
    ]
    chunk = half
    lane = lane_ids(chunk)
    for slot in range(slots):
        row, column = corners[slot]
        back = lax.rem(LANES - column, LANES)
        inside = lane < tile - column
        for plane in range(4):
            for start in range(0, width, chunk):
                source = pl.ds(row + start, chunk)
                target = pl.ds(slot * width + start, chunk)
                for j in range(2):
                    window[plane, j, target, :] = jnp.where(
                        inside,
                        pltpu.roll(obj[plane, j, source, :], back, 1),
                        pltpu.roll(obj[plane, j + 1, source, :], tile - column, 1),
                    )
    span = 2 * LANES

    def put(slot, block, row, a, b):
        high, low = halves_of(jnp.concatenate([a, b], 1))
        data[slot][block, pl.ds(row, step), :] = high
        data[slot][block, pl.ds(width + row, step), :] = low

    def multiply_right(slot, odd):
        for block in range(2):
            rows = slice(block * width, (block + 1) * width)
            left = data[slot][block]
            out = jnp.dot(left, right_ref[odd * block, 0], preferred_element_type=f32)
            low = jnp.dot(left[:width], right_ref[odd * block, 1], preferred_element_type=f32)
            out_right[slot][rows, :] = out[:width] + (out[width:] + low)
            yield

    def put_mid(slot, block, start, first, second):
        for part in range(2):
            high, low = halves_of(jnp.concatenate([first[part], second[part]], 1))
            mid[slot][block, pl.ds(part * half + start, step), :] = high
            mid[slot][block, pl.ds((2 + part) * half + start, step), :] = low

    def multiply_left(slot, odd):
        for block in range(2):
            both = left_ref[odd * block]
            high = mid[slot][block, :width]
            low = mid[slot][block, width:]
            out = jnp.dot(both, high, preferred_element_type=f32)
            rest = jnp.dot(both[:width], low, preferred_element_type=f32)
            out_left[slot][block] = out[:width] + (out[width:] + rest)
            yield

    def get_right(slot, block, row):
        rows = pl.ds(block * width + row, step)
        return out_right[slot][rows, :LANES], out_right[slot][rows, LANES:]

    def get_left(slot, block, j, start):
        columns = slice(j * LANES, (j + 1) * LANES)
        return (
            out_left[slot][block, pl.ds(start, step), columns],
            out_left[slot][block, pl.ds(half + start, step), columns],
        )

    def forward(slot, source):
        for row in range(0, half, step):
            for side, ((a0, b0), (a1, b1)) in enumerate(source(slot, row)):
                place = side * half + row
                put(slot, 0, place, a0 + a1, b0 + b1)
                put(slot, 1, place, a0 - a1, b0 - b1)
            if row % part_rows == part_rows - step:
                yield
        yield from multiply_right(slot, 1)
        for row in range(0, half, step):
            even, odd = [], []
            for j in range(2):
                a0, b0 = get_right(slot, j, row)
                a1, b1 = get_right(slot, j, half + row)
                even.append((a0 + a1, b0 + b1))
                odd.append((a0 - a1, b0 - b1))
            put_mid(slot, 0, row, *even)
            put_mid(slot, 1, row, *odd)
            if row % part_rows == part_rows - step:
                yield
        yield from multiply_left(slot, 1)

    def inverse(slot, source):
        for row in range(0, width, step):
            for j, (a, b) in enumerate(source(slot, row)):
                put(slot, j, row, a, b)
            if row % (2 * part_rows) == 2 * part_rows - step:
                yield
        yield from multiply_right(slot, 2)
        for row in range(0, width, step):
            a0, b0 = get_right(slot, 0, row)
            a1, b1 = get_right(slot, 1, row)
            put_mid(slot, row // half, row % half, (a0 + a1, b0 + b1), (a0 - a1, b0 - b1))
            if row % (2 * part_rows) == 2 * part_rows - step:
                yield
        yield from multiply_left(slot, 2)

    def frequency(slot, row, j):
        return get_left(slot, row // half, j, row % half)

    def natural(slot, row, j):
        b0, a0 = get_left(slot, 0, j, row)
        b1, a1 = get_left(slot, 1, j, row)
        return (a0 + a1, b0 + b1), (a0 - a1, b0 - b1)

    def at(ref, first, row, j):
        rows = pl.ds(row, step)
        columns = slice(j * LANES, (j + 1) * LANES)
        return ref[first, rows, columns], ref[first + 1, rows, columns]

    def seen(ref, first, slot, row, j):
        rows = pl.ds(slot * width + row, step)
        return ref[first, j, rows, :], ref[first + 1, j, rows, :]

    def keep(ref, first, slot, row, j, real, imag):
        rows = pl.ds(slot * width + row, step)
        ref[first, j, rows, :] = real
        ref[first + 1, j, rows, :] = imag

    def entry(slot, row):
        return [
            [times(*at(wave_ref, 0, place, j), *seen(window, 0, slot, place, j)) for j in range(2)]
            for place in (row, half + row)
        ]

    def from_natural(handle):
        def source(slot, row):
            pairs = [natural(slot, row, j) for j in range(2)]
            return [
                [handle(slot, side * half + row, j, *pairs[j][side]) for j in range(2)]
                for side in range(2)
            ]

        return source

    def from_frequency(handle):
        def source(slot, row):
            out = []
            for j in range(2):
                real, imag = handle(slot, row, j, *frequency(slot, row, j))
                out.append((imag, real))
            return out

        return source

    @from_frequency
    def propagate(slot, row, j, real, imag):
        return times(*at(trans_ref, 0, row, j), real, imag)

    @from_natural
    def leave(slot, row, j, real, imag):
        keep(carried, 0, slot, row, j, real, imag)
        return times(real, imag, *seen(window, 2, slot, row, j))

    @from_frequency
    def residual(slot, row, j, real, imag):
        columns = slice(j * LANES, (j + 1) * LANES)
        factor = real * real + imag * imag - measured_ref[slot, pl.ds(row, step), columns]
        return factor * real, factor * imag

    @from_natural
    def before(slot, row, j, real, imag):
        inner = times_conj(*seen(window, 2, slot, row, j), real, imag)
        second = times_conj(*seen(carried, 0, slot, row, j), real, imag)
        keep(window, 2, slot, row, j, *second)
        return inner

    @from_frequency
    def propagate_back(slot, row, j, real, imag):
        return times_conj(*at(trans_ref, 0, row, j), real, imag)

    def stages(slot):
        yield from forward(slot, entry)
        yield from inverse(slot, propagate)
        yield from forward(slot, leave)
        yield from inverse(slot, residual)
        yield from forward(slot, before)
        yield from inverse(slot, propagate_back)

    running = [stages(slot) for slot in range(slots)]
    turn = 0
    while any(x is not None for x in running):
        for slot in range(slots):
            if running[slot] is not None and turn >= slot * lag:
                if next(running[slot], "end") == "end":
                    running[slot] = None
        turn += 1

    live = [(slot < places[0, 2 * slots]).astype(f32) for slot in range(slots)]
    core = lax.axis_index("core")
    share = width // cores
    for row in range(0, half, step):
        sums = [[None] * 4 for side in range(2)]
        for j in range(2):
            for slot in range(slots):
                for side, (real, imag) in enumerate(natural(slot, row, j)):
                    place = side * half + row
                    term = times_conj(*seen(window, 0, slot, place, j), real, imag)
                    keep(
                        window,
                        0,
                        slot,
                        place,
                        j,
                        *times_conj(*at(wave_ref, 0, place, j), real, imag),
                    )
                    for part in range(2):
                        value = live[slot] * term[part]
                        old = sums[side][2 * part + j]
                        sums[side][2 * part + j] = value if old is None else old + value
        for side in range(2):
            place = side * half + row
            which = lax.rem(place // share + core, cores)
            for j, block in enumerate(packed(sums[side], half)):
                terms[which, j, pl.ds(place % share, step), :] = block
    for k, out in enumerate(terms_out):
        out[...] = terms[k]


def place_kernel(paired, cores, places_ref, window, own_out, near_out, far_out, acc, places, arrived):
    copy = pltpu.make_async_copy(places_ref, places, arrived)
    copy.start()
    acc[...] = jnp.zeros(acc.shape, f32)
    sides = acc.shape[1]
    tile = acc.shape[2] // 3
    slots = window.shape[2] // (2 * tile)
    width = window.shape[2] // slots
    half = width // 2
    column_of = lax.axis_index("col")
    row_starts = [pl.multiple_of(place * tile, 8) for place in row_places(cores)]
    copy.wait()
    shift = tile - half
    corners = [
        (places[0, 2 * slot] + shift, places[0, 2 * slot + 1] + shift) for slot in range(slots)
    ]
    live = [(slot < places[0, 2 * slots]).astype(f32) for slot in range(slots)]
    chunk = half
    lane = lane_ids(chunk)
    for slot in range(slots):
        row, column = corners[slot]
        inside = lane >= column
        over = column + LANES - tile
        for plane in range(4):
            for start in range(0, width, chunk):
                rows = pl.ds(slot * width + start, chunk)
                target = pl.ds(row + start, chunk)
                first, second = (live[slot] * window[plane, j, rows, :] for j in range(2))
                pieces = [jnp.where(inside, pltpu.roll(second, column, 1), pltpu.roll(first, over, 1))]
                if paired:
                    value = live[slot] * window[plane, 1 - column_of, rows, :]
                    value = pltpu.roll(value, jnp.where(column_of == 0, over, column), 1)
                    pieces.append(jnp.where(inside.astype(jnp.int32) == column_of, value, 0.0))
                else:
                    pieces.append(jnp.where(inside, pltpu.roll(first, column, 1), 0.0))
                    pieces.append(jnp.where(inside, 0.0, pltpu.roll(second, over, 1)))
                for side, piece in enumerate(pieces):
                    acc[plane, side, target, :] = acc[plane, side, target, :] + piece
    for start, out in zip(row_starts, (own_out, near_out, far_out)):
        rows = pl.ds(start, tile)
        for side in range(sides):
            planes = [acc[plane, side, rows, :] for plane in range(4)]
            for j, block in enumerate(packed(planes, tile)):
                k = 3 * side + j
                out[:, k * LANES : (k + 1) * LANES] = block


def fold_kernel(own_ref, near_ref, far_ref, *outs):
    columns = outs[0].shape[1]
    for side, out in enumerate(outs):
        part = slice(side * columns, (side + 1) * columns)
        out[...] = own_ref[:, part] + near_ref[:, part] + far_ref[:, part]


def add_kernel(first_ref, second_ref, out_ref):
    out_ref[...] = first_ref[...] + second_ref[...]


def spread_sum_kernel(count, pieces_ref, out_ref):
    rows = pieces_ref.shape[0] // count
    total = pieces_ref[:rows]
    for k in range(1, count):
        total = total + pieces_ref[k * rows : (k + 1) * rows]
    for k in range(count):
        out_ref[k * rows : (k + 1) * rows] = total


def update_kernel(rate, cores, object_ref, probe_ref, *refs):
    object_out, probe_out = refs[-2:]
    sums = refs[:cores]
    tile = object_ref.shape[2]
    total = refs[cores][...]
    for ref in refs[cores + 1 : -2]:
        total = total + ref[...]
    parts = [total[:, j * LANES : (j + 1) * LANES] for j in range(3)]
    parts.append(last_of(parts, tile))
    for plane in range(4):
        object_out[plane // 2, plane % 2] = (
            object_ref[plane // 2, plane % 2] - object_rate * parts[plane][:, :tile]
        )
    width = probe_ref.shape[1]
    half = width // 2
    share = width // cores
    lane = lane_ids(share)
    for k, ref in enumerate(sums):
        start = share * lax.rem(lax.axis_index("core") + k, cores)
        rows = pl.ds(pl.multiple_of(start, 8), share)
        parts = [ref[j] for j in range(3)]
        parts.append(last_of(parts, half))
        for j in range(2):
            head, tail = parts[2 * j], pltpu.roll(parts[2 * j + 1], half, 1)
            probe_out[j, rows, :LANES] = probe_ref[j, rows, :LANES] - rate * jnp.where(
                lane < half, head, tail
            )
            probe_out[j, rows, LANES:] = (
                probe_ref[j, rows, LANES:] - rate * tail[:, : width - LANES]
            )


def passed_along(x, axis, by):
    peers = lax.axis_size(axis)
    pairs = [(i, i + by) for i in range(peers) if 0 <= i + by < peers]
    return lax.ppermute(x, axis, pairs)


def from_near(x, cores):
    if cores == 2:
        return lax.ppermute(x, "core", [(0, 1), (1, 0)])
    return passed_along(x, ROWS, 1)


def from_far(x, cores):
    if cores == 2:
        ends = range(1, lax.axis_size(ROWS) - 1, 2)
        pairs = [(i, i + 1) for i in ends] + [(i + 1, i) for i in ends]
        return lax.ppermute(x, ROWS, pairs)
    return passed_along(x, ROWS, -1)


def from_far_beside(x):
    ends = range(1, lax.axis_size(ROWS) - 1, 2)
    pairs = []
    for i in ends:
        for j in range(2):
            pairs += [(2 * i + j, 2 * i + 3 - j), (2 * i + 2 + j, 2 * i + 1 - j)]
    return lax.ppermute(x, ROWS + ("col",), pairs)


def all_sum(x, group):
    count = math.prod(lax.axis_size(axis) for axis in group)
    shape = x.shape
    x = x.reshape(-1, 2, LANES)
    pairs = x.shape[0]
    piece = -(-pairs // count)
    if piece * count > pairs:
        x = jnp.pad(x, ((0, piece * count - pairs), (0, 0), (0, 0)))
    x = x.reshape(count, piece, 2, LANES)
    x = lax.all_to_all(x, group, 0, 0, tiled=True)
    whole = x.shape
    x = pl.pallas_call(
        functools.partial(spread_sum_kernel, count),
        out_shape=jax.ShapeDtypeStruct((count * piece * 2, LANES), f32),
        in_specs=[VMEM],
        out_specs=VMEM,
        compiler_params=pltpu.CompilerParams(vmem_limit_bytes=6 * 1024 * 1024),
    )(x.reshape(count * piece * 2, LANES)).reshape(whole)
    x = lax.all_to_all(x, group, 0, 0, tiled=True)
    return x.reshape(count * piece, 2, LANES)[:pairs].reshape(shape)


def shards(object_slices, probe, propagator_phase, measured, offsets, counts):
    tile = object_slices.shape[-1]
    width = probe.shape[-1]
    slots = measured.shape[2]
    cores = lax.axis_size("core")
    cols_count = lax.axis_size("col")
    devices = lax.axis_size(ROWS) * cols_count
    paired = cols_count == 2
    large = pltpu.CompilerParams(vmem_limit_bytes=18 * 1024 * 1024)
    small = pltpu.CompilerParams(vmem_limit_bytes=6 * 1024 * 1024)

    def shape(*dims, kind=f32):
        return jax.ShapeDtypeStruct(dims, kind)

    cells = pl.pallas_call(
        pack_kernel,
        out_shape=shape(tile, 3 * LANES),
        in_specs=[VMEM],
        out_specs=VMEM,
        cost_estimate=pl.CostEstimate(flops=10**10, bytes_accessed=10**7, transcendentals=0),
        compiler_params=small,
    )(object_slices)
    if paired:
        beside = [lax.ppermute(object_slices, "col", [(0, 1), (1, 0)])]
    else:
        beside = [passed_along(cells, "col", 1), passed_along(cells, "col", -1)]
    own = [cells] + beside
    near = [from_near(x, cores) for x in own]
    if paired and cores == 2:
        far = [from_far(cells, cores), from_far_beside(cells)]
    else:
        far = [from_far(x, cores) for x in own]

    wave, trans, intensities, places = pl.pallas_call(
        prepare_kernel,
        out_shape=[
            shape(2, width, 2 * LANES),
            shape(2, width, 2 * LANES),
            shape(slots, width, 2 * LANES),
            shape(8, LANES, kind=jnp.int32),
        ],
        in_specs=[VMEM] * 5,
        out_specs=[VMEM] * 4,
        cost_estimate=pl.CostEstimate(flops=10**10, bytes_accessed=10**7, transcendentals=0),
        compiler_params=small,
    )(offsets, counts, probe, propagator_phase, measured)

    total = slots * width
    sides = len(own)
    strip = shape(tile, sides * 3 * LANES)
    scratch = [
        pltpu.VMEM((4, 3, 3 * tile, LANES), f32),
        pltpu.VMEM((2, 2, total, LANES), f32),
        pltpu.VMEM((cores, 3, width // cores, LANES), f32),
        pltpu.SMEM((8, LANES), jnp.int32),
        pltpu.SemaphoreType.DMA,
    ]
    scratch += [pltpu.VMEM((2, 2 * width, 2 * LANES), bf16)] * slots
    scratch += [pltpu.VMEM((2 * width, 2 * LANES), f32)] * slots
    scratch += [pltpu.VMEM((2, 2 * width, 2 * LANES), bf16)] * slots
    scratch += [pltpu.VMEM((2, width, 2 * LANES), f32)] * slots
    term = shape(3, width // cores, LANES)
    gradients, *terms = pl.pallas_call(
        functools.partial(position_kernel, paired, cores),
        out_shape=[shape(4, 2, total, LANES)] + [term] * cores,
        in_specs=[ANY] + [VMEM] * (3 * sides + 5),
        out_specs=[VMEM] * (1 + cores),
        scratch_shapes=scratch,
        compiler_params=large,
    )(places, *own, *near, *far, wave, trans, intensities, *matrices(width))
    own_strip, near_strip, far_strip = pl.pallas_call(
        functools.partial(place_kernel, paired, cores),
        out_shape=[strip] * 3,
        in_specs=[ANY, VMEM],
        out_specs=[VMEM] * 3,
        scratch_shapes=[
            pltpu.VMEM((4, sides, 3 * tile, LANES), f32),
            pltpu.SMEM((8, LANES), jnp.int32),
            pltpu.SemaphoreType.DMA,
        ],
        compiler_params=small,
    )(places, gradients)

    if cores == 2:
        joined = pl.pallas_call(
            add_kernel,
            out_shape=term,
            in_specs=[VMEM] * 2,
            out_specs=VMEM,
            compiler_params=small,
        )(terms[0], from_near(terms[1], cores))
        mine = all_sum(joined, ("pair", "col"))
        sums = [mine, from_near(mine, cores)]
    else:
        sums = [all_sum(terms[0], ("pair", "col"))]
    if cores == 1:
        near_strip, far_strip = passed_along(near_strip, ROWS, -1), passed_along(far_strip, ROWS, 1)
    else:
        near_strip, far_strip = from_near(near_strip, cores), from_far(far_strip, cores)
    share = shape(tile, 3 * LANES)
    parts = pl.pallas_call(
        fold_kernel,
        out_shape=[share] * sides,
        in_specs=[VMEM] * 3,
        out_specs=[VMEM] * sides,
        compiler_params=small,
    )(own_strip, near_strip, far_strip)
    if paired:
        received = [lax.ppermute(parts[1], "col", [(0, 1), (1, 0)])]
    else:
        received = [passed_along(parts[1], "col", -1), passed_along(parts[2], "col", 1)]
    return pl.pallas_call(
        functools.partial(update_kernel, probe_rate / (slots * devices), cores),
        out_shape=[shape(*object_slices.shape), shape(*probe.shape)],
        in_specs=[VMEM] * (3 + cores + len(received)),
        out_specs=[VMEM] * 2,
        compiler_params=small,
    )(object_slices, probe, *sums, parts[0], *received)


def solution(mesh):
    rows, cols = mesh.devices.shape
    cores = 2 if rows % 2 == 0 else 1
    finer = Mesh(mesh.devices.reshape(rows // cores, cores, cols), ROWS + ("col",))
    return jax.shard_map(
        shards,
        mesh=finer,
        in_specs=(
            P(None, None, ROWS, "col"),
            P(),
            P(),
            P(ROWS, "col", None, None, None),
            P(ROWS, "col", None, None),
            P(ROWS, "col"),
        ),
        out_specs=(P(None, None, ROWS, "col"), P()),
        check_vma=False,
    )
```

```python
import functools
import math

import jax
import jax.numpy as jnp
import numpy as np
from jax import lax
from jax.experimental import pallas as pl
from jax.experimental.pallas import tpu as pltpu
from jax.sharding import Mesh
from jax.sharding import PartitionSpec as P

object_rate = 0.02
probe_rate = 0.3

LANES = 128
f32 = jnp.float32
bf16 = jnp.bfloat16
VMEM = pl.BlockSpec(memory_space=pltpu.VMEM)
ANY = pl.BlockSpec(memory_space=pl.ANY)
ROWS = ("pair", "core")


def matrices(width):
    half = width // 2
    k = np.arange(half)
    turns = [2 * k[:, None] * k[None, :], k[:, None] * (2 * k[None, :] + 1)]
    turns.append(turns[1].T)
    rights, lefts = [], []

    def halves(matrix):
        high = matrix.astype(np.float32).astype(bf16)
        low = (matrix - high.astype(np.float64)).astype(np.float32).astype(bf16)
        return high, low

    for turn in turns:
        angle = (turn % width) * (2.0 * math.pi / width)
        cosine = np.cos(angle) / math.sqrt(width)
        sine = np.sin(angle) / math.sqrt(width)
        right = np.zeros((2, LANES, 2, LANES))
        right[0, :half, 0, :half] = cosine
        right[0, :half, 1, :half] = -sine
        right[1, :half, 0, :half] = sine
        right[1, :half, 1, :half] = cosine
        high, low = halves(right.reshape(2 * LANES, 2 * LANES))
        rights.append(np.concatenate([high, high, low], 0))
        high, low = halves(np.block([[cosine.T, sine.T], [-sine.T, cosine.T]]))
        lefts.append(np.concatenate([high, low], 0))
    return np.stack(rights), np.stack(lefts)


def sorters(width):
    half = width // 2

    def ids(shape, axis):
        return lax.broadcasted_iota(jnp.int32, shape, axis)

    shape = (width, 2 * LANES)
    source = ids(shape, 0)
    columns = ids(shape, 1) == (source & 1) * LANES + (source >> 1)
    shape = (width, width)
    target = ids(shape, 0)
    rows = ids(shape, 1) == jnp.where(target < half, 2 * target, 2 * (target - half) + 1)
    return [jnp.where(x, 1.0, 0.0).astype(bf16) for x in (columns, rows)]


def times(a_real, a_imag, b_real, b_imag):
    return (a_real * b_real - a_imag * b_imag, a_real * b_imag + a_imag * b_real)


def times_conj(a_real, a_imag, b_real, b_imag):
    return (a_real * b_real + a_imag * b_imag, a_real * b_imag - a_imag * b_real)


def halves_of(value):
    high = value.astype(bf16)
    return high, (value - high.astype(f32)).astype(bf16)


def lane_ids(rows):
    return lax.broadcasted_iota(jnp.int32, (rows, LANES), 1)


def packed(planes, half):
    lane = lane_ids(planes[0].shape[0])
    rest = LANES - half
    return [
        jnp.where(lane < half, planes[j], pltpu.roll(planes[3], (half - rest * j) % LANES, 1))
        for j in range(3)
    ]


def last_of(parts, half):
    lane = lane_ids(parts[0].shape[0])
    rest = LANES - half
    out = pltpu.roll(parts[0], rest, 1)
    for j in range(1, 3):
        out = jnp.where(lane < rest * j, out, pltpu.roll(parts[j], (rest * j + rest) % LANES, 1))
    return out


def cosine_and_sine(x):
    turns = jnp.floor(x * (2.0 / math.pi) + 0.5)
    rest = ((x - turns * 1.5703125) - turns * 4.837512969970703125e-4) - turns * 7.54978995489188e-8
    square = rest * rest
    sine = ((-1.9515295891e-4 * square + 8.3321608736e-3) * square - 1.6666654611e-1) * square
    sine = sine * rest + rest
    cosine = (2.443315711809948e-5 * square - 1.388731625493765e-3) * square + 4.166664568298827e-2
    cosine = cosine * square * square - 0.5 * square + 1.0
    quarter = turns.astype(jnp.int32) & 3
    odd = (quarter & 1) == 1
    return (
        jnp.where(odd, sine, cosine) * jnp.where((quarter == 1) | (quarter == 2), -1.0, 1.0),
        jnp.where(odd, cosine, sine) * jnp.where(quarter >= 2, -1.0, 1.0),
    )


def pack_kernel(object_ref, out_ref):
    tile = object_ref.shape[2]
    pad = jnp.zeros((tile, LANES - tile), f32)
    planes = [
        jnp.concatenate([object_ref[plane // 2, plane % 2], pad], 1) for plane in range(4)
    ]
    for j, block in enumerate(packed(planes, tile)):
        out_ref[:, j * LANES : (j + 1) * LANES] = block


def prepare_kernel(
    offsets_ref,
    counts_ref,
    probe_ref,
    phase_ref,
    measured_ref,
    wave_out,
    trans_out,
    measured_out,
    places_out,
):
    lanes = lax.broadcasted_iota(jnp.int32, places_out.shape, 1)
    slots = measured_out.shape[0]
    places = jnp.where(lanes == 2 * slots, counts_ref[...], 0)
    for slot in range(slots):
        for axis in range(2):
            value = offsets_ref[0, 0, slot : slot + 1, axis : axis + 1]
            places = jnp.where(lanes == 2 * slot + axis, value, places)
    places_out[...] = places
    width = probe_ref.shape[1]
    half = width // 2
    lane = lane_ids(width)
    for j in range(2):
        head = probe_ref[j, :, :LANES]
        tail = jnp.concatenate(
            [probe_ref[j, :, LANES:], jnp.zeros((width, 2 * LANES - width), f32)], 1
        )
        rest = LANES - half
        wave_out[j, :, :LANES] = jnp.where(lane < half, head, 0.0)
        wave_out[j, :, LANES:] = jnp.where(
            lane < rest, pltpu.roll(head, rest, 1), pltpu.roll(tail, rest, 1)
        )
    columns, rows = sorters(width)
    planes = [phase_ref[...]] + [measured_ref[0, 0, j] for j in range(measured_out.shape[0])]
    for j, left in enumerate(planes):
        total = jnp.zeros((width, 2 * LANES), f32)
        for part in range(3):
            piece = left.astype(bf16)
            left = left - piece.astype(f32)
            moved = jnp.dot(piece, columns, preferred_element_type=f32)
            total = total + jnp.dot(rows, moved.astype(bf16), preferred_element_type=f32)
        if j > 0:
            measured_out[j - 1] = total
            continue
        used = lax.rem(lax.broadcasted_iota(jnp.int32, total.shape, 1), LANES) < half
        for side, value in enumerate(cosine_and_sine(total)):
            trans_out[side] = jnp.where(used, value, 0.0)


def row_places(cores):
    core = lax.axis_index("core") if cores == 2 else 1
    return 1, 2 - 2 * core, 2 * core


def position_kernel(
    paired,
    cores,
    places_ref,
    *refs,
):
    sides = 2 if paired else 3
    tiles = refs[: 3 * sides]
    (
        wave_ref,
        trans_ref,
        measured_ref,
        right_ref,
        left_ref,
        window,
    ) = refs[3 * sides : 3 * sides + 6]
    terms_out = refs[3 * sides + 6 : 3 * sides + 6 + cores]
    (
        obj,
        carried,
        terms,
        places,
        arrived,
    ) = refs[3 * sides + 6 + cores : 3 * sides + 11 + cores]
    copy = pltpu.make_async_copy(places_ref, places, arrived)
    copy.start()
    slots = measured_ref.shape[0]
    work = refs[3 * sides + 11 + cores :]
    data, out_right, mid, out_left = (work[k * slots : (k + 1) * slots] for k in range(4))
    width = wave_ref.shape[1]
    half = width // 2
    tile = obj.shape[2] // 3
    total = slots * width
    step = 16
    part_rows = half // 2
    lag = 2
    column_of = lax.axis_index("col")
    row_starts = [pl.multiple_of(place * tile, 8) for place in row_places(cores)]

    for row in range(3):
        rows = pl.ds(row_starts[row], tile)
        for side in range(sides):
            if paired:
                place = 1 if side == 0 else 2 - 2 * column_of
            else:
                place = (1, 0, 2)[side]
            ref = tiles[row * sides + side]
            parts = [ref[:, j * LANES : (j + 1) * LANES] for j in range(3)]
            parts.append(last_of(parts, tile))
            for plane in range(4):
                obj[plane, place, rows, :] = parts[plane]
        if paired:
            for plane in range(4):
                obj[plane, 2 * column_of, rows, :] = jnp.zeros((tile, LANES), f32)

    copy.wait()
    shift = tile - half
    corners = [
        (places[0, 2 * slot] + shift, places[0, 2 * slot + 1] + shift)
        for slot in range(slots)
    ]
    chunk = half
    lane = lane_ids(chunk)
    for slot in range(slots):
        row, column = corners[slot]
        back = lax.rem(LANES - column, LANES)
        inside = lane < tile - column
        for plane in range(4):
            for start in range(0, width, chunk):
                source = pl.ds(row + start, chunk)
                target = pl.ds(slot * width + start, chunk)
                for j in range(2):
                    window[plane, j, target, :] = jnp.where(
                        inside,
                        pltpu.roll(obj[plane, j, source, :], back, 1),
                        pltpu.roll(obj[plane, j + 1, source, :], tile - column, 1),
                    )
    span = 2 * LANES

    def put(slot, block, row, a, b):
        rows = pl.ds(block * width + row, step)
        high, low = halves_of(jnp.concatenate([a, b], 1))
        data[slot][rows, :span] = high
        data[slot][rows, span:] = low

    def multiply_right(slot, odd):
        for block in range(2):
            rows = slice(block * width, (block + 1) * width)
            left = jnp.concatenate([data[slot][rows, :], data[slot][rows, :span]], 1)
            out_right[slot][rows, :] = jnp.dot(
                left, right_ref[odd * block], preferred_element_type=f32
            )
            yield

    def put_mid(slot, block, start, first, second):
        for part in range(2):
            high, low = halves_of(jnp.concatenate([first[part], second[part]], 1))
            mid[slot][block, pl.ds(part * half + start, step), :] = high
            mid[slot][block, pl.ds((2 + part) * half + start, step), :] = low

    def multiply_left(slot, odd):
        for block in range(2):
            both = left_ref[odd * block]
            high = mid[slot][block, :width]
            low = mid[slot][block, width:]
            out = jnp.dot(both, high, preferred_element_type=f32)
            rest = jnp.dot(both[:width], low, preferred_element_type=f32)
            out_left[slot][block] = out[:width] + (out[width:] + rest)
            yield

    def get_right(slot, block, row):
        rows = pl.ds(block * width + row, step)
        return out_right[slot][rows, :LANES], out_right[slot][rows, LANES:]

    def get_left(slot, block, j, start):
        columns = slice(j * LANES, (j + 1) * LANES)
        return (
            out_left[slot][block, pl.ds(start, step), columns],
            out_left[slot][block, pl.ds(half + start, step), columns],
        )

    def forward(slot, source):
        for row in range(0, half, step):
            for side, ((a0, b0), (a1, b1)) in enumerate(source(slot, row)):
                place = side * half + row
                put(slot, 0, place, a0 + a1, b0 + b1)
                put(slot, 1, place, a0 - a1, b0 - b1)
            if row % part_rows == part_rows - step:
                yield
        yield from multiply_right(slot, 1)
        for row in range(0, half, step):
            even, odd = [], []
            for j in range(2):
                a0, b0 = get_right(slot, j, row)
                a1, b1 = get_right(slot, j, half + row)
                even.append((a0 + a1, b0 + b1))
                odd.append((a0 - a1, b0 - b1))
            put_mid(slot, 0, row, *even)
            put_mid(slot, 1, row, *odd)
            if row % part_rows == part_rows - step:
                yield
        yield from multiply_left(slot, 1)

    def inverse(slot, source):
        for row in range(0, width, step):
            for j, (a, b) in enumerate(source(slot, row)):
                put(slot, j, row, a, b)
            if row % (2 * part_rows) == 2 * part_rows - step:
                yield
        yield from multiply_right(slot, 2)
        for row in range(0, width, step):
            a0, b0 = get_right(slot, 0, row)
            a1, b1 = get_right(slot, 1, row)
            put_mid(slot, row // half, row % half, (a0 + a1, b0 + b1), (a0 - a1, b0 - b1))
            if row % (2 * part_rows) == 2 * part_rows - step:
                yield
        yield from multiply_left(slot, 2)

    def frequency(slot, row, j):
        return get_left(slot, row // half, j, row % half)

    def natural(slot, row, j):
        b0, a0 = get_left(slot, 0, j, row)
        b1, a1 = get_left(slot, 1, j, row)
        return (a0 + a1, b0 + b1), (a0 - a1, b0 - b1)

    def at(ref, first, row, j):
        rows = pl.ds(row, step)
        columns = slice(j * LANES, (j + 1) * LANES)
        return ref[first, rows, columns], ref[first + 1, rows, columns]

    def seen(ref, first, slot, row, j):
        rows = pl.ds(slot * width + row, step)
        return ref[first, j, rows, :], ref[first + 1, j, rows, :]

    def keep(ref, first, slot, row, j, real, imag):
        rows = pl.ds(slot * width + row, step)
        ref[first, j, rows, :] = real
        ref[first + 1, j, rows, :] = imag

    def entry(slot, row):
        return [
            [times(*at(wave_ref, 0, place, j), *seen(window, 0, slot, place, j)) for j in range(2)]
            for place in (row, half + row)
        ]

    def from_natural(handle):
        def source(slot, row):
            pairs = [natural(slot, row, j) for j in range(2)]
            return [
                [handle(slot, side * half + row, j, *pairs[j][side]) for j in range(2)]
                for side in range(2)
            ]

        return source

    def from_frequency(handle):
        def source(slot, row):
            out = []
            for j in range(2):
                real, imag = handle(slot, row, j, *frequency(slot, row, j))
                out.append((imag, real))
            return out

        return source

    @from_frequency
    def propagate(slot, row, j, real, imag):
        return times(*at(trans_ref, 0, row, j), real, imag)

    @from_natural
    def leave(slot, row, j, real, imag):
        keep(carried, 0, slot, row, j, real, imag)
        return times(real, imag, *seen(window, 2, slot, row, j))

    @from_frequency
    def residual(slot, row, j, real, imag):
        columns = slice(j * LANES, (j + 1) * LANES)
        factor = real * real + imag * imag - measured_ref[slot, pl.ds(row, step), columns]
        return factor * real, factor * imag

    @from_natural
    def before(slot, row, j, real, imag):
        inner = times_conj(*seen(window, 2, slot, row, j), real, imag)
        second = times_conj(*seen(carried, 0, slot, row, j), real, imag)
        keep(window, 2, slot, row, j, *second)
        return inner

    @from_frequency
    def propagate_back(slot, row, j, real, imag):
        return times_conj(*at(trans_ref, 0, row, j), real, imag)

    def stages(slot):
        yield from forward(slot, entry)
        yield from inverse(slot, propagate)
        yield from forward(slot, leave)
        yield from inverse(slot, residual)
        yield from forward(slot, before)
        yield from inverse(slot, propagate_back)

    running = [stages(slot) for slot in range(slots)]
    turn = 0
    while any(x is not None for x in running):
        for slot in range(slots):
            if running[slot] is not None and turn >= slot * lag:
                if next(running[slot], "end") == "end":
                    running[slot] = None
        turn += 1

    live = [(slot < places[0, 2 * slots]).astype(f32) for slot in range(slots)]
    core = lax.axis_index("core")
    share = width // cores
    for row in range(0, half, step):
        sums = [[None] * 4 for side in range(2)]
        for j in range(2):
            for slot in range(slots):
                for side, (real, imag) in enumerate(natural(slot, row, j)):
                    place = side * half + row
                    term = times_conj(*seen(window, 0, slot, place, j), real, imag)
                    keep(
                        window,
                        0,
                        slot,
                        place,
                        j,
                        *times_conj(*at(wave_ref, 0, place, j), real, imag),
                    )
                    for part in range(2):
                        value = live[slot] * term[part]
                        old = sums[side][2 * part + j]
                        sums[side][2 * part + j] = value if old is None else old + value
        for side in range(2):
            place = side * half + row
            which = lax.rem(place // share + core, cores)
            for j, block in enumerate(packed(sums[side], half)):
                terms[which, j, pl.ds(place % share, step), :] = block
    for k, out in enumerate(terms_out):
        out[...] = terms[k]


def place_kernel(paired, cores, places_ref, window, own_out, near_out, far_out, acc, places, arrived):
    copy = pltpu.make_async_copy(places_ref, places, arrived)
    copy.start()
    acc[...] = jnp.zeros(acc.shape, f32)
    sides = acc.shape[1]
    tile = acc.shape[2] // 3
    slots = window.shape[2] // (2 * tile)
    width = window.shape[2] // slots
    half = width // 2
    column_of = lax.axis_index("col")
    row_starts = [pl.multiple_of(place * tile, 8) for place in row_places(cores)]
    copy.wait()
    shift = tile - half
    corners = [
        (places[0, 2 * slot] + shift, places[0, 2 * slot + 1] + shift) for slot in range(slots)
    ]
    live = [(slot < places[0, 2 * slots]).astype(f32) for slot in range(slots)]
    chunk = half
    lane = lane_ids(chunk)
    for slot in range(slots):
        row, column = corners[slot]
        inside = lane >= column
        over = column + LANES - tile
        for plane in range(4):
            for start in range(0, width, chunk):
                rows = pl.ds(slot * width + start, chunk)
                target = pl.ds(row + start, chunk)
                first, second = (live[slot] * window[plane, j, rows, :] for j in range(2))
                pieces = [jnp.where(inside, pltpu.roll(second, column, 1), pltpu.roll(first, over, 1))]
                if paired:
                    value = live[slot] * window[plane, 1 - column_of, rows, :]
                    value = pltpu.roll(value, jnp.where(column_of == 0, over, column), 1)
                    pieces.append(jnp.where(inside.astype(jnp.int32) == column_of, value, 0.0))
                else:
                    pieces.append(jnp.where(inside, pltpu.roll(first, column, 1), 0.0))
                    pieces.append(jnp.where(inside, 0.0, pltpu.roll(second, over, 1)))
                for side, piece in enumerate(pieces):
                    acc[plane, side, target, :] = acc[plane, side, target, :] + piece
    for start, out in zip(row_starts, (own_out, near_out, far_out)):
        rows = pl.ds(start, tile)
        for side in range(sides):
            planes = [acc[plane, side, rows, :] for plane in range(4)]
            for j, block in enumerate(packed(planes, tile)):
                k = 3 * side + j
                out[:, k * LANES : (k + 1) * LANES] = block


def fold_kernel(own_ref, near_ref, far_ref, *outs):
    columns = outs[0].shape[1]
    for side, out in enumerate(outs):
        part = slice(side * columns, (side + 1) * columns)
        out[...] = own_ref[:, part] + near_ref[:, part] + far_ref[:, part]


def update_kernel(rate, cores, object_ref, probe_ref, *refs):
    object_out, probe_out = refs[-2:]
    sums = refs[:cores]
    tile = object_ref.shape[2]
    total = refs[cores][...]
    for ref in refs[cores + 1 : -2]:
        total = total + ref[...]
    parts = [total[:, j * LANES : (j + 1) * LANES] for j in range(3)]
    parts.append(last_of(parts, tile))
    for plane in range(4):
        object_out[plane // 2, plane % 2] = (
            object_ref[plane // 2, plane % 2] - object_rate * parts[plane][:, :tile]
        )
    width = probe_ref.shape[1]
    half = width // 2
    share = width // cores
    lane = lane_ids(share)
    for k, ref in enumerate(sums):
        start = share * lax.rem(lax.axis_index("core") + k, cores)
        rows = pl.ds(pl.multiple_of(start, 8), share)
        parts = [ref[j] for j in range(3)]
        parts.append(last_of(parts, half))
        for j in range(2):
            head, tail = parts[2 * j], pltpu.roll(parts[2 * j + 1], half, 1)
            probe_out[j, rows, :LANES] = probe_ref[j, rows, :LANES] - rate * jnp.where(
                lane < half, head, tail
            )
            probe_out[j, rows, LANES:] = (
                probe_ref[j, rows, LANES:] - rate * tail[:, : width - LANES]
            )


def passed_along(x, axis, by):
    peers = lax.axis_size(axis)
    pairs = [(i, i + by) for i in range(peers) if 0 <= i + by < peers]
    return lax.ppermute(x, axis, pairs)


def from_near(x, cores):
    if cores == 2:
        return lax.ppermute(x, "core", [(0, 1), (1, 0)])
    return passed_along(x, ROWS, 1)


def from_far(x, cores):
    if cores == 2:
        ends = range(1, lax.axis_size(ROWS) - 1, 2)
        pairs = [(i, i + 1) for i in ends] + [(i + 1, i) for i in ends]
        return lax.ppermute(x, ROWS, pairs)
    return passed_along(x, ROWS, -1)


def from_far_beside(x):
    ends = range(1, lax.axis_size(ROWS) - 1, 2)
    pairs = []
    for i in ends:
        for j in range(2):
            pairs += [(2 * i + j, 2 * i + 3 - j), (2 * i + 2 + j, 2 * i + 1 - j)]
    return lax.ppermute(x, ROWS + ("col",), pairs)


def all_sum(x, group):
    count = math.prod(lax.axis_size(axis) for axis in group)
    shape = x.shape
    x = x.reshape(-1, 2, LANES)
    pairs = x.shape[0]
    piece = -(-pairs // count)
    if piece * count > pairs:
        x = jnp.pad(x, ((0, piece * count - pairs), (0, 0), (0, 0)))
    x = x.reshape(count, piece, 2, LANES)
    x = lax.all_to_all(x, group, 0, 0, tiled=True)
    x = jnp.broadcast_to(jnp.sum(x, 0)[None], x.shape)
    x = lax.all_to_all(x, group, 0, 0, tiled=True)
    return x.reshape(count * piece, 2, LANES)[:pairs].reshape(shape)


def shards(object_slices, probe, propagator_phase, measured, offsets, counts):
    tile = object_slices.shape[-1]
    width = probe.shape[-1]
    slots = measured.shape[2]
    cores = lax.axis_size("core")
    cols_count = lax.axis_size("col")
    devices = lax.axis_size(ROWS) * cols_count
    paired = cols_count == 2
    large = pltpu.CompilerParams(vmem_limit_bytes=18 * 1024 * 1024)
    small = pltpu.CompilerParams(vmem_limit_bytes=6 * 1024 * 1024)

    def shape(*dims, kind=f32):
        return jax.ShapeDtypeStruct(dims, kind)

    cells = pl.pallas_call(
        pack_kernel,
        out_shape=shape(tile, 3 * LANES),
        in_specs=[VMEM],
        out_specs=VMEM,
        cost_estimate=pl.CostEstimate(flops=10**10, bytes_accessed=10**7, transcendentals=0),
        compiler_params=small,
    )(object_slices)
    if paired:
        beside = [lax.ppermute(cells, "col", [(0, 1), (1, 0)])]
    else:
        beside = [passed_along(cells, "col", 1), passed_along(cells, "col", -1)]
    own = [cells] + beside
    near = [from_near(x, cores) for x in own]
    if paired and cores == 2:
        far = [from_far(cells, cores), from_far_beside(cells)]
    else:
        far = [from_far(x, cores) for x in own]

    wave, trans, intensities, places = pl.pallas_call(
        prepare_kernel,
        out_shape=[
            shape(2, width, 2 * LANES),
            shape(2, width, 2 * LANES),
            shape(slots, width, 2 * LANES),
            shape(8, LANES, kind=jnp.int32),
        ],
        in_specs=[VMEM] * 5,
        out_specs=[VMEM] * 4,
        cost_estimate=pl.CostEstimate(flops=10**10, bytes_accessed=10**7, transcendentals=0),
        compiler_params=small,
    )(offsets, counts, probe, propagator_phase, measured)

    total = slots * width
    sides = len(own)
    strip = shape(tile, sides * 3 * LANES)
    scratch = [
        pltpu.VMEM((4, 3, 3 * tile, LANES), f32),
        pltpu.VMEM((2, 2, total, LANES), f32),
        pltpu.VMEM((cores, 3, width // cores, LANES), f32),
        pltpu.SMEM((8, LANES), jnp.int32),
        pltpu.SemaphoreType.DMA,
    ]
    scratch += [pltpu.VMEM((2 * width, 4 * LANES), bf16)] * slots
    scratch += [pltpu.VMEM((2 * width, 2 * LANES), f32)] * slots
    scratch += [pltpu.VMEM((2, 2 * width, 2 * LANES), bf16)] * slots
    scratch += [pltpu.VMEM((2, width, 2 * LANES), f32)] * slots
    term = shape(3, width // cores, LANES)
    gradients, *terms = pl.pallas_call(
        functools.partial(position_kernel, paired, cores),
        out_shape=[shape(4, 2, total, LANES)] + [term] * cores,
        in_specs=[ANY] + [VMEM] * (3 * sides + 5),
        out_specs=[VMEM] * (1 + cores),
        scratch_shapes=scratch,
        compiler_params=large,
    )(places, *own, *near, *far, wave, trans, intensities, *matrices(width))
    own_strip, near_strip, far_strip = pl.pallas_call(
        functools.partial(place_kernel, paired, cores),
        out_shape=[strip] * 3,
        in_specs=[ANY, VMEM],
        out_specs=[VMEM] * 3,
        scratch_shapes=[
            pltpu.VMEM((4, sides, 3 * tile, LANES), f32),
            pltpu.SMEM((8, LANES), jnp.int32),
            pltpu.SemaphoreType.DMA,
        ],
        compiler_params=small,
    )(places, gradients)

    if cores == 2:
        mine = all_sum(terms[0] + from_near(terms[1], cores), ("pair", "col"))
        sums = [mine, from_near(mine, cores)]
    else:
        sums = [all_sum(terms[0], ("pair", "col"))]
    if cores == 1:
        near_strip, far_strip = passed_along(near_strip, ROWS, -1), passed_along(far_strip, ROWS, 1)
    else:
        near_strip, far_strip = from_near(near_strip, cores), from_far(far_strip, cores)
    share = shape(tile, 3 * LANES)
    parts = pl.pallas_call(
        fold_kernel,
        out_shape=[share] * sides,
        in_specs=[VMEM] * 3,
        out_specs=[VMEM] * sides,
        compiler_params=small,
    )(own_strip, near_strip, far_strip)
    if paired:
        received = [lax.ppermute(parts[1], "col", [(0, 1), (1, 0)])]
    else:
        received = [passed_along(parts[1], "col", -1), passed_along(parts[2], "col", 1)]
    return pl.pallas_call(
        functools.partial(update_kernel, probe_rate / (slots * devices), cores),
        out_shape=[shape(*object_slices.shape), shape(*probe.shape)],
        in_specs=[VMEM] * (3 + cores + len(received)),
        out_specs=[VMEM] * 2,
        compiler_params=small,
    )(object_slices, probe, *sums, parts[0], *received)


def solution(mesh):
    rows, cols = mesh.devices.shape
    cores = 2 if rows % 2 == 0 else 1
    finer = Mesh(mesh.devices.reshape(rows // cores, cores, cols), ROWS + ("col",))
    return jax.shard_map(
        shards,
        mesh=finer,
        in_specs=(
            P(None, None, ROWS, "col"),
            P(),
            P(),
            P(ROWS, "col", None, None, None),
            P(ROWS, "col", None, None),
            P(ROWS, "col"),
        ),
        out_specs=(P(None, None, ROWS, "col"), P()),
        check_vma=False,
    )
```
